512 devices in a mesh: gx: 8 (over z_lo), gy: 4 (over z_hi, core), gz: 16 (over y, x).
Axes of the slice: x: 4, y: 4, z: 16 (z_hi: 2, z_lo: 8; z = z_hi * 8 + z_lo), core: 2. Of those that a mesh axis runs over, the one named last changes fastest.
Arguments:
- probe_vectors: float32 [32, 16, 32, 2048], P(None, 'gx', 'gy', 'gz'), may hold values from -6 to 6
- layer_ids: int32 [16, 32, 2048], P('gx', 'gy', 'gz'), may hold values from 0 to 15
- layer_kappa: float32 [16], replicated, may hold values from 0.1 to 10
- slot_order: int32 [32, 16], replicated, may hold values from 0 to 511, as said below
Outputs:
- factored: float32 [16384, 16384], P(('gx', 'gy'), 'gz')
The draws below stay inside these ranges and needn't reach their ends.
Inputs may be any that keep to these rules, and one draw needn't show every extreme that they name: `slot_order`: the entries are an ordering of 0 to 511, and in each column the entries divided by 16, rounded down, are an ordering of 0 to 31.
All inputs are finite; a program needn't handle non-finite values.
Results may differ from the reference program's by a relative error of at most 0.00013.
Values sent between devices are 32-bit elements; how exact they have to be, the bound alone decides.
No kernel may reach another device: no remote copies, remote signals or barrier semaphores. Data moves between devices by JAX's collectives and lax.ppermute only.
A program may use at most 128 MiB of HBM per device.

```python
import math
import jax
import jax.numpy as jnp
from jax import lax

K = 32
CX = 2
CY = 8
CZ = 128
PASSES = 4
LAYERS = 16
NPAN = 2
NX = 16
NY = 32
NZ = 2048
ORDER = 16384
PW = 256
N_GX = 8
N_GY = 4
N_GZ = 16
DEVICES = 512


def draw_slot_order(key, part):
    row_count = N_GX * N_GY
    group_key, place_key = jax.random.split(jax.random.fold_in(key, 11))
    group_keys = jax.random.split(group_key, N_GZ)
    place_keys = jax.random.split(place_key, row_count)
    groups = jax.vmap(lambda subkey: jax.random.permutation(subkey, row_count))(group_keys).T
    places = jax.vmap(lambda subkey: jax.random.permutation(subkey, N_GZ))(place_keys)
    columns = jnp.arange(N_GZ, dtype=jnp.int32)[None, :]
    position_in = places[groups, columns]
    return (groups * N_GZ + position_in).astype(jnp.int32)


def place_ends(array, key, low, high):
    longest = array.shape.index(max(array.shape))
    spots = []
    for shift in (0, 1):
        where = [jax.random.randint(jax.random.fold_in(key, axis), (), 0, length) for axis, length in enumerate(array.shape)]
        where[longest] = (where[longest] + shift) % array.shape[longest]
        spots.append(tuple(where))
    return array.at[spots[0]].set(low).at[spots[1]].set(high)


def level_of(stream_key, extent, shards, smallest, high):
    factor_of = 1.0
    for dim, parts in shards:
        heights = jax.random.uniform(jax.random.fold_in(jax.random.fold_in(stream_key, 6), dim), (parts,), jnp.float32, smallest / len(shards), high / len(shards))
        factor_of = factor_of * jnp.repeat(jnp.exp(heights), extent[dim] // parts).reshape((-1,) + (1,) * (len(extent) - 1 - dim))
    return factor_of


def normal_values(key, extent, deviation, bound, pieces=(), kind=jnp.bfloat16):
    result = jax.random.normal(key, extent, jnp.float32) * deviation
    if len(pieces) > 0:
        result = level_of(key, extent, pieces, -0.22, 0.18) * result
    return jnp.clip(result, min=-bound, max=bound).astype(kind)


def setup_inputs(seed: int = 0) -> dict:
    key_list = jax.random.split(jax.random.key(seed), 5)
    return {
        "probe_vectors": normal_values(key_list[0], (K, NX, NY, NZ), 1.0, 6.0, ((1, 8), (2, 4), (3, 16)), jnp.float32),
        "layer_ids": place_ends(jax.random.randint(key_list[1], (NX, NY, NZ), 0, LAYERS), jax.random.fold_in(key_list[1], 1), 0, LAYERS - 1).astype(jnp.int32),
        "layer_kappa": jnp.clip(jnp.exp(jax.random.uniform(key_list[2], (LAYERS,), jnp.float32, math.log(0.1), math.log(10.0))), 0.1, 10.0),
        "slot_order": draw_slot_order(jax.random.fold_in(key_list[4], 71), 0),
    }


upper_edge = 120.0
lower_edge = 24.0
coarse_shift = 1.0

def cheb_factors(step_index):
    center = (upper_edge + lower_edge) / (upper_edge - lower_edge)
    growth = math.log(center + math.sqrt(center * center - 1.0))

    def chebval(degree):
        expo = math.exp(degree * growth)
        return 0.5 * (expo + 1.0 / expo)
    if step_index == 0:
        return (1.0 / chebval(1), 0.0)
    return (2.0 * chebval(step_index) / chebval(step_index + 1), chebval(step_index - 1) / chebval(step_index + 1))

def face_weights(kappa_pad):
    center = kappa_pad[1:-1, 1:-1, 1:-1]
    x_plus = 0.5 * (center + kappa_pad[2:, 1:-1, 1:-1])
    x_minus = 0.5 * (center + kappa_pad[:-2, 1:-1, 1:-1])
    y_plus = 0.5 * (center + kappa_pad[1:-1, 2:, 1:-1])
    y_minus = 0.5 * (center + kappa_pad[1:-1, :-2, 1:-1])
    z_plus = 0.5 * (center + kappa_pad[1:-1, 1:-1, 2:])
    z_minus = 0.5 * (center + kappa_pad[1:-1, 1:-1, :-2])
    diagonal = x_plus + x_minus + y_plus + y_minus + z_plus + z_minus
    return ((x_plus, x_minus, y_plus, y_minus, z_plus, z_minus), diagonal)

def apply_operator(field_pad, weights, diagonal):
    x_plus, x_minus, y_plus, y_minus, z_plus, z_minus = weights
    interior = field_pad[..., 1:-1, 1:-1, 1:-1]
    beside = x_plus * field_pad[..., 2:, 1:-1, 1:-1] + x_minus * field_pad[..., :-2, 1:-1, 1:-1]
    beside = beside + y_plus * field_pad[..., 1:-1, 2:, 1:-1] + y_minus * field_pad[..., 1:-1, :-2, 1:-1]
    beside = beside + z_plus * field_pad[..., 1:-1, 1:-1, 2:] + z_minus * field_pad[..., 1:-1, 1:-1, :-2]
    return diagonal * interior - beside

def cheb_update(current, previous, applied, step_index):
    factor_one, factor_two = cheb_factors(step_index)
    shifted = (upper_edge + lower_edge) / (upper_edge - lower_edge) * current - 2.0 / (upper_edge - lower_edge) * applied
    return factor_one * shifted - factor_two * previous

def split_cells(values):
    return values.reshape(N_GX, CX, N_GY, CY, N_GZ, CZ)

def reference(probe_vectors, layer_ids, layer_kappa, slot_order):
    highest = lax.Precision.HIGHEST
    conductivity = layer_kappa[layer_ids]
    weights, diagonal = face_weights(jnp.pad(conductivity, 1))

    def filtered(vector):
        current = vector
        previous = jnp.zeros_like(vector)
        for step_index in range(PASSES):
            applied = apply_operator(jnp.pad(current, 1), weights, diagonal)
            current, previous = (cheb_update(current, previous, applied, step_index), current)
        return current
    basis = lax.map(filtered, probe_vectors)
    x_cell = jnp.arange(NX) % CX
    y_cell = jnp.arange(NY) % CY
    z_cell = jnp.arange(NZ) % CZ
    x_plus, x_minus, y_plus, y_minus, z_plus, z_minus = weights
    local_weights = (jnp.where((x_cell != CX - 1)[:, None, None], x_plus, 0.0), jnp.where((x_cell != 0)[:, None, None], x_minus, 0.0), jnp.where((y_cell != CY - 1)[None, :, None], y_plus, 0.0), jnp.where((y_cell != 0)[None, :, None], y_minus, 0.0), jnp.where((z_cell != CZ - 1)[None, None, :], z_plus, 0.0), jnp.where((z_cell != 0)[None, None, :], z_minus, 0.0))
    local_image = lax.map(lambda vector: apply_operator(jnp.pad(vector, 1), local_weights, diagonal), basis)
    scaling = 1.0 / math.sqrt(CX * CY * CZ)
    shaped = basis.reshape(K, N_GX, CX, N_GY, CY, N_GZ, CZ)
    shaped_image = local_image.reshape(K, N_GX, CX, N_GY, CY, N_GZ, CZ)
    self_blocks = scaling * jnp.einsum('kaxbycz,laxbycz->abckl', shaped, shaped_image, precision=highest)
    self_blocks = self_blocks + coarse_shift * jnp.eye(K, dtype=jnp.float32)
    x_block = -scaling * jnp.einsum('kabycz,abycz,labycz->abckl', shaped[:, :-1, CX - 1], split_cells(x_plus)[:-1, CX - 1], shaped[:, 1:, 0], precision=highest)
    y_block = -scaling * jnp.einsum('kaxbcz,axbcz,laxbcz->abckl', shaped[:, :, :, :-1, CY - 1], split_cells(y_plus)[:, :, :-1, CY - 1], shaped[:, :, :, 1:, 0], precision=highest)
    z_block = -scaling * jnp.einsum('kaxbyc,axbyc,laxbyc->abckl', shaped[:, :, :, :, :, :-1, CZ - 1], split_cells(z_plus)[:, :, :, :, :-1, CZ - 1], shaped[:, :, :, :, :, 1:, 0], precision=highest)
    position = slot_order.reshape(N_GX, N_GY, N_GZ).astype(jnp.int32)
    blocks = jnp.zeros((DEVICES, K, DEVICES, K), jnp.float32)
    flat_pos = position.ravel()
    blocks = blocks.at[flat_pos, :, flat_pos, :].set(self_blocks.reshape(-1, K, K))
    pairs = ((position[:-1].ravel(), position[1:].ravel(), x_block), (position[:, :-1].ravel(), position[:, 1:].ravel(), y_block), (position[:, :, :-1].ravel(), position[:, :, 1:].ravel(), z_block))
    for lower_pos, upper_pos, block_set in pairs:
        blocks = blocks.at[lower_pos, :, upper_pos, :].set(block_set.reshape(-1, K, K))
        blocks = blocks.at[upper_pos, :, lower_pos, :].set(jnp.swapaxes(block_set, -1, -2).reshape(-1, K, K))
    coarse = blocks.reshape(ORDER, ORDER)
    factored_cols = NPAN * PW
    factor_top = jnp.linalg.cholesky(coarse[:factored_cols, :factored_cols])
    below = jax.scipy.linalg.solve_triangular(factor_top, coarse[factored_cols:, :factored_cols].T, lower=True).T
    trailing = coarse[factored_cols:, factored_cols:] - jnp.dot(below, below.T, precision=highest)
    top_rows = jnp.concatenate([factor_top, jnp.zeros((factored_cols, ORDER - factored_cols), jnp.float32)], 1)
    return jnp.concatenate([top_rows, jnp.concatenate([below, trailing], 1)], 0)
```

```python
import functools
import math

import jax
import jax.numpy as jnp
from jax import lax
from jax.experimental import pallas as pl
from jax.experimental.pallas import tpu as pltpu
from jax.sharding import PartitionSpec as P

PASSES = 4
UPPER = 120.0
LOWER = 24.0
SHIFT = 1.0
F32 = jnp.float32
BF16 = jnp.bfloat16
HIGHEST = lax.Precision.HIGHEST


VM = pl.BlockSpec(memory_space=pltpu.VMEM)
SM = pl.BlockSpec(memory_space=pltpu.SMEM)


def cheb_factors(step_index):
    center = (UPPER + LOWER) / (UPPER - LOWER)
    growth = math.log(center + math.sqrt(center * center - 1.0))

    def chebval(degree):
        expo = math.exp(degree * growth)
        return 0.5 * (expo + 1.0 / expo)

    if step_index == 0:
        return (1.0 / chebval(1), 0.0)
    return (
        2.0 * chebval(step_index) / chebval(step_index + 1),
        chebval(step_index - 1) / chebval(step_index + 1),
    )


def iota(shape, dim):
    return lax.broadcasted_iota(jnp.int32, shape, dim)


def roll(value, shift, axis):
    shift = shift % value.shape[axis]
    if shift == 0:
        return value
    return pltpu.roll(value, shift, axis)


def pack_kernel(vec_ref, ids_ref, kappa_ref, out_ref):
    ids = ids_ref[...]
    kappa = jnp.zeros(ids.shape, F32)
    for layer in range(kappa_ref.shape[0]):
        kappa = jnp.where(ids == layer, kappa_ref[layer], kappa)
    out_ref[:, 0:16, :] = vec_ref[...]
    out_ref[:, 16:32, :] = jnp.broadcast_to(kappa[None], (out_ref.shape[0], 16, 128))


def slab_plane(ref, field, plane):
    i, x = plane // 2, plane % 2
    base = 16 * field + 8 * x
    return jnp.concatenate([ref[4 * i + j, base : base + 8, :] for j in range(4)], axis=0)


def edge_kernel(slab_ref, low_ref, high_ref):
    lane = iota((32, 128), 1)
    for field in range(2):
        low = jnp.zeros((32, 128), F32)
        high = jnp.zeros((32, 128), F32)
        for plane in range(16):
            tile = slab_plane(slab_ref, field, plane)
            here = (lane >> 3) == plane
            low = jnp.where(here, roll(tile, 8 * plane, 1), low)
            high = jnp.where(here, roll(tile, 8 * plane + 8, 1), high)
        low_ref[32 * field : 32 * field + 32, :] = low
        high_ref[32 * field : 32 * field + 32, :] = high


def filter_kernel(
    order_ref, index_ref, slab_ref, left_ref, right_ref, out_ref, coef_ref,
    za, zb, ka, wxp, wxm, wyp, wym, wzp, wzm, dia,
):
    mine = index_ref[0]
    at_z = index_ref[2]
    lane = iota((32, 128), 1)
    zero_plane = jnp.zeros((32, 256), F32)
    for dest, field in ((za, 0), (ka, 1)):
        dest[0] = zero_plane
        dest[17] = zero_plane
        for plane in range(16):
            dest[plane + 1, :, 0:128] = slab_plane(slab_ref, field, plane)
            rows = slice(32 * field, 32 * field + 32)
            right = roll(right_ref[rows, :], -8 * plane, 1)
            left = roll(left_ref[rows, :], 120 - 8 * plane, 1)
            dest[plane + 1, :, 128:256] = jnp.where(
                lane < 8, right, jnp.where(lane >= 120, left, 0.0)
            )
    zb[0] = zero_plane
    zb[17] = zero_plane
    wide = iota((32, 256), 1)
    row = iota((32, 256), 0)
    inside = (
        (wide < 128) | ((wide < 192) & (at_z < 15)) | ((wide >= 192) & (at_z > 0))
    )
    half = 0.5 * 2.0 / (UPPER - LOWER)
    center = (UPPER + LOWER) / (UPPER - LOWER)

    def weights(plane, carry):
        k = ka[plane + 1]
        xp = half * (k + ka[plane + 2])
        xm = half * (k + ka[plane])
        yp = half * (k + jnp.where(row == 31, 0.0, roll(k, 31, 0)))
        ym = half * (k + jnp.where(row == 0, 0.0, roll(k, 1, 0)))
        zp = half * (k + roll(k, 255, 1))
        zm = half * (k + roll(k, 1, 1))
        total = xp + xm + yp + ym + zp + zm
        wxp[plane] = jnp.where(inside, xp, 0.0)
        wxm[plane] = jnp.where(inside, xm, 0.0)
        wyp[plane] = jnp.where(inside & (row != 31), yp, 0.0)
        wym[plane] = jnp.where(inside & (row != 0), ym, 0.0)
        wzp[plane] = jnp.where(inside, zp, 0.0)
        wzm[plane] = jnp.where(inside, zm, 0.0)
        dia[plane] = jnp.where(inside, center - total, 0.0)
        return carry

    lax.fori_loop(0, 16, weights, 0)
    for step in range(PASSES):
        src, dest = (za, zb) if step % 2 == 0 else (zb, za)
        one, two = cheb_factors(step)

        def sweep(plane, carry, src=src, dest=dest, one=one, two=two, step=step):
            z = src[plane + 1]
            acc = dia[plane] * z
            acc = acc + wxp[plane] * src[plane + 2] + wxm[plane] * src[plane]
            acc = acc + wyp[plane] * roll(z, 31, 0) + wym[plane] * roll(z, 1, 0)
            acc = acc + wzp[plane] * roll(z, 255, 1) + wzm[plane] * roll(z, 1, 1)
            acc = one * acc
            if step > 0:
                acc = acc - two * dest[plane + 1]
            dest[plane + 1] = acc
            return carry

        lax.fori_loop(0, 16, sweep, 0)

    sub = iota((8, 128), 0)
    lane8 = iota((8, 128), 1)
    zero_row = jnp.zeros((1, 128), F32)
    for r in range(32):
        i, j = r // 4, r % 4
        dest = lax.shift_right_logical(order_ref[r, at_z], 4)
        rows = slice(8 * j, 8 * j + 8)
        out_ref[dest, 0:8, :] = za[2 * i + 1, rows, 0:128]
        out_ref[dest, 8:16, :] = za[2 * i + 2, rows, 0:128]
        out_ref[dest, 16:24, :] = za[2 * i, rows, 0:128]
        out_ref[dest, 24:32, :] = za[2 * i + 3, rows, 0:128]
        packed = jnp.zeros((8, 128), F32)
        for x in range(2):
            out_ref[dest, 32 + x : 33 + x, :] = (
                za[2 * i + 1 + x, 8 * j - 1 : 8 * j, 0:128] if j > 0 else zero_row
            )
            out_ref[dest, 34 + x : 35 + x, :] = (
                za[2 * i + 1 + x, 8 * j + 8 : 8 * j + 9, 0:128] if j < 3 else zero_row
            )
            tile = za[2 * i + 1 + x, rows, 128:256]
            packed = jnp.where(lane8 == 8 * x + sub, tile[:, 127:128], packed)
            packed = jnp.where(lane8 == 16 + 8 * x + sub, tile[:, 0:1], packed)
        out_ref[dest, 36:37, :] = jnp.sum(packed, axis=0, keepdims=True)
        out_ref[dest, 37:40, :] = jnp.zeros((3, 128), F32)

        def coefficients(slot, i=i, j=j, rows=rows):
            coef_ref[slot, 0:8, :] = ka[2 * i + 1, rows, 0:128]
            coef_ref[slot, 8:16, :] = ka[2 * i + 2, rows, 0:128]
            coef_ref[slot, 16:24, :] = ka[2 * i, rows, 0:128]
            coef_ref[slot, 24:32, :] = ka[2 * i + 3, rows, 0:128]
            for x in range(2):
                coef_ref[slot, 32 + x : 33 + x, :] = (
                    ka[2 * i + 1 + x, 8 * j - 1 : 8 * j, 0:128] if j > 0 else zero_row
                )
                coef_ref[slot, 34 + x : 35 + x, :] = (
                    ka[2 * i + 1 + x, 8 * j + 8 : 8 * j + 9, 0:128] if j < 3 else zero_row
                )
                coef_ref[slot, 40 + 8 * x : 48 + 8 * x, :] = ka[2 * i + 1 + x, rows, 128:256]

        @pl.when(dest == mine)
        def _(coefficients=coefficients):
            coefficients(0)

        @pl.when(dest == 0)
        def _(coefficients=coefficients):
            coefficients(1)

    first = out_ref[0, 0:40, :]

    def spread(dest, carry):
        out_ref[dest, 40:80, :] = first
        return carry

    lax.fori_loop(0, 32, spread, 0)


def nt_dot(a, b):
    return lax.dot_general(
        a, b, (((1,), (1,)), ((), ())), precision=HIGHEST, preferred_element_type=F32
    )


def galerkin_kernel(data_ref, coef_ref, out_ref, left, image, cross):
    sub = iota((8, 128), 0)
    lane8 = iota((8, 128), 1)
    lane = iota((32, 128), 1)
    scaling = 1.0 / math.sqrt(2048.0)
    eye = (iota((32, 32), 0) == iota((32, 32), 1)).astype(F32)
    for part in range(2):
        base = 40 * part

        def field(r, base=base):
            return data_ref[pl.ds(base + r, 32, stride=80), :]

        def span(r):
            return slice(128 * r, 128 * r + 128)

        for r in range(16):
            left[:, span(r)] = field(r)
        k0 = coef_ref[part, 0:8, :]
        k1 = coef_ref[part, 8:16, :]
        km = coef_ref[part, 16:24, :]
        kp = coef_ref[part, 24:32, :]
        columns = jnp.zeros((32, 128), F32)
        y_low, y_high = [], []
        for x in range(2):
            k = (k0, k1)[x]
            below = coef_ref[part, 32 + x : 33 + x, :]
            above = coef_ref[part, 34 + x : 35 + x, :]
            ends = coef_ref[part, 40 + 8 * x : 48 + 8 * x, :]
            xm = 0.5 * (k + (km, k0)[x])
            xp = 0.5 * (k + (k1, kp)[x])
            ym = 0.5 * (k + jnp.where(sub == 0, below, roll(k, 1, 0)))
            yp = 0.5 * (k + jnp.where(sub == 7, above, roll(k, 7, 0)))
            zm = 0.5 * (k + jnp.where(lane8 == 0, ends[:, 127:128], roll(k, 1, 1)))
            zp = 0.5 * (k + jnp.where(lane8 == 127, ends[:, 0:1], roll(k, 127, 1)))
            diag = xp + xm + yp + ym + zp + zm
            zm_in = jnp.where(lane8 == 0, 0.0, zm)
            zp_in = jnp.where(lane8 == 127, 0.0, zp)
            for y in range(8):
                r = 8 * x + y
                one = slice(y, y + 1)
                z = left[:, span(r)]
                beside = zp_in[one] * roll(z, 127, 1) + zm_in[one] * roll(z, 1, 1)
                if x == 0:
                    beside = beside + xp[one] * left[:, span(r + 8)]
                else:
                    beside = beside + xm[one] * left[:, span(r - 8)]
                if y < 7:
                    beside = beside + yp[one] * left[:, span(r + 1)]
                if y > 0:
                    beside = beside + ym[one] * left[:, span(r - 1)]
                image[:, span(r)] = diag[one] * z - beside
                if x == 0:
                    cross[:, span(r)] = xm[one] * field(16 + y)
                else:
                    cross[:, span(r)] = xp[one] * field(24 + y)
                if y == 0:
                    y_low.append((r, ym[one] * field(32 + x)))
                if y == 7:
                    y_high.append((r, yp[one] * field(34 + x)))
                columns = jnp.where(lane == r, roll(zm[one] * z, r, 1), columns)
                columns = jnp.where(lane == 16 + r, roll(zp[one] * z, 17 + r, 1), columns)
        rows = slice(32 * part, 32 * part + 32)
        own = nt_dot(left[...], image[...])
        out_ref[rows, 0:32] = scaling * own + SHIFT * eye
        out_ref[rows, 32:64] = -scaling * nt_dot(left[:, 0:1024], cross[:, 0:1024])
        out_ref[rows, 64:96] = -scaling * nt_dot(left[:, 1024:2048], cross[:, 1024:2048])
        for at, pair in ((96, y_low), (128, y_high)):
            block = sum(nt_dot(left[:, span(r)], ghost) for r, ghost in pair)
            out_ref[rows, at : at + 32] = -scaling * block
        ghost = field(36)
        low = jnp.where(lane < 16, columns, 0.0)
        high = jnp.where((lane >= 16) & (lane < 32), columns, 0.0)
        out_ref[rows, 160:192] = -scaling * nt_dot(low, ghost)
        out_ref[rows, 192:224] = -scaling * nt_dot(high, ghost)
        out_ref[rows, 224:256] = jnp.zeros((32, 32), F32)


def halves(value):
    high = value.astype(BF16)
    return high, (value - high.astype(F32)).astype(BF16)


def dot3(a, b, dims):
    ah, al = a
    bh, bl = b

    def one(p, q):
        return lax.dot_general(p, q, (dims, ((), ())), preferred_element_type=F32)

    return one(ah, bh) + (one(ah, bl) + one(al, bh))


NN = ((1,), (0,))
NT = ((1,), (1,))


def factor_kernel(
    order_ref, index_ref, rows_ref, data_ref, out_ref,
    diag, al, il, tinv, pm, am, xm, mm, lt, ua, vm, cm, um, ready, done, count,
):
    mine = index_ref[0]
    at_z = index_ref[2]
    lane = iota((32, 128), 1)
    corner = (mine == 0) & (at_z == 0)

    def base(l):
        return rows_ref[0, l]

    def own_row(l):
        return rows_ref[1, l]

    def slot0(l):
        return order_ref[base(l), l]

    def place(dest, row, tile, sub, source_row, u, clear=None):
        source = data_ref[pl.ds(source_row, 32), 128 * (u // 4) : 128 * (u // 4) + 128]
        moved = pltpu.roll(source, lax.rem(32 * sub - 32 * (u % 4) + 128, 128), 1)
        here = (lane >> 5) == sub
        at = (pl.ds(row, 32), pl.ds(pl.multiple_of(128 * tile, 128), 128))
        dest[at] = dest[at] + jnp.where(here, moved, 0.0)

    def linked(l):
        return base(l) == base(l + 1)

    for l in range(16):
        done[l] = 0
        diag[32 * l : 32 * l + 32, :] = data_ref[64 * l + 32 : 64 * l + 64, 0:128]
    count[0] = 0
    tinv[...] = jnp.zeros(tinv.shape, F32)
    pm[...] = jnp.zeros(pm.shape, F32)
    any_link = base(0) == base(1)
    for l in range(1, 15):
        any_link = any_link | linked(l)
    whole = any_link | corner

    @pl.when(whole)
    def _():
        am[...] = jnp.zeros(am.shape, F32)
        lt[...] = jnp.zeros(lt.shape, F32)
        mm[...] = jnp.zeros(mm.shape, F32)
        xm[...] = (iota((512, 512), 0) == iota((512, 512), 1)).astype(F32)
        for l in range(16):
            place(am, 32 * l, l // 4, l % 4, 64 * l + 32, 0)
            if l > 0:

                @pl.when(linked(l - 1))
                def _(l=l):
                    place(am, 32 * l, (l - 1) // 4, (l - 1) % 4, 64 * l + 32, 5)

            if l < 15:

                @pl.when(linked(l))
                def _(l=l):
                    place(am, 32 * l, (l + 1) // 4, (l + 1) % 4, 64 * l + 32, 6)

    def find_ready():
        previous = jnp.int32(99)
        for l in range(16):
            if l > 0:
                previous = jnp.where(linked(l - 1), previous, 99)
            open_ = done[l] == 0
            ready[l] = jnp.where(open_ & (previous > slot0(l)), 1, 0)
            previous = jnp.where(open_, slot0(l), previous)
        previous = jnp.int32(99)
        for l in reversed(range(16)):
            if l < 15:
                previous = jnp.where(linked(l), previous, 99)
            open_ = done[l] == 0
            ready[l] = jnp.where(open_ & (previous > slot0(l)), ready[l], 0)
            previous = jnp.where(open_, slot0(l), previous)
        total = jnp.int32(0)
        for l in range(16):
            done[l] = done[l] + ready[l]
            total = total + done[l]
        count[0] = total

    def batched_inverse():
        for i in range(32):
            al[i, :, 0:16] = jnp.transpose(diag[pl.ds(i, 16, stride=32), :])[0:32, :]
            il[i, :, :] = (iota((32, 128), 0) == i).astype(F32)
        for j in range(32):
            low = 8 * (j // 8)
            pivot = al[j, j : j + 1, :]
            inv = lax.rsqrt(pivot)
            inv = inv * (1.5 - 0.5 * pivot * inv * inv)
            row_a = al[j, low:32, :] * inv
            row_i = il[j, 0 : low + 8, :] * inv
            il[j, 0 : low + 8, :] = row_i

            def update(i, carry, j=j, low=low, row_a=row_a, row_i=row_i, inv=inv):
                f = al[i, j : j + 1, :] * inv
                al[i, low:32, :] = al[i, low:32, :] - f * row_a
                il[i, 0 : low + 8, :] = il[i, 0 : low + 8, :] - f * row_i
                return carry

            lax.fori_loop(j + 1, 32, update, 0, unroll=4 if j < 28 else 1)
        for i in range(32):
            tinv[pl.ds(i, 16, stride=32), :] = jnp.where(
                iota((16, 128), 1) < 32,
                jnp.transpose(jnp.concatenate([il[i], jnp.zeros((96, 128), F32)], axis=0))[0:16, :],
                0.0,
            )
        for l in range(16):
            at = (slice(32 * l, 32 * l + 32), slice(128 * (l // 4), 128 * (l // 4) + 128))
            moved = roll(tinv[32 * l : 32 * l + 32, :], 32 * (l % 4), 1)
            pm[at] = jnp.where(ready[l] > 0, moved, 0.0)

    def nn(a, b):
        return lax.dot_general(a, b, (NN, ((), ())), precision=HIGHEST, preferred_element_type=F32)

    find_ready()
    batched_inverse()

    @pl.when(jnp.logical_not(whole))
    def _():
        mm[...] = pm[...]

    @pl.when(whole)
    def _():
        def level(unused):
            for c in range(4):
                rows = slice(128 * c, 128 * c + 128)
                part = nn(pm[rows, :], am[...])
                ua[rows, :] = part
                lt[rows, :] = lt[rows, :] + part
                part = nn(pm[rows, :], xm[...])
                vm[rows, :] = part
                mm[rows, :] = mm[rows, :] + part
            more = count[0] < 16

            @pl.when(more)
            def _():
                turned = jnp.transpose(ua[...])
                column = iota((1, 512), 1) >> 5
                keep = jnp.ones((1, 512), F32)
                for l in range(16):
                    keep = jnp.where((column == l) & (done[l] > 0), 0.0, keep)
                for c in range(4):
                    rows = slice(128 * c, 128 * c + 128)
                    am[rows, :] = jnp.where(
                        keep > 0.0, am[rows, :] - nn(turned[rows, :], ua[...]), 0.0
                    )
                    xm[rows, :] = xm[rows, :] - nn(turned[rows, :], vm[...])
                for l in range(16):

                    @pl.when(done[l] > 0)
                    def _(l=l):
                        am[32 * l : 32 * l + 32, :] = jnp.zeros((32, 512), F32)

                    @pl.when(done[l] == 0)
                    def _(l=l):
                        at = (
                            slice(32 * l, 32 * l + 32),
                            slice(128 * (l // 4), 128 * (l // 4) + 128),
                        )
                        diag[32 * l : 32 * l + 32, :] = roll(am[at], -32 * (l % 4), 1)

                find_ready()
                batched_inverse()

            return more

        lax.while_loop(lambda more: more, level, jnp.bool_(True))

    def row_at(l):
        return 32 * (order_ref[own_row(l), l] - 16 * mine)

    @pl.when(mine > 0)
    def _():
        ua[...] = jnp.zeros(ua.shape, F32)
        for l in range(16):
            r = own_row(l)
            step = base(l) - r
            col = lax.rem(r, 4)
            for u, hit in (
                (1, step == -4),
                (2, step == 4),
                (3, (step == -1) & (col > 0)),
                (4, (step == 1) & (col < 3)),
            ):

                @pl.when(hit)
                def _(l=l, u=u):
                    place(ua, pl.multiple_of(row_at(l), 32), l // 4, l % 4, 64 * l, u)

            for u, other in ((5, l - 1), (6, l + 1)):
                if 0 <= other < 16:

                    @pl.when(base(other) == r)
                    def _(l=l, u=u, other=other):
                        place(
                            ua, pl.multiple_of(row_at(l), 32), other // 4, other % 4, 64 * l, u
                        )

        wide = halves(mm[...])
        for c in range(4):
            rows = slice(128 * c, 128 * c + 128)
            vm[rows, :] = dot3(halves(ua[rows, :]), wide, NT)

    def neighbours(r, l):
        col = lax.rem(r, 4)
        found = [
            (1, r >= 4, r - 4, l),
            (2, r < 28, r + 4, l),
            (3, col > 0, r - 1, l),
            (4, col < 3, r + 1, l),
        ]
        if l > 0:
            found.append((5, r >= 0, r, l - 1))
        if l < 15:
            found.append((6, r >= 0, r, l + 1))
        return found

    def column_of(r, l):
        slot = order_ref[jnp.clip(r, 0, 31), l]
        return jnp.where(slot >= 16, slot, -1) - 32 * at_z

    @pl.when(mine > 0)
    def _():
        cm[...] = jnp.zeros(cm.shape, F32)
        for l in range(16):
            for u, ok, r, ll in neighbours(base(l), l):
                at = column_of(r, ll)

                @pl.when(ok & (at >= 0) & (at < 32))
                def _(l=l, u=u, at=at):
                    place(
                        cm, 32 * l, lax.shift_right_logical(at, 2), lax.rem(at, 4), 64 * l + 32, u
                    )

        for c in range(8):
            cols = slice(128 * c, 128 * c + 128)
            um[:, cols] = dot3(halves(mm[...]), halves(cm[:, cols]), NN)
        wide = halves(um[...])
        for c in range(4):
            rows = slice(128 * c, 128 * c + 128)
            out_ref[rows, :] = -dot3(halves(vm[rows, :]), wide, NN)
        for l in range(16):
            r = own_row(l)
            for u, ok, rr, ll in [(0, r >= 0, r, l)] + neighbours(r, l):
                at = column_of(rr, ll)

                @pl.when(ok & (at >= 0) & (at < 32))
                def _(l=l, u=u, at=at):
                    place(
                        out_ref, pl.multiple_of(row_at(l), 32),
                        lax.shift_right_logical(at, 2), lax.rem(at, 4), 64 * l, u,
                    )

    @pl.when(mine == 0)
    def _():
        out_ref[...] = jnp.zeros(out_ref.shape, F32)

    @pl.when(corner)
    def _():
        turned = jnp.transpose(lt[...])
        for l in range(16):
            vm[pl.ds(pl.multiple_of(32 * slot0(l), 32), 32), :] = turned[32 * l : 32 * l + 32, :]

    @pl.when(at_z == 0)
    def _():
        tall = iota((512, 128), 1)
        out_ref[:, 0:512] = jnp.zeros((512, 512), F32)
        for l in range(16):
            slot = slot0(l)
            sub = lax.rem(slot, 4)
            source = vm[:, 128 * (l // 4) : 128 * (l // 4) + 128]
            moved = pltpu.roll(source, lax.rem(32 * sub - 32 * (l % 4) + 128, 128), 1)
            tile = pl.multiple_of(128 * lax.shift_right_logical(slot, 2), 128)
            at = (slice(0, 512), pl.ds(tile, 128))
            out_ref[at] = jnp.where((tall >> 5) == sub, moved, out_ref[at])

    @pl.when(corner)
    def _():
        lower = iota((512, 512), 0) >= iota((512, 512), 1)
        out_ref[:, 0:512] = jnp.where(lower, out_ref[:, 0:512], 0.0)


def on_device(probe_vectors, layer_ids, layer_kappa, slot_order):
    index_x = lax.axis_index("gx")
    index_y = lax.axis_index("gy")
    index_z = lax.axis_index("gz")
    grid_z = lax.axis_size("gz")
    mine = index_x * lax.axis_size("gy") + index_y
    group_of = slot_order // 16
    ids = jnp.arange(32, dtype=jnp.int32)[:, None]
    wanted = jnp.stack([jnp.zeros((), jnp.int32), mine])
    rows = jnp.sum(jnp.where(group_of[None] == wanted[:, None, None], ids[None], 0), axis=1)
    index = jnp.stack([mine, jnp.zeros((), jnp.int32), index_z]).astype(jnp.int32)

    send = pl.pallas_call(
        pack_kernel,
        out_shape=jax.ShapeDtypeStruct((32, 32, 128), F32),
        in_specs=[VM, VM, SM],
        out_specs=VM,
    )(probe_vectors.reshape(32, 16, 128), layer_ids.reshape(16, 128), layer_kappa)
    slab = lax.all_to_all(send, ("gx", "gy"), 0, 0, tiled=True)
    low, high = pl.pallas_call(
        edge_kernel,
        out_shape=[jax.ShapeDtypeStruct((64, 128), F32)] * 2,
        in_specs=[VM],
        out_specs=[VM, VM],
    )(slab)
    upward = [(i, i + 1) for i in range(grid_z - 1)]
    downward = [(b, a) for a, b in upward]
    from_left = lax.ppermute(high, "gz", upward)
    from_right = lax.ppermute(low, "gz", downward)
    pieces, coef = pl.pallas_call(
        filter_kernel,
        out_shape=[
            jax.ShapeDtypeStruct((32, 80, 128), F32),
            jax.ShapeDtypeStruct((2, 56, 128), F32),
        ],
        in_specs=[SM, SM, VM, VM, VM],
        out_specs=[VM, VM],
        scratch_shapes=[pltpu.VMEM((18, 32, 256), F32)] * 3 + [pltpu.VMEM((16, 32, 256), F32)] * 7,
    )(slot_order, index, slab, from_left, from_right)
    owned = lax.all_to_all(pieces, ("gx", "gy"), 0, 0, tiled=True)
    blocks = pl.pallas_call(
        galerkin_kernel,
        out_shape=jax.ShapeDtypeStruct((64, 256), F32),
        in_specs=[VM, VM],
        out_specs=VM,
        scratch_shapes=[pltpu.VMEM((32, 2048), F32)] * 3,
    )(owned.reshape(32 * 80, 128), coef)
    spread = lax.all_to_all(
        jnp.broadcast_to(blocks[None], (16, 64, 256)), "gz", 0, 0, tiled=True
    )
    big = pltpu.VMEM((512, 512), F32)
    return pl.pallas_call(
        factor_kernel,
        out_shape=jax.ShapeDtypeStruct((512, 1024), F32),
        in_specs=[SM, SM, SM, VM],
        out_specs=VM,
        scratch_shapes=[
            pltpu.VMEM((512, 128), F32),
            pltpu.VMEM((32, 32, 128), F32),
            pltpu.VMEM((32, 32, 128), F32),
            pltpu.VMEM((512, 128), F32),
            big, big, big, big, big, big, big,
            pltpu.VMEM((512, 1024), F32),
            pltpu.VMEM((512, 1024), F32),
            pltpu.SMEM((16,), jnp.int32),
            pltpu.SMEM((16,), jnp.int32),
            pltpu.SMEM((1,), jnp.int32),
        ],
    )(slot_order, index, rows, spread.reshape(1024, 256))


def solution(mesh):
    in_specs = (P(None, "gx", "gy", "gz"), P("gx", "gy", "gz"), P(), P())
    out_specs = P(("gx", "gy"), "gz")
    return jax.shard_map(
        on_device, mesh=mesh, in_specs=in_specs, out_specs=out_specs, check_vma=False
    )
```

```python
import functools
import math

import jax
import jax.numpy as jnp
from jax import lax
from jax.experimental import pallas as pl
from jax.experimental.pallas import tpu as pltpu
from jax.sharding import PartitionSpec as P

PASSES = 4
UPPER = 120.0
LOWER = 24.0
SHIFT = 1.0
F32 = jnp.float32
BF16 = jnp.bfloat16
HIGHEST = lax.Precision.HIGHEST


VM = pl.BlockSpec(memory_space=pltpu.VMEM)
SM = pl.BlockSpec(memory_space=pltpu.SMEM)


def cheb_factors(step_index):
    center = (UPPER + LOWER) / (UPPER - LOWER)
    growth = math.log(center + math.sqrt(center * center - 1.0))

    def chebval(degree):
        expo = math.exp(degree * growth)
        return 0.5 * (expo + 1.0 / expo)

    if step_index == 0:
        return (1.0 / chebval(1), 0.0)
    return (
        2.0 * chebval(step_index) / chebval(step_index + 1),
        chebval(step_index - 1) / chebval(step_index + 1),
    )


def iota(shape, dim):
    return lax.broadcasted_iota(jnp.int32, shape, dim)


def roll(value, shift, axis):
    shift = shift % value.shape[axis]
    if shift == 0:
        return value
    return pltpu.roll(value, shift, axis)


def pack_kernel(vec_ref, ids_ref, kappa_ref, out_ref):
    ids = ids_ref[...]
    kappa = jnp.zeros(ids.shape, F32)
    for layer in range(kappa_ref.shape[0]):
        kappa = jnp.where(ids == layer, kappa_ref[layer], kappa)
    out_ref[:, 0:16, :] = vec_ref[...]
    out_ref[:, 16:32, :] = jnp.broadcast_to(kappa[None], (out_ref.shape[0], 16, 128))


def slab_plane(ref, field, plane):
    i, x = plane // 2, plane % 2
    base = 16 * field + 8 * x
    return jnp.concatenate([ref[4 * i + j, base : base + 8, :] for j in range(4)], axis=0)


def edge_kernel(slab_ref, low_ref, high_ref):
    lane = iota((32, 128), 1)
    for field in range(2):
        low = jnp.zeros((32, 128), F32)
        high = jnp.zeros((32, 128), F32)
        for plane in range(16):
            tile = slab_plane(slab_ref, field, plane)
            here = (lane >> 3) == plane
            low = jnp.where(here, roll(tile, 8 * plane, 1), low)
            high = jnp.where(here, roll(tile, 8 * plane + 8, 1), high)
        low_ref[32 * field : 32 * field + 32, :] = low
        high_ref[32 * field : 32 * field + 32, :] = high


def filter_kernel(
    order_ref, index_ref, slab_ref, left_ref, right_ref, out_ref, coef_ref,
    za, zb, ka, wxp, wxm, wyp, wym, wzp, wzm, dia,
):
    mine = index_ref[0]
    at_z = index_ref[2]
    lane = iota((32, 128), 1)
    zero_plane = jnp.zeros((32, 256), F32)
    for dest, field in ((za, 0), (ka, 1)):
        dest[0] = zero_plane
        dest[17] = zero_plane
        for plane in range(16):
            dest[plane + 1, :, 0:128] = slab_plane(slab_ref, field, plane)
            rows = slice(32 * field, 32 * field + 32)
            right = roll(right_ref[rows, :], -8 * plane, 1)
            left = roll(left_ref[rows, :], 120 - 8 * plane, 1)
            dest[plane + 1, :, 128:256] = jnp.where(
                lane < 8, right, jnp.where(lane >= 120, left, 0.0)
            )
    zb[0] = zero_plane
    zb[17] = zero_plane
    wide = iota((32, 256), 1)
    row = iota((32, 256), 0)
    inside = (
        (wide < 128) | ((wide < 192) & (at_z < 15)) | ((wide >= 192) & (at_z > 0))
    )
    half = 0.5 * 2.0 / (UPPER - LOWER)
    center = (UPPER + LOWER) / (UPPER - LOWER)

    def weights(plane, carry):
        k = ka[plane + 1]
        xp = half * (k + ka[plane + 2])
        xm = half * (k + ka[plane])
        yp = half * (k + jnp.where(row == 31, 0.0, roll(k, 31, 0)))
        ym = half * (k + jnp.where(row == 0, 0.0, roll(k, 1, 0)))
        zp = half * (k + roll(k, 255, 1))
        zm = half * (k + roll(k, 1, 1))
        total = xp + xm + yp + ym + zp + zm
        wxp[plane] = jnp.where(inside, xp, 0.0)
        wxm[plane] = jnp.where(inside, xm, 0.0)
        wyp[plane] = jnp.where(inside & (row != 31), yp, 0.0)
        wym[plane] = jnp.where(inside & (row != 0), ym, 0.0)
        wzp[plane] = jnp.where(inside, zp, 0.0)
        wzm[plane] = jnp.where(inside, zm, 0.0)
        dia[plane] = jnp.where(inside, center - total, 0.0)
        return carry

    lax.fori_loop(0, 16, weights, 0)
    for step in range(PASSES):
        src, dest = (za, zb) if step % 2 == 0 else (zb, za)
        one, two = cheb_factors(step)

        def sweep(plane, carry, src=src, dest=dest, one=one, two=two, step=step):
            z = src[plane + 1]
            acc = dia[plane] * z
            acc = acc + wxp[plane] * src[plane + 2] + wxm[plane] * src[plane]
            acc = acc + wyp[plane] * roll(z, 31, 0) + wym[plane] * roll(z, 1, 0)
            acc = acc + wzp[plane] * roll(z, 255, 1) + wzm[plane] * roll(z, 1, 1)
            acc = one * acc
            if step > 0:
                acc = acc - two * dest[plane + 1]
            dest[plane + 1] = acc
            return carry

        lax.fori_loop(0, 16, sweep, 0)

    sub = iota((8, 128), 0)
    lane8 = iota((8, 128), 1)
    zero_row = jnp.zeros((1, 128), F32)
    for r in range(32):
        i, j = r // 4, r % 4
        dest = lax.shift_right_logical(order_ref[r, at_z], 4)
        rows = slice(8 * j, 8 * j + 8)
        out_ref[dest, 0:8, :] = za[2 * i + 1, rows, 0:128]
        out_ref[dest, 8:16, :] = za[2 * i + 2, rows, 0:128]
        out_ref[dest, 16:24, :] = za[2 * i, rows, 0:128]
        out_ref[dest, 24:32, :] = za[2 * i + 3, rows, 0:128]
        packed = jnp.zeros((8, 128), F32)
        for x in range(2):
            out_ref[dest, 50 + x : 51 + x, :] = (
                za[2 * i + 1 + x, 8 * j - 1 : 8 * j, 0:128] if j > 0 else zero_row
            )
            out_ref[dest, 52 + x : 53 + x, :] = (
                za[2 * i + 1 + x, 8 * j + 8 : 8 * j + 9, 0:128] if j < 3 else zero_row
            )
            tile = za[2 * i + 1 + x, rows, 128:256]
            packed = jnp.where(lane8 == 8 * x + sub, tile[:, 127:128], packed)
            packed = jnp.where(lane8 == 16 + 8 * x + sub, tile[:, 0:1], packed)
        out_ref[dest, 54:55, :] = jnp.sum(packed, axis=0, keepdims=True)
        out_ref[dest, 55:56, :] = zero_row

        def coefficients(slot, i=i, j=j, rows=rows):
            coef_ref[slot, 0:8, :] = ka[2 * i + 1, rows, 0:128]
            coef_ref[slot, 8:16, :] = ka[2 * i + 2, rows, 0:128]
            coef_ref[slot, 16:24, :] = ka[2 * i, rows, 0:128]
            coef_ref[slot, 24:32, :] = ka[2 * i + 3, rows, 0:128]
            for x in range(2):
                coef_ref[slot, 32 + x : 33 + x, :] = (
                    ka[2 * i + 1 + x, 8 * j - 1 : 8 * j, 0:128] if j > 0 else zero_row
                )
                coef_ref[slot, 34 + x : 35 + x, :] = (
                    ka[2 * i + 1 + x, 8 * j + 8 : 8 * j + 9, 0:128] if j < 3 else zero_row
                )
                coef_ref[slot, 40 + 8 * x : 48 + 8 * x, :] = ka[2 * i + 1 + x, rows, 128:256]

        @pl.when(dest == mine)
        def _(coefficients=coefficients):
            coefficients(0)

        @pl.when(dest == 0)
        def _(coefficients=coefficients):
            coefficients(1)

    first = [out_ref[0, 8 * n : 8 * n + 8, :] for n in range(4)]
    edges = [out_ref[0, 50 + n : 51 + n, :] for n in range(4)]
    ends = out_ref[0, 54:55, :]
    lane1 = iota((1, 128), 1)
    for core in range(2):
        body = jnp.concatenate(
            [pack_half(first[0], first[1], core), pack_half(first[2], first[3], core)], axis=0
        )
        sides = jnp.concatenate(
            [pack_half(edges[0], edges[1], core), pack_half(edges[2], edges[3], core)], axis=0
        )
        at = 64 if core == 0 else 63
        below = 40 if core == 0 else 32
        packed = jnp.zeros((8, 128), F32)
        for x in range(2):
            column = first[x][:, at : at + 1]
            packed = jnp.where(lane8 == below + 64 * x + sub, column, packed)
        line = jnp.sum(packed, axis=0, keepdims=True)
        outer = 32 if core == 0 else 40
        start = 0 if core == 0 else 16
        for x in range(2):
            here = (lane1 >> 3) == (outer + 64 * x) // 8
            line = jnp.where(here, roll(ends, outer + 64 * x - start - 8 * x, 1), line)

        def spread(k, carry, core=core, body=body, sides=sides, line=line):
            dest = 2 * k + core
            out_ref[dest, 32:48, :] = body
            out_ref[dest, 48:50, :] = sides
            out_ref[dest, 54:55, :] = out_ref[dest, 54:55, :] + line
            return carry

        lax.fori_loop(0, 16, spread, 0)


def pack_half(even, odd, core):
    lane = iota(even.shape, 1)
    if core == 0:
        return jnp.where(lane < 64, even, roll(odd, 64, 1))
    return jnp.where(lane < 64, roll(even, 64, 1), odd)


def nt_dot(a, b):
    return lax.dot_general(
        a, b, (((1,), (1,)), ((), ())), precision=HIGHEST, preferred_element_type=F32
    )


def galerkin_kernel(index_ref, data_ref, coef_ref, out_ref, left, image, cross, ending):
    sub = iota((8, 128), 0)
    lane8 = iota((8, 128), 1)
    lane = iota((32, 128), 1)
    scaling = 1.0 / math.sqrt(2048.0)
    eye = (iota((32, 32), 0) == iota((32, 32), 1)).astype(F32)
    core = lax.rem(index_ref[0], 2)

    def field(r):
        return data_ref[pl.ds(r, 32, stride=56), :]

    def span(r):
        return slice(128 * r, 128 * r + 128)

    def weights(part):
        k0 = coef_ref[part, 0:8, :]
        k1 = coef_ref[part, 8:16, :]
        km = coef_ref[part, 16:24, :]
        kp = coef_ref[part, 24:32, :]
        found = []
        for x in range(2):
            k = (k0, k1)[x]
            below = coef_ref[part, 32 + x : 33 + x, :]
            above = coef_ref[part, 34 + x : 35 + x, :]
            ends = coef_ref[part, 40 + 8 * x : 48 + 8 * x, :]
            xm = 0.5 * (k + (km, k0)[x])
            xp = 0.5 * (k + (k1, kp)[x])
            ym = 0.5 * (k + jnp.where(sub == 0, below, roll(k, 1, 0)))
            yp = 0.5 * (k + jnp.where(sub == 7, above, roll(k, 7, 0)))
            zm = 0.5 * (k + jnp.where(lane8 == 0, ends[:, 127:128], roll(k, 1, 1)))
            zp = 0.5 * (k + jnp.where(lane8 == 127, ends[:, 0:1], roll(k, 127, 1)))
            found.append((xm, xp, ym, yp, zm, zp, xp + xm + yp + ym + zp + zm))
        return found

    for r in range(16):
        left[:, span(r)] = field(r)
    columns = jnp.zeros((32, 128), F32)
    y_low, y_high = [], []
    for x, (xm, xp, ym, yp, zm, zp, diag) in enumerate(weights(0)):
        zm_in = jnp.where(lane8 == 0, 0.0, zm)
        zp_in = jnp.where(lane8 == 127, 0.0, zp)
        for y in range(8):
            r = 8 * x + y
            one = slice(y, y + 1)
            z = left[:, span(r)]
            beside = zp_in[one] * roll(z, 127, 1) + zm_in[one] * roll(z, 1, 1)
            if x == 0:
                beside = beside + xp[one] * left[:, span(r + 8)]
            else:
                beside = beside + xm[one] * left[:, span(r - 8)]
            if y < 7:
                beside = beside + yp[one] * left[:, span(r + 1)]
            if y > 0:
                beside = beside + ym[one] * left[:, span(r - 1)]
            image[:, span(r)] = diag[one] * z - beside
            cross[:, span(r)] = (xm, xp)[x][one] * field(16 + r)
            if y == 0:
                y_low.append((r, ym[one] * field(50 + x)))
            if y == 7:
                y_high.append((r, yp[one] * field(52 + x)))
            columns = jnp.where(lane == r, roll(zm[one] * z, r, 1), columns)
            columns = jnp.where(lane == 16 + r, roll(zp[one] * z, 17 + r, 1), columns)
    out_ref[0:32, 0:32] = scaling * nt_dot(left[...], image[...]) + SHIFT * eye
    out_ref[0:32, 32:64] = -scaling * nt_dot(left[:, 0:1024], cross[:, 0:1024])
    out_ref[0:32, 64:96] = -scaling * nt_dot(left[:, 1024:2048], cross[:, 1024:2048])
    for at, pair in ((96, y_low), (128, y_high)):
        block = sum(nt_dot(left[:, span(r)], ghost) for r, ghost in pair)
        out_ref[0:32, at : at + 32] = -scaling * block
    ghost = field(54)
    low = jnp.where(lane < 16, columns, 0.0)
    high = jnp.where((lane >= 16) & (lane < 32), columns, 0.0)
    out_ref[0:32, 160:192] = -scaling * nt_dot(low, ghost)
    out_ref[0:32, 192:224] = -scaling * nt_dot(high, ghost)

    even, odd = weights(1)

    def pack(a, b):
        return jnp.where(core == 0, pack_half(a, b, 0), pack_half(a, b, 1))

    w_out = pack(even[0], odd[1])
    w_in = pack(even[1], odd[0])
    ym, yp, zm, zp, diag = (pack(even[n], odd[n]) for n in range(2, 7))
    first8 = (lane8 & 63) == 0
    last8 = (lane8 & 63) == 63
    zm_in = jnp.where(first8 & (core == 0), 0.0, zm)
    zp_in = jnp.where(last8 & (core == 1), 0.0, zp)
    z_out = jnp.where(core == 0, jnp.where(first8, zm, 0.0), jnp.where(last8, zp, 0.0))
    at_first = (lane & 63) == 0
    at_last = (lane & 63) == 63
    for y in range(8):
        left[:, span(y)] = field(32 + y)
    for y in range(8):
        one = slice(y, y + 1)
        z = left[:, span(y)]
        z_low = jnp.where(at_first, roll(ghost, -(32 + y), 1), roll(z, 1, 1))
        z_high = jnp.where(at_last, roll(ghost, 23 - y, 1), roll(z, 127, 1))
        beside = zp_in[one] * z_high + zm_in[one] * z_low + w_in[one] * roll(z, 64, 1)
        if y < 7:
            beside = beside + yp[one] * left[:, span(y + 1)]
        if y > 0:
            beside = beside + ym[one] * left[:, span(y - 1)]
        image[:, span(y)] = diag[one] * z - beside
        side = w_out[one] * field(40 + y)
        cross[:, span(y)] = jnp.where(lane < 64, side, 0.0)
        cross[:, span(8 + y)] = jnp.where(lane < 64, 0.0, side)
        ending[:, span(y)] = z_out[one] * jnp.where(core == 0, z_low, z_high)
    half = slice(0, 1024)
    rows = slice(32, 64)
    shift = jnp.where(core == 0, SHIFT, 0.0) * eye
    out_ref[rows, 0:32] = scaling * nt_dot(left[:, half], image[:, half]) + shift
    out_ref[rows, 32:64] = -scaling * nt_dot(left[:, half], cross[:, half])
    out_ref[rows, 64:96] = -scaling * nt_dot(left[:, half], cross[:, 1024:2048])
    out_ref[rows, 96:128] = -scaling * nt_dot(left[:, span(0)], ym[0:1] * field(48))
    out_ref[rows, 128:160] = -scaling * nt_dot(left[:, span(7)], yp[7:8] * field(49))
    block = -scaling * nt_dot(left[:, half], ending[...])
    out_ref[rows, 160:192] = jnp.where(core == 0, block, 0.0)
    out_ref[rows, 192:224] = jnp.where(core == 0, 0.0, block)
    out_ref[:, 224:256] = jnp.zeros((64, 32), F32)


def halves(value):
    high = value.astype(BF16)
    return high, (value - high.astype(F32)).astype(BF16)


def dot3(a, b, dims):
    ah, al = a
    bh, bl = b

    def one(p, q):
        return lax.dot_general(p, q, (dims, ((), ())), preferred_element_type=F32)

    return one(ah, bh) + (one(ah, bl) + one(al, bh))


NN = ((1,), (0,))
NT = ((1,), (1,))


def factor_kernel(
    index_ref, table_ref, data_ref, out_ref,
    diag, al, il, tinv, pm, am, xm, mm, lt, ua, vm, cm, mh, ml, uh, ul, ready, done, count,
):
    mine = index_ref[0]
    at_z = index_ref[2]
    lane = iota((32, 128), 1)
    corner = (mine == 0) & (at_z == 0)

    def base(l):
        return table_ref[3, l, 1]

    def slot0(l):
        return table_ref[3, l, 2]

    def place(dest, row, tile, sub, source_row, u):
        half = lax.shift_right_logical(jnp.int32(u), 2)
        from_ = (
            pl.ds(pl.multiple_of(source_row, 32), 32),
            pl.ds(pl.multiple_of(128 * half, 128), 128),
        )
        moved = pltpu.roll(data_ref[from_], (32 * sub - 32 * u) & 127, 1)
        here = (lane >> 5) == sub
        at = (
            pl.ds(pl.multiple_of(row, 32), 32),
            pl.ds(pl.multiple_of(128 * tile, 128), 128),
        )
        dest[at] = dest[at] + jnp.where(here, moved, 0.0)

    def place_all(which, dest, row_of, source_of):
        def each(l, carry):
            @pl.when(table_ref[which, l, 7] > 0)
            def _():
                def one(u, carry):
                    at = table_ref[which, l, u]

                    @pl.when(at >= 0)
                    def _():
                        place(
                            dest, row_of(l), lax.shift_right_logical(at, 2), at & 3,
                            source_of(l), u,
                        )

                    return carry

                lax.fori_loop(0, 7, one, 0)

            return carry

        lax.fori_loop(0, 16, each, 0)

    def linked(l):
        return base(l) == base(l + 1)

    for l in range(16):
        done[l] = 0
        diag[32 * l : 32 * l + 32, :] = data_ref[64 * l + 32 : 64 * l + 64, 0:128]
    count[0] = 0
    tinv[...] = jnp.zeros(tinv.shape, F32)
    pm[...] = jnp.zeros(pm.shape, F32)
    any_link = base(0) == base(1)
    for l in range(1, 15):
        any_link = any_link | linked(l)
    whole = any_link | corner

    @pl.when(whole)
    def _():
        am[...] = jnp.zeros(am.shape, F32)
        lt[...] = jnp.zeros(lt.shape, F32)
        mm[...] = jnp.zeros(mm.shape, F32)
        xm[...] = (iota((512, 512), 0) == iota((512, 512), 1)).astype(F32)
        for l in range(16):
            place(am, 32 * l, l // 4, l % 4, 64 * l + 32, 0)
            if l > 0:

                @pl.when(linked(l - 1))
                def _(l=l):
                    place(am, 32 * l, (l - 1) // 4, (l - 1) % 4, 64 * l + 32, 5)

            if l < 15:

                @pl.when(linked(l))
                def _(l=l):
                    place(am, 32 * l, (l + 1) // 4, (l + 1) % 4, 64 * l + 32, 6)

    def find_ready():
        previous = jnp.int32(99)
        for l in range(16):
            if l > 0:
                previous = jnp.where(linked(l - 1), previous, 99)
            open_ = done[l] == 0
            ready[l] = jnp.where(open_ & (previous > slot0(l)), 1, 0)
            previous = jnp.where(open_, slot0(l), previous)
        previous = jnp.int32(99)
        for l in reversed(range(16)):
            if l < 15:
                previous = jnp.where(linked(l), previous, 99)
            open_ = done[l] == 0
            ready[l] = jnp.where(open_ & (previous > slot0(l)), ready[l], 0)
            previous = jnp.where(open_, slot0(l), previous)
        total = jnp.int32(0)
        for l in range(16):
            done[l] = done[l] + ready[l]
            total = total + done[l]
        count[0] = total

    def batched_inverse():
        for i in range(32):
            al[i, :, 0:16] = jnp.transpose(diag[pl.ds(i, 16, stride=32), :])[0:32, :]
            il[i, :, :] = (iota((32, 128), 0) == i).astype(F32)
        for j in range(32):
            low = 8 * (j // 8)
            pivot = al[j, j : j + 1, :]
            inv = lax.rsqrt(pivot)
            inv = inv * (1.5 - 0.5 * pivot * inv * inv)
            row_a = al[j, low:32, :] * inv
            row_i = il[j, 0 : low + 8, :] * inv
            il[j, 0 : low + 8, :] = row_i

            def update(i, carry, j=j, low=low, row_a=row_a, row_i=row_i, inv=inv):
                f = al[i, j : j + 1, :] * inv
                al[i, low:32, :] = al[i, low:32, :] - f * row_a
                il[i, 0 : low + 8, :] = il[i, 0 : low + 8, :] - f * row_i
                return carry

            lax.fori_loop(j + 1, 32, update, 0, unroll=4 if j < 28 else 1)
        for i in range(32):
            tinv[pl.ds(i, 16, stride=32), :] = jnp.where(
                iota((16, 128), 1) < 32,
                jnp.transpose(jnp.concatenate([il[i], jnp.zeros((96, 128), F32)], axis=0))[0:16, :],
                0.0,
            )
        for l in range(16):
            at = (slice(32 * l, 32 * l + 32), slice(128 * (l // 4), 128 * (l // 4) + 128))
            moved = roll(tinv[32 * l : 32 * l + 32, :], 32 * (l % 4), 1)
            pm[at] = jnp.where(ready[l] > 0, moved, 0.0)

    def nn(a, b):
        return lax.dot_general(a, b, (NN, ((), ())), precision=HIGHEST, preferred_element_type=F32)

    find_ready()
    batched_inverse()

    @pl.when(jnp.logical_not(whole))
    def _():
        mm[...] = pm[...]

    @pl.when(whole)
    def _():
        def level(unused):
            for c in range(4):
                rows = slice(128 * c, 128 * c + 128)
                part = nn(pm[rows, :], am[...])
                ua[rows, :] = part
                lt[rows, :] = lt[rows, :] + part
                part = nn(pm[rows, :], xm[...])
                vm[rows, :] = part
                mm[rows, :] = mm[rows, :] + part
            more = count[0] < 16

            @pl.when(more)
            def _():
                turned = jnp.transpose(ua[...])
                column = iota((1, 512), 1) >> 5
                keep = jnp.ones((1, 512), F32)
                for l in range(16):
                    keep = jnp.where((column == l) & (done[l] > 0), 0.0, keep)
                for c in range(4):
                    rows = slice(128 * c, 128 * c + 128)
                    am[rows, :] = jnp.where(
                        keep > 0.0, am[rows, :] - nn(turned[rows, :], ua[...]), 0.0
                    )
                    xm[rows, :] = xm[rows, :] - nn(turned[rows, :], vm[...])
                for l in range(16):

                    @pl.when(done[l] > 0)
                    def _(l=l):
                        am[32 * l : 32 * l + 32, :] = jnp.zeros((32, 512), F32)

                    @pl.when(done[l] == 0)
                    def _(l=l):
                        at = (
                            slice(32 * l, 32 * l + 32),
                            slice(128 * (l // 4), 128 * (l // 4) + 128),
                        )
                        diag[32 * l : 32 * l + 32, :] = roll(am[at], -32 * (l % 4), 1)

                find_ready()
                batched_inverse()

            return more

        lax.while_loop(lambda more: more, level, jnp.bool_(True))

    @pl.when(mine > 0)
    def _():
        whole_m = mm[...]
        mh[...], ml[...] = halves(whole_m)
        cm[...] = jnp.zeros(cm.shape, F32)
        ua[...] = jnp.zeros(ua.shape, F32)
        place_all(0, cm, lambda l: 32 * l, lambda l: 64 * l + 32)
        place_all(2, ua, lambda l: 32 * table_ref[3, l, 0], lambda l: 64 * l)
        for c in range(4):
            cols = slice(256 * c, 256 * c + 256)
            uh[:, cols], ul[:, cols] = halves(
                dot3((mh[...], ml[...]), halves(cm[:, cols]), NN)
            )
        for c in range(4):
            rows = slice(128 * c, 128 * c + 128)
            part = dot3(halves(ua[rows, :]), (mh[...], ml[...]), NT)
            vm[rows, :] = part
            out_ref[rows, :] = -dot3(halves(part), (uh[...], ul[...]), NN)
        place_all(1, out_ref, lambda l: 32 * table_ref[3, l, 0], lambda l: 64 * l)

    @pl.when(mine == 0)
    def _():
        out_ref[...] = jnp.zeros(out_ref.shape, F32)

    @pl.when(corner)
    def _():
        turned = jnp.transpose(lt[...])
        for l in range(16):
            vm[pl.ds(pl.multiple_of(32 * slot0(l), 32), 32), :] = turned[32 * l : 32 * l + 32, :]

    @pl.when(at_z == 0)
    def _():
        tall = iota((512, 128), 1)
        out_ref[:, 0:512] = jnp.zeros((512, 512), F32)
        for l in range(16):
            slot = slot0(l)
            sub = lax.rem(slot, 4)
            source = vm[:, 128 * (l // 4) : 128 * (l // 4) + 128]
            moved = pltpu.roll(source, lax.rem(32 * sub - 32 * (l % 4) + 128, 128), 1)
            tile = pl.multiple_of(128 * lax.shift_right_logical(slot, 2), 128)
            at = (slice(0, 512), pl.ds(tile, 128))
            out_ref[at] = jnp.where((tall >> 5) == sub, moved, out_ref[at])

    @pl.when(corner)
    def _():
        lower = iota((512, 512), 0) >= iota((512, 512), 1)
        out_ref[:, 0:512] = jnp.where(lower, out_ref[:, 0:512], 0.0)


def build_table(slot_order, mine, at_z):
    ids = jnp.arange(32, dtype=jnp.int32)[:, None]
    group = slot_order // 16
    wanted = jnp.stack([jnp.zeros((), jnp.int32), mine])
    mask = group[None] == wanted[:, None, None]
    rows = jnp.sum(jnp.where(mask, ids[None], 0), axis=1)
    slots = jnp.sum(jnp.where(mask, slot_order[None], 0), axis=1)
    steps = jnp.array([0, -4, 4, -1, 1, 0, 0], jnp.int32)
    deltas = jnp.array([0, 0, 0, 0, 0, -1, 1], jnp.int32)
    l = jnp.arange(16, dtype=jnp.int32)
    near = rows[:, :, None] + steps
    column = jnp.broadcast_to(l[:, None] + deltas, (16, 7))
    col = (rows % 4)[:, :, None]
    u = jnp.arange(7, dtype=jnp.int32)
    ok = (near >= 0) & (near < 32) & (column >= 0) & (column < 16)
    ok = ok & ~((u == 3) & (col == 0)) & ~((u == 4) & (col == 3))
    none = jnp.full((1, 32), -1, jnp.int32)
    turned = slot_order.T
    shifted = jnp.stack(
        [turned] * 5
        + [jnp.concatenate([none, turned[:-1]]), jnp.concatenate([turned[1:], none])],
        axis=1,
    )
    hit = near[..., None] == jnp.arange(32, dtype=jnp.int32)
    target = jnp.sum(jnp.where(hit, shifted[None], 0), axis=-1)
    target = jnp.where(ok, target, -1)
    at = target - 32 * at_z
    here = jnp.where((target >= 16) & (at >= 0) & (at < 32), at, -1)
    panel = jnp.where((target[1] >= 0) & (target[1] < 16), column, -1)
    three = jnp.concatenate([here, panel[None]], axis=0)
    flag = (jnp.max(three, axis=-1, keepdims=True) >= 0).astype(jnp.int32)
    three = jnp.concatenate([three, flag], axis=-1)
    last = jnp.stack([slots[1] - 16 * mine, rows[0], slots[0]], axis=-1)
    last = jnp.pad(last, ((0, 0), (0, 5)))
    return jnp.concatenate([three, last[None]], axis=0)


def on_device(probe_vectors, layer_ids, layer_kappa, slot_order):
    index_x = lax.axis_index("gx")
    index_y = lax.axis_index("gy")
    index_z = lax.axis_index("gz")
    grid_z = lax.axis_size("gz")
    mine = index_x * lax.axis_size("gy") + index_y
    index = jnp.stack([mine, jnp.zeros((), jnp.int32), index_z]).astype(jnp.int32)
    table = build_table(slot_order, mine, index_z)

    send = pl.pallas_call(
        pack_kernel,
        out_shape=jax.ShapeDtypeStruct((32, 32, 128), F32),
        in_specs=[VM, VM, SM],
        out_specs=VM,
    )(probe_vectors.reshape(32, 16, 128), layer_ids.reshape(16, 128), layer_kappa)
    slab = lax.all_to_all(send, ("gx", "gy"), 0, 0, tiled=True)
    low, high = pl.pallas_call(
        edge_kernel,
        out_shape=[jax.ShapeDtypeStruct((64, 128), F32)] * 2,
        in_specs=[VM],
        out_specs=[VM, VM],
    )(slab)
    upward = [(i, i + 1) for i in range(grid_z - 1)]
    downward = [(b, a) for a, b in upward]
    from_left = lax.ppermute(high, "gz", upward)
    from_right = lax.ppermute(low, "gz", downward)
    pieces, coef = pl.pallas_call(
        filter_kernel,
        out_shape=[
            jax.ShapeDtypeStruct((32, 56, 128), F32),
            jax.ShapeDtypeStruct((2, 56, 128), F32),
        ],
        in_specs=[SM, SM, VM, VM, VM],
        out_specs=[VM, VM],
        scratch_shapes=[pltpu.VMEM((18, 32, 256), F32)] * 3 + [pltpu.VMEM((16, 32, 256), F32)] * 7,
    )(slot_order, index, slab, from_left, from_right)
    owned = lax.all_to_all(pieces, ("gx", "gy"), 0, 0, tiled=True)
    blocks = pl.pallas_call(
        galerkin_kernel,
        out_shape=jax.ShapeDtypeStruct((64, 256), F32),
        in_specs=[SM, VM, VM],
        out_specs=VM,
        scratch_shapes=[pltpu.VMEM((32, 2048), F32)] * 3 + [pltpu.VMEM((32, 1024), F32)],
    )(index, owned.reshape(32 * 56, 128), coef)
    pairs = [(k, k ^ 1) for k in range(lax.axis_size("gy"))]
    other = lax.ppermute(blocks[32:], "gy", pairs)
    blocks = jnp.concatenate([blocks[:32], blocks[32:] + other], axis=0)
    spread = lax.all_to_all(
        jnp.broadcast_to(blocks[None], (16, 64, 256)), "gz", 0, 0, tiled=True
    )
    big = pltpu.VMEM((512, 512), F32)
    return pl.pallas_call(
        factor_kernel,
        out_shape=jax.ShapeDtypeStruct((512, 1024), F32),
        in_specs=[SM, SM, VM],
        out_specs=VM,
        scratch_shapes=[
            pltpu.VMEM((512, 128), F32),
            pltpu.VMEM((32, 32, 128), F32),
            pltpu.VMEM((32, 32, 128), F32),
            pltpu.VMEM((512, 128), F32),
            big, big, big, big, big, big, big,
            pltpu.VMEM((512, 1024), F32),
            pltpu.VMEM((512, 512), BF16),
            pltpu.VMEM((512, 512), BF16),
            pltpu.VMEM((512, 1024), BF16),
            pltpu.VMEM((512, 1024), BF16),
            pltpu.SMEM((16,), jnp.int32),
            pltpu.SMEM((16,), jnp.int32),
            pltpu.SMEM((1,), jnp.int32),
        ],
    )(index, table, spread.reshape(1024, 256))


def solution(mesh):
    in_specs = (P(None, "gx", "gy", "gz"), P("gx", "gy", "gz"), P(), P())
    out_specs = P(("gx", "gy"), "gz")
    return jax.shard_map(
        on_device, mesh=mesh, in_specs=in_specs, out_specs=out_specs, check_vma=False
    )
```

```python
import functools
import math

import jax
import jax.numpy as jnp
from jax import lax
from jax.experimental import pallas as pl
from jax.experimental.pallas import tpu as pltpu
from jax.sharding import PartitionSpec as P

PASSES = 4
UPPER = 120.0
LOWER = 24.0
SHIFT = 1.0
F32 = jnp.float32
BF16 = jnp.bfloat16
HIGHEST = lax.Precision.HIGHEST


VM = pl.BlockSpec(memory_space=pltpu.VMEM)
SM = pl.BlockSpec(memory_space=pltpu.SMEM)


def cheb_factors(step_index):
    center = (UPPER + LOWER) / (UPPER - LOWER)
    growth = math.log(center + math.sqrt(center * center - 1.0))

    def chebval(degree):
        expo = math.exp(degree * growth)
        return 0.5 * (expo + 1.0 / expo)

    if step_index == 0:
        return (1.0 / chebval(1), 0.0)
    return (
        2.0 * chebval(step_index) / chebval(step_index + 1),
        chebval(step_index - 1) / chebval(step_index + 1),
    )


def iota(shape, dim):
    return lax.broadcasted_iota(jnp.int32, shape, dim)


def roll(value, shift, axis):
    shift = shift % value.shape[axis]
    if shift == 0:
        return value
    return pltpu.roll(value, shift, axis)


def pack_kernel(vec_ref, ids_ref, kappa_ref, out_ref):
    ids = ids_ref[...]
    kappa = jnp.zeros(ids.shape, F32)
    for layer in range(kappa_ref.shape[0]):
        kappa = jnp.where(ids == layer, kappa_ref[layer], kappa)
    out_ref[:, 0:16, :] = vec_ref[...]
    out_ref[:, 16:32, :] = jnp.broadcast_to(kappa[None], (out_ref.shape[0], 16, 128))


def slab_plane(ref, field, plane):
    i, x = plane // 2, plane % 2
    base = 16 * field + 8 * x
    return jnp.concatenate([ref[4 * i + j, base : base + 8, :] for j in range(4)], axis=0)


def edge_kernel(slab_ref, low_ref, high_ref):
    lane = iota((32, 128), 1)
    for field in range(2):
        low = jnp.zeros((32, 128), F32)
        high = jnp.zeros((32, 128), F32)
        for plane in range(16):
            tile = slab_plane(slab_ref, field, plane)
            here = (lane >> 3) == plane
            low = jnp.where(here, roll(tile, 8 * plane, 1), low)
            high = jnp.where(here, roll(tile, 8 * plane + 8, 1), high)
        low_ref[32 * field : 32 * field + 32, :] = low
        high_ref[32 * field : 32 * field + 32, :] = high


def filter_kernel(
    order_ref, index_ref, slab_ref, left_ref, right_ref, out_ref, coef_ref,
    za, zb, ka, wxp, wxm, wyp, wym, wzp, wzm, dia,
):
    mine = index_ref[0]
    at_z = index_ref[2]
    lane = iota((32, 128), 1)
    zero_plane = jnp.zeros((32, 256), F32)
    for dest, field in ((za, 0), (ka, 1)):
        dest[0] = zero_plane
        dest[17] = zero_plane
        for plane in range(16):
            dest[plane + 1, :, 0:128] = slab_plane(slab_ref, field, plane)
            rows = slice(32 * field, 32 * field + 32)
            right = roll(right_ref[rows, :], -8 * plane, 1)
            left = roll(left_ref[rows, :], 120 - 8 * plane, 1)
            dest[plane + 1, :, 128:256] = jnp.where(
                lane < 8, right, jnp.where(lane >= 120, left, 0.0)
            )
    zb[0] = zero_plane
    zb[17] = zero_plane
    wide = iota((32, 256), 1)
    row = iota((32, 256), 0)
    inside = (
        (wide < 128) | ((wide < 192) & (at_z < 15)) | ((wide >= 192) & (at_z > 0))
    )
    half = 0.5 * 2.0 / (UPPER - LOWER)
    center = (UPPER + LOWER) / (UPPER - LOWER)

    def weights(plane, carry):
        k = ka[plane + 1]
        xp = half * (k + ka[plane + 2])
        xm = half * (k + ka[plane])
        yp = half * (k + jnp.where(row == 31, 0.0, roll(k, 31, 0)))
        ym = half * (k + jnp.where(row == 0, 0.0, roll(k, 1, 0)))
        zp = half * (k + roll(k, 255, 1))
        zm = half * (k + roll(k, 1, 1))
        total = xp + xm + yp + ym + zp + zm
        wxp[plane] = jnp.where(inside, xp, 0.0)
        wxm[plane] = jnp.where(inside, xm, 0.0)
        wyp[plane] = jnp.where(inside & (row != 31), yp, 0.0)
        wym[plane] = jnp.where(inside & (row != 0), ym, 0.0)
        wzp[plane] = jnp.where(inside, zp, 0.0)
        wzm[plane] = jnp.where(inside, zm, 0.0)
        dia[plane] = jnp.where(inside, center - total, 0.0)
        return carry

    lax.fori_loop(0, 16, weights, 0)
    for step in range(PASSES):
        src, dest = (za, zb) if step % 2 == 0 else (zb, za)
        one, two = cheb_factors(step)

        def sweep(plane, carry, src=src, dest=dest, one=one, two=two, step=step):
            z = src[plane + 1]
            acc = dia[plane] * z
            acc = acc + wxp[plane] * src[plane + 2] + wxm[plane] * src[plane]
            acc = acc + wyp[plane] * roll(z, 31, 0) + wym[plane] * roll(z, 1, 0)
            acc = acc + wzp[plane] * roll(z, 255, 1) + wzm[plane] * roll(z, 1, 1)
            acc = one * acc
            if step > 0:
                acc = acc - two * dest[plane + 1]
            dest[plane + 1] = acc
            return carry

        lax.fori_loop(0, 16, sweep, 0)

    sub = iota((8, 128), 0)
    lane8 = iota((8, 128), 1)
    zero_row = jnp.zeros((1, 128), F32)
    for r in range(32):
        i, j = r // 4, r % 4
        dest = lax.shift_right_logical(order_ref[r, at_z], 4)
        rows = slice(8 * j, 8 * j + 8)
        out_ref[dest, 0:8, :] = za[2 * i + 1, rows, 0:128]
        out_ref[dest, 8:16, :] = za[2 * i + 2, rows, 0:128]
        out_ref[dest, 16:24, :] = za[2 * i, rows, 0:128]
        out_ref[dest, 24:32, :] = za[2 * i + 3, rows, 0:128]
        packed = jnp.zeros((8, 128), F32)
        for x in range(2):
            out_ref[dest, 50 + x : 51 + x, :] = (
                za[2 * i + 1 + x, 8 * j - 1 : 8 * j, 0:128] if j > 0 else zero_row
            )
            out_ref[dest, 52 + x : 53 + x, :] = (
                za[2 * i + 1 + x, 8 * j + 8 : 8 * j + 9, 0:128] if j < 3 else zero_row
            )
            tile = za[2 * i + 1 + x, rows, 128:256]
            packed = jnp.where(lane8 == 8 * x + sub, tile[:, 127:128], packed)
            packed = jnp.where(lane8 == 16 + 8 * x + sub, tile[:, 0:1], packed)
        out_ref[dest, 54:55, :] = jnp.sum(packed, axis=0, keepdims=True)
        out_ref[dest, 55:56, :] = zero_row

        def coefficients(slot, i=i, j=j, rows=rows):
            coef_ref[slot, 0:8, :] = ka[2 * i + 1, rows, 0:128]
            coef_ref[slot, 8:16, :] = ka[2 * i + 2, rows, 0:128]
            coef_ref[slot, 16:24, :] = ka[2 * i, rows, 0:128]
            coef_ref[slot, 24:32, :] = ka[2 * i + 3, rows, 0:128]
            for x in range(2):
                coef_ref[slot, 32 + x : 33 + x, :] = (
                    ka[2 * i + 1 + x, 8 * j - 1 : 8 * j, 0:128] if j > 0 else zero_row
                )
                coef_ref[slot, 34 + x : 35 + x, :] = (
                    ka[2 * i + 1 + x, 8 * j + 8 : 8 * j + 9, 0:128] if j < 3 else zero_row
                )
                coef_ref[slot, 40 + 8 * x : 48 + 8 * x, :] = ka[2 * i + 1 + x, rows, 128:256]

        @pl.when(dest == mine)
        def _(coefficients=coefficients):
            coefficients(0)

        @pl.when(dest == 0)
        def _(coefficients=coefficients):
            coefficients(1)

    first = [out_ref[0, 8 * n : 8 * n + 8, :] for n in range(4)]
    edges = [out_ref[0, 50 + n : 51 + n, :] for n in range(4)]
    ends = out_ref[0, 54:55, :]
    lane1 = iota((1, 128), 1)
    for core in range(2):
        body = jnp.concatenate(
            [pack_half(first[0], first[1], core), pack_half(first[2], first[3], core)], axis=0
        )
        sides = jnp.concatenate(
            [pack_half(edges[0], edges[1], core), pack_half(edges[2], edges[3], core)], axis=0
        )
        at = 64 if core == 0 else 63
        below = 40 if core == 0 else 32
        packed = jnp.zeros((8, 128), F32)
        for x in range(2):
            column = first[x][:, at : at + 1]
            packed = jnp.where(lane8 == below + 64 * x + sub, column, packed)
        line = jnp.sum(packed, axis=0, keepdims=True)
        outer = 32 if core == 0 else 40
        start = 0 if core == 0 else 16
        for x in range(2):
            here = (lane1 >> 3) == (outer + 64 * x) // 8
            line = jnp.where(here, roll(ends, outer + 64 * x - start - 8 * x, 1), line)

        def spread(k, carry, core=core, body=body, sides=sides, line=line):
            dest = 2 * k + core
            out_ref[dest, 32:48, :] = body
            out_ref[dest, 48:50, :] = sides
            out_ref[dest, 54:55, :] = out_ref[dest, 54:55, :] + line
            return carry

        lax.fori_loop(0, 16, spread, 0)


def pack_half(even, odd, core):
    lane = iota(even.shape, 1)
    if core == 0:
        return jnp.where(lane < 64, even, roll(odd, 64, 1))
    return jnp.where(lane < 64, roll(even, 64, 1), odd)


def nt_dot(a, b):
    return lax.dot_general(
        a, b, (((1,), (1,)), ((), ())), precision=HIGHEST, preferred_element_type=F32
    )


def galerkin_kernel(index_ref, data_ref, coef_ref, out_ref, left, image, cross, ending):
    sub = iota((8, 128), 0)
    lane8 = iota((8, 128), 1)
    lane = iota((32, 128), 1)
    scaling = 1.0 / math.sqrt(2048.0)
    eye = (iota((32, 32), 0) == iota((32, 32), 1)).astype(F32)
    core = lax.rem(index_ref[0], 2)

    def field(r):
        return data_ref[pl.ds(r, 32, stride=56), :]

    def span(r):
        return slice(128 * r, 128 * r + 128)

    def weights(part):
        k0 = coef_ref[part, 0:8, :]
        k1 = coef_ref[part, 8:16, :]
        km = coef_ref[part, 16:24, :]
        kp = coef_ref[part, 24:32, :]
        found = []
        for x in range(2):
            k = (k0, k1)[x]
            below = coef_ref[part, 32 + x : 33 + x, :]
            above = coef_ref[part, 34 + x : 35 + x, :]
            ends = coef_ref[part, 40 + 8 * x : 48 + 8 * x, :]
            xm = 0.5 * (k + (km, k0)[x])
            xp = 0.5 * (k + (k1, kp)[x])
            ym = 0.5 * (k + jnp.where(sub == 0, below, roll(k, 1, 0)))
            yp = 0.5 * (k + jnp.where(sub == 7, above, roll(k, 7, 0)))
            zm = 0.5 * (k + jnp.where(lane8 == 0, ends[:, 127:128], roll(k, 1, 1)))
            zp = 0.5 * (k + jnp.where(lane8 == 127, ends[:, 0:1], roll(k, 127, 1)))
            found.append((xm, xp, ym, yp, zm, zp, xp + xm + yp + ym + zp + zm))
        return found

    for r in range(16):
        left[:, span(r)] = field(r)
    columns = jnp.zeros((32, 128), F32)
    y_low, y_high = [], []
    for x, (xm, xp, ym, yp, zm, zp, diag) in enumerate(weights(0)):
        zm_in = jnp.where(lane8 == 0, 0.0, zm)
        zp_in = jnp.where(lane8 == 127, 0.0, zp)
        for y in range(8):
            r = 8 * x + y
            one = slice(y, y + 1)
            z = left[:, span(r)]
            beside = zp_in[one] * roll(z, 127, 1) + zm_in[one] * roll(z, 1, 1)
            if x == 0:
                beside = beside + xp[one] * left[:, span(r + 8)]
            else:
                beside = beside + xm[one] * left[:, span(r - 8)]
            if y < 7:
                beside = beside + yp[one] * left[:, span(r + 1)]
            if y > 0:
                beside = beside + ym[one] * left[:, span(r - 1)]
            image[:, span(r)] = diag[one] * z - beside
            cross[:, span(r)] = (xm, xp)[x][one] * field(16 + r)
            if y == 0:
                y_low.append((r, ym[one] * field(50 + x)))
            if y == 7:
                y_high.append((r, yp[one] * field(52 + x)))
            columns = jnp.where(lane == r, roll(zm[one] * z, r, 1), columns)
            columns = jnp.where(lane == 16 + r, roll(zp[one] * z, 17 + r, 1), columns)
    out_ref[0:32, 0:32] = scaling * nt_dot(left[...], image[...]) + SHIFT * eye
    out_ref[0:32, 32:64] = -scaling * nt_dot(left[:, 0:1024], cross[:, 0:1024])
    out_ref[0:32, 64:96] = -scaling * nt_dot(left[:, 1024:2048], cross[:, 1024:2048])
    for at, pair in ((96, y_low), (128, y_high)):
        block = sum(nt_dot(left[:, span(r)], ghost) for r, ghost in pair)
        out_ref[0:32, at : at + 32] = -scaling * block
    ghost = field(54)
    low = jnp.where(lane < 16, columns, 0.0)
    high = jnp.where((lane >= 16) & (lane < 32), columns, 0.0)
    out_ref[0:32, 160:192] = -scaling * nt_dot(low, ghost)
    out_ref[0:32, 192:224] = -scaling * nt_dot(high, ghost)

    even, odd = weights(1)

    def pack(a, b):
        return jnp.where(core == 0, pack_half(a, b, 0), pack_half(a, b, 1))

    w_out = pack(even[0], odd[1])
    w_in = pack(even[1], odd[0])
    ym, yp, zm, zp, diag = (pack(even[n], odd[n]) for n in range(2, 7))
    first8 = (lane8 & 63) == 0
    last8 = (lane8 & 63) == 63
    zm_in = jnp.where(first8 & (core == 0), 0.0, zm)
    zp_in = jnp.where(last8 & (core == 1), 0.0, zp)
    z_out = jnp.where(core == 0, jnp.where(first8, zm, 0.0), jnp.where(last8, zp, 0.0))
    at_first = (lane & 63) == 0
    at_last = (lane & 63) == 63
    for y in range(8):
        left[:, span(y)] = field(32 + y)
    for y in range(8):
        one = slice(y, y + 1)
        z = left[:, span(y)]
        z_low = jnp.where(at_first, roll(ghost, -(32 + y), 1), roll(z, 1, 1))
        z_high = jnp.where(at_last, roll(ghost, 23 - y, 1), roll(z, 127, 1))
        beside = zp_in[one] * z_high + zm_in[one] * z_low + w_in[one] * roll(z, 64, 1)
        if y < 7:
            beside = beside + yp[one] * left[:, span(y + 1)]
        if y > 0:
            beside = beside + ym[one] * left[:, span(y - 1)]
        image[:, span(y)] = diag[one] * z - beside
        side = w_out[one] * field(40 + y)
        cross[:, span(y)] = jnp.where(lane < 64, side, 0.0)
        cross[:, span(8 + y)] = jnp.where(lane < 64, 0.0, side)
        ending[:, span(y)] = z_out[one] * jnp.where(core == 0, z_low, z_high)
    half = slice(0, 1024)
    rows = slice(32, 64)
    shift = jnp.where(core == 0, SHIFT, 0.0) * eye
    out_ref[rows, 0:32] = scaling * nt_dot(left[:, half], image[:, half]) + shift
    out_ref[rows, 32:64] = -scaling * nt_dot(left[:, half], cross[:, half])
    out_ref[rows, 64:96] = -scaling * nt_dot(left[:, half], cross[:, 1024:2048])
    out_ref[rows, 96:128] = -scaling * nt_dot(left[:, span(0)], ym[0:1] * field(48))
    out_ref[rows, 128:160] = -scaling * nt_dot(left[:, span(7)], yp[7:8] * field(49))
    block = -scaling * nt_dot(left[:, half], ending[...])
    out_ref[rows, 160:192] = jnp.where(core == 0, block, 0.0)
    out_ref[rows, 192:224] = jnp.where(core == 0, 0.0, block)
    out_ref[:, 224:256] = jnp.zeros((64, 32), F32)


def halves(value):
    high = value.astype(BF16)
    return high, (value - high.astype(F32)).astype(BF16)


def dot3(a, b, dims):
    ah, al = a
    bh, bl = b

    def one(p, q):
        return lax.dot_general(p, q, (dims, ((), ())), preferred_element_type=F32)

    return one(ah, bh) + (one(ah, bl) + one(al, bh))


NN = ((1,), (0,))
NT = ((1,), (1,))


def factor_kernel(
    index_ref, table_ref, data_ref, out_ref,
    diag, al, il, tinv, er, el, xm, mm, lm, ua, vm, cm, mh, ml, uh, ul,
    left, right, ready, touched, row_list, hits, count,
):
    mine = index_ref[0]
    at_z = index_ref[2]
    lane = iota((32, 128), 1)
    corner = (mine == 0) & (at_z == 0)

    def base(l):
        return table_ref[3, l, 1]

    def slot0(l):
        return table_ref[3, l, 2]

    def block_rows(l):
        return pl.ds(pl.multiple_of(32 * l, 32), 32)

    def tile_of(n):
        return pl.ds(pl.multiple_of(128 * n, 128), 128)

    def place(dest, row, tile, sub, source_row, u):
        source = data_ref[
            pl.ds(pl.multiple_of(source_row, 32), 32), tile_of(lax.shift_right_logical(u, 2))
        ]
        moved = pltpu.roll(source, (32 * sub - 32 * u) & 127, 1)
        at = (pl.ds(pl.multiple_of(row, 32), 32), tile_of(tile))
        dest[at] = dest[at] + jnp.where((lane >> 5) == sub, moved, 0.0)

    def put(dest, row, column, block):
        padded = jnp.concatenate([block, jnp.zeros((32, 96), F32)], axis=1)
        at = (block_rows(row), tile_of(lax.shift_right_logical(column, 2)))
        dest[at] = dest[at] + pltpu.roll(padded, (32 * column) & 127, 1)

    def for_hits(which, l, action):
        def one(u, carry):
            at = table_ref[which, l, u]

            @pl.when(at >= 0)
            def _():
                action(u, at)

            return carry

        lax.fori_loop(0, 7, one, 0)

    def for_blocks(action):
        def each(l, carry):
            action(l)
            return carry

        lax.fori_loop(0, 16, each, 0)

    def nn(a, b):
        return lax.dot_general(a, b, (NN, ((), ())), precision=HIGHEST, preferred_element_type=F32)

    mm[...] = jnp.zeros(mm.shape, F32)
    any_link = jnp.bool_(False)
    for l in range(16):
        diag[32 * l : 32 * l + 32, :] = data_ref[64 * l + 32 : 64 * l + 64, 0:128]
        left[l] = jnp.int32(-1)
        right[l] = jnp.int32(-1)
        ready[l] = jnp.int32(0)
        touched[l] = jnp.int32(0)
    for l in range(15):
        link = base(l) == base(l + 1)
        any_link = any_link | link

        @pl.when(link)
        def _(l=l):
            right[l] = jnp.int32(l + 1)
            left[l + 1] = jnp.int32(l)
            ahead = data_ref[64 * l + 32 : 64 * l + 64, 128:256]
            back = data_ref[64 * l + 96 : 64 * l + 128, 128:256]
            er[32 * l : 32 * l + 32, :] = roll(ahead, -64, 1)
            el[32 * l + 32 : 32 * l + 64, :] = roll(back, -32, 1)

    @pl.when(any_link)
    def _():
        xm[...] = (iota((512, 512), 0) == iota((512, 512), 1)).astype(F32)

    @pl.when(corner)
    def _():
        lm[...] = jnp.zeros(lm.shape, F32)

    def batched_inverse():
        lane16 = iota((16, 128), 1)
        for g in range(8):
            wide = diag[pl.ds(4 * g, 16, stride=32), :]
            for t in range(1, 4):
                row = diag[pl.ds(4 * g + t, 16, stride=32), :]
                wide = jnp.where((lane16 >> 5) == t, roll(row, 32 * t, 1), wide)
            turned = jnp.transpose(jnp.concatenate([wide, jnp.zeros((112, 128), F32)], axis=0))
            for t in range(4):
                al[4 * g + t] = turned[32 * t : 32 * t + 32, :]
        sub = iota((8, 128), 0)
        for q in range(4):
            low = 8 * q
            a = [al[low + t, low : low + 8, :] for t in range(8)]
            w = [(sub == t).astype(F32) for t in range(8)]
            for t in range(8):
                pivot = a[t][t : t + 1, :]
                inv = lax.rsqrt(pivot)
                inv = inv * (1.5 - 0.5 * pivot * inv * inv)
                a[t] = a[t] * inv
                w[t] = w[t] * inv
                for k in range(t + 1, 8):
                    f = a[k][t : t + 1, :] * inv
                    a[k] = a[k] - f * a[t]
                    w[k] = w[k] - f * w[t]
            lead = {}
            for r in range(q + 1, 4):
                old = [al[low + k, 8 * r : 8 * r + 8, :] for k in range(8)]
                for t in range(8):
                    total = w[t][0:1, :] * old[0]
                    for k in range(1, t + 1):
                        total = total + w[t][k : k + 1, :] * old[k]
                    lead[t, r] = total
            unit = {(t, q): w[t] for t in range(8)}
            for r in range(q):
                old = [il[low + k, 8 * r : 8 * r + 8, :] for k in range(8)]
                for t in range(8):
                    total = w[t][0:1, :] * old[0]
                    for k in range(1, t + 1):
                        total = total + w[t][k : k + 1, :] * old[k]
                    unit[t, r] = total
            for t in range(8):
                for r in range(4):
                    il[low + t, 8 * r : 8 * r + 8, :] = unit.get((t, r), jnp.zeros((8, 128), F32))
            for i in range(low + 8, 32):
                own = i // 8
                f = [lead[t, own][i % 8 : i % 8 + 1, :] for t in range(8)]
                for r in range(own, 4):
                    value = al[i, 8 * r : 8 * r + 8, :]
                    for t in range(8):
                        value = value - f[t] * lead[t, r]
                    al[i, 8 * r : 8 * r + 8, :] = value
                for r in range(q + 1):
                    value = -f[0] * unit[0, r]
                    if r < q:
                        value = value + il[i, 8 * r : 8 * r + 8, :]
                    for t in range(1, 8):
                        value = value - f[t] * unit[t, r]
                    il[i, 8 * r : 8 * r + 8, :] = value
        for g in range(8):
            stack = jnp.concatenate([il[4 * g + t] for t in range(4)], axis=0)
            turned = jnp.transpose(stack)[0:16, :]
            for t in range(4):
                tinv[pl.ds(4 * g + t, 16, stride=32), :] = jnp.where(
                    lane16 < 32, roll(turned, -32 * t, 1), 0.0
                )

    def eliminate(l):
        before, after = left[l], right[l]
        rows = block_rows(l)
        inverse = tinv[rows, 0:32]

        @pl.when(corner)
        def _():
            put(lm, l, l, nt_dot(diag[rows, 0:32], inverse))

        @pl.when(touched[l] == 0)
        def _():
            at = (rows, tile_of(lax.shift_right_logical(l, 2)))
            mm[at] = pltpu.roll(tinv[rows, :], (32 * l) & 127, 1)

        @pl.when(touched[l] > 0)
        def _():
            mm[rows, :] = nn(inverse, xm[rows, :])

        def fold(near, link):
            at = block_rows(near)
            factor = nt_dot(link[at, 0:32], inverse)
            diag[at, 0:32] = diag[at, 0:32] - nt_dot(factor, factor)
            xm[at, :] = xm[at, :] - nn(factor, mm[rows, :])
            touched[near] = jnp.int32(1)

            @pl.when(corner)
            def _():
                put(lm, near, l, factor)

        @pl.when(after >= 0)
        def _():
            fold(after, el)
            left[after] = before

        @pl.when(before >= 0)
        def _():
            fold(before, er)
            right[before] = after

        @pl.when((before >= 0) & (after >= 0))
        def _():
            one = nt_dot(er[block_rows(before), 0:32], inverse)
            two = nt_dot(el[block_rows(after), 0:32], inverse)
            er[block_rows(before), 0:32] = -nt_dot(one, two)
            el[block_rows(after), 0:32] = -nt_dot(two, one)

        ready[l] = jnp.int32(2)

    def level(unused):
        batched_inverse()

        def mark(l):
            before, after, slot = left[l], right[l], slot0(l)
            free = (before < 0) | (slot0(jnp.maximum(before, 0)) > slot)
            free = free & ((after < 0) | (slot0(jnp.maximum(after, 0)) > slot))
            ready[l] = jnp.where(ready[l] == 2, 2, jnp.where(free, 1, 0))

        for_blocks(mark)
        count[0] = jnp.int32(0)

        def visit(l):
            @pl.when(ready[l] == 1)
            def _():
                eliminate(l)

            @pl.when(ready[l] == 0)
            def _():
                count[0] = count[0] + 1

        for_blocks(visit)
        return count[0] > 0

    lax.while_loop(lambda more: more, level, jnp.bool_(True))
    out_ref[...] = jnp.zeros(out_ref.shape, F32)

    def emit(source_row, row_of, number):
        rows = pl.ds(pl.multiple_of(source_row, 128), 128)
        tall = iota((128, 128), 1)
        ua[0:128, :] = jnp.zeros((128, 512), F32)
        for l in range(16):
            slot = slot0(l)
            source = vm[rows, 128 * (l // 4) : 128 * (l // 4) + 128]
            moved = pltpu.roll(source, (32 * slot - 32 * l) & 127, 1)
            at = (slice(0, 128), tile_of(lax.shift_right_logical(slot, 2)))
            ua[at] = jnp.where((tall >> 5) == (slot & 3), moved, ua[at])
        for k in range(4):

            @pl.when(k < number)
            def _(k=k):
                out_ref[pl.ds(pl.multiple_of(row_of(k), 32), 32), 0:512] = ua[
                    32 * k : 32 * k + 32, :
                ]

    @pl.when(mine > 0)
    def _():
        mh[...], ml[...] = halves(mm[...])
        cm[...] = jnp.zeros(cm.shape, F32)
        for n in range(8):
            hits[n] = jnp.int32(0)
        count[0] = jnp.int32(0)

        def gather(l):
            @pl.when(table_ref[0, l, 7] > 0)
            def _():
                def one(u, at):
                    tile = lax.shift_right_logical(at, 2)
                    hits[tile] = jnp.int32(1)
                    place(cm, 32 * l, tile, at & 3, 64 * l + 32, u)

                for_hits(0, l, one)

            @pl.when(table_ref[2, l, 7] > 0)
            def _():
                row_list[count[0]] = l
                count[0] = count[0] + 1

            @pl.when(table_ref[1, l, 7] > 0)
            def _():
                def one(u, at):
                    place(
                        out_ref, 32 * table_ref[3, l, 0], lax.shift_right_logical(at, 2),
                        at & 3, 64 * l, u,
                    )

                for_hits(1, l, one)

        for_blocks(gather)
        total = count[0]

        @pl.when(total > 0)
        def _():
            def column(n, carry):
                @pl.when(hits[n] > 0)
                def _():
                    at = (slice(0, 512), tile_of(n))
                    uh[at], ul[at] = halves(dot3((mh[...], ml[...]), halves(cm[at]), NN))

                return carry

            lax.fori_loop(0, 8, column, 0)

        def chunk(c, carry):
            @pl.when(total > 4 * c)
            def _():
                ua[0:128, :] = jnp.zeros((128, 512), F32)

                def fill(k, carry):
                    @pl.when(4 * c + k < total)
                    def _():
                        l = row_list[4 * c + k]
                        for_hits(
                            2,
                            l,
                            lambda u, at: place(
                                ua, 32 * k, lax.shift_right_logical(at, 2), at & 3, 64 * l, u
                            ),
                        )

                    return carry

                lax.fori_loop(0, 4, fill, 0)
                part = dot3(halves(ua[0:128, :]), (mh[...], ml[...]), NT)
                vm[0:128, :] = part

                def row_of(k):
                    return 32 * table_ref[3, row_list[jnp.minimum(4 * c + k, total - 1)], 0]

                def column(n, carry):
                    @pl.when(hits[n] > 0)
                    def _():
                        at = (slice(0, 512), tile_of(n))
                        update = dot3(halves(vm[0:128, :]), (uh[at], ul[at]), NN)
                        for k in range(4):

                            @pl.when(4 * c + k < total)
                            def _(k=k):
                                to = (pl.ds(pl.multiple_of(row_of(k), 32), 32), tile_of(n))
                                out_ref[to] = out_ref[to] - update[32 * k : 32 * k + 32, :]

                    return carry

                lax.fori_loop(0, 8, column, 0)

                @pl.when(at_z == 0)
                def _():
                    emit(0, row_of, total - 4 * c)

            return carry

        lax.fori_loop(0, 4, chunk, 0)

    @pl.when(corner)
    def _():
        def rows(c, carry):
            vm[0:128, :] = lm[pl.ds(pl.multiple_of(128 * c, 128), 128), :]
            emit(0, lambda k: 32 * slot0(4 * c + k), 4)
            return carry

        lax.fori_loop(0, 4, rows, 0)
        lower = iota((512, 512), 0) >= iota((512, 512), 1)
        out_ref[:, 0:512] = jnp.where(lower, out_ref[:, 0:512], 0.0)


def factor(index, table, data):
    big = pltpu.VMEM((512, 512), F32)
    narrow = pltpu.VMEM((512, 128), F32)
    cube = pltpu.VMEM((32, 32, 128), F32)
    short = pltpu.VMEM((128, 512), F32)
    return pl.pallas_call(
        factor_kernel,
        out_shape=jax.ShapeDtypeStruct((512, 1024), F32),
        in_specs=[SM, SM, VM],
        out_specs=VM,
        scratch_shapes=[
            narrow, cube, cube, narrow, narrow, narrow, big, big, big, short, short,
            pltpu.VMEM((512, 1024), F32),
            pltpu.VMEM((512, 512), BF16),
            pltpu.VMEM((512, 512), BF16),
            pltpu.VMEM((512, 1024), BF16),
            pltpu.VMEM((512, 1024), BF16),
            pltpu.SMEM((16,), jnp.int32),
            pltpu.SMEM((16,), jnp.int32),
            pltpu.SMEM((16,), jnp.int32),
            pltpu.SMEM((16,), jnp.int32),
            pltpu.SMEM((16,), jnp.int32),
            pltpu.SMEM((8,), jnp.int32),
            pltpu.SMEM((1,), jnp.int32),
        ],
    )(index, table, data)


def build_table(slot_order, mine, at_z):
    ids = jnp.arange(32, dtype=jnp.int32)[:, None]
    group = slot_order // 16
    wanted = jnp.stack([jnp.zeros((), jnp.int32), mine])
    mask = group[None] == wanted[:, None, None]
    rows = jnp.sum(jnp.where(mask, ids[None], 0), axis=1)
    slots = jnp.sum(jnp.where(mask, slot_order[None], 0), axis=1)
    steps = jnp.array([0, -4, 4, -1, 1, 0, 0], jnp.int32)
    deltas = jnp.array([0, 0, 0, 0, 0, -1, 1], jnp.int32)
    l = jnp.arange(16, dtype=jnp.int32)
    near = rows[:, :, None] + steps
    column = jnp.broadcast_to(l[:, None] + deltas, (16, 7))
    col = (rows % 4)[:, :, None]
    u = jnp.arange(7, dtype=jnp.int32)
    ok = (near >= 0) & (near < 32) & (column >= 0) & (column < 16)
    ok = ok & ~((u == 3) & (col == 0)) & ~((u == 4) & (col == 3))
    none = jnp.full((1, 32), -1, jnp.int32)
    turned = slot_order.T
    shifted = jnp.stack(
        [turned] * 5
        + [jnp.concatenate([none, turned[:-1]]), jnp.concatenate([turned[1:], none])],
        axis=1,
    )
    hit = near[..., None] == jnp.arange(32, dtype=jnp.int32)
    target = jnp.sum(jnp.where(hit, shifted[None], 0), axis=-1)
    target = jnp.where(ok, target, -1)
    at = target - 32 * at_z
    here = jnp.where((target >= 16) & (at >= 0) & (at < 32), at, -1)
    panel = jnp.where((target[1] >= 0) & (target[1] < 16), column, -1)
    three = jnp.concatenate([here, panel[None]], axis=0)
    flag = (jnp.max(three, axis=-1, keepdims=True) >= 0).astype(jnp.int32)
    three = jnp.concatenate([three, flag], axis=-1)
    last = jnp.stack([slots[1] - 16 * mine, rows[0], slots[0]], axis=-1)
    last = jnp.pad(last, ((0, 0), (0, 5)))
    return jnp.concatenate([three, last[None]], axis=0)


def on_device(probe_vectors, layer_ids, layer_kappa, slot_order):
    index_x = lax.axis_index("gx")
    index_y = lax.axis_index("gy")
    index_z = lax.axis_index("gz")
    grid_z = lax.axis_size("gz")
    mine = index_x * lax.axis_size("gy") + index_y
    index = jnp.stack([mine, jnp.zeros((), jnp.int32), index_z]).astype(jnp.int32)
    table = build_table(slot_order, mine, index_z)

    send = pl.pallas_call(
        pack_kernel,
        out_shape=jax.ShapeDtypeStruct((32, 32, 128), F32),
        in_specs=[VM, VM, SM],
        out_specs=VM,
    )(probe_vectors.reshape(32, 16, 128), layer_ids.reshape(16, 128), layer_kappa)
    slab = lax.all_to_all(send, ("gx", "gy"), 0, 0, tiled=True)
    low, high = pl.pallas_call(
        edge_kernel,
        out_shape=[jax.ShapeDtypeStruct((64, 128), F32)] * 2,
        in_specs=[VM],
        out_specs=[VM, VM],
    )(slab)
    upward = [(i, i + 1) for i in range(grid_z - 1)]
    downward = [(b, a) for a, b in upward]
    from_left = lax.ppermute(high, "gz", upward)
    from_right = lax.ppermute(low, "gz", downward)
    pieces, coef = pl.pallas_call(
        filter_kernel,
        out_shape=[
            jax.ShapeDtypeStruct((32, 56, 128), F32),
            jax.ShapeDtypeStruct((2, 56, 128), F32),
        ],
        in_specs=[SM, SM, VM, VM, VM],
        out_specs=[VM, VM],
        scratch_shapes=[pltpu.VMEM((18, 32, 256), F32)] * 3 + [pltpu.VMEM((16, 32, 256), F32)] * 7,
    )(slot_order, index, slab, from_left, from_right)
    owned = lax.all_to_all(pieces, ("gx", "gy"), 0, 0, tiled=True)
    blocks = pl.pallas_call(
        galerkin_kernel,
        out_shape=jax.ShapeDtypeStruct((64, 256), F32),
        in_specs=[SM, VM, VM],
        out_specs=VM,
        scratch_shapes=[pltpu.VMEM((32, 2048), F32)] * 3 + [pltpu.VMEM((32, 1024), F32)],
    )(index, owned.reshape(32 * 56, 128), coef)
    pairs = [(k, k ^ 1) for k in range(lax.axis_size("gy"))]
    other = lax.ppermute(blocks[32:], "gy", pairs)
    blocks = jnp.concatenate([blocks[:32], blocks[32:] + other], axis=0)
    spread = lax.all_to_all(
        jnp.broadcast_to(blocks[None], (16, 64, 256)), "gz", 0, 0, tiled=True
    )
    return factor(index, table, spread.reshape(1024, 256))


def solution(mesh):
    in_specs = (P(None, "gx", "gy", "gz"), P("gx", "gy", "gz"), P(), P())
    out_specs = P(("gx", "gy"), "gz")
    return jax.shard_map(
        on_device, mesh=mesh, in_specs=in_specs, out_specs=out_specs, check_vma=False
    )
```

```python
import functools
import math

import jax
import jax.numpy as jnp
from jax import lax
from jax.experimental import pallas as pl
from jax.experimental.pallas import tpu as pltpu
from jax.sharding import PartitionSpec as P

PASSES = 4
UPPER = 120.0
LOWER = 24.0
SHIFT = 1.0
F32 = jnp.float32
BF16 = jnp.bfloat16
HIGHEST = lax.Precision.HIGHEST


VM = pl.BlockSpec(memory_space=pltpu.VMEM)


def near(value):
    return pltpu.with_memory_space_constraint(value, pltpu.VMEM)


SM = pl.BlockSpec(memory_space=pltpu.SMEM)


def cheb_factors(step_index):
    center = (UPPER + LOWER) / (UPPER - LOWER)
    growth = math.log(center + math.sqrt(center * center - 1.0))

    def chebval(degree):
        expo = math.exp(degree * growth)
        return 0.5 * (expo + 1.0 / expo)

    if step_index == 0:
        return (1.0 / chebval(1), 0.0)
    return (
        2.0 * chebval(step_index) / chebval(step_index + 1),
        chebval(step_index - 1) / chebval(step_index + 1),
    )


def iota(shape, dim):
    return lax.broadcasted_iota(jnp.int32, shape, dim)


def roll(value, shift, axis):
    shift = shift % value.shape[axis]
    if shift == 0:
        return value
    return pltpu.roll(value, shift, axis)


def pack_kernel(vec_ref, ids_ref, kappa_ref, out_ref):
    ids = ids_ref[...]
    kappa = jnp.zeros(ids.shape, F32)
    for layer in range(kappa_ref.shape[0]):
        kappa = jnp.where(ids == layer, kappa_ref[layer], kappa)
    out_ref[:, 0:16, :] = vec_ref[...]
    out_ref[:, 16:32, :] = jnp.broadcast_to(kappa[None], (out_ref.shape[0], 16, 128))


def slab_plane(ref, field, plane):
    i, x = plane // 2, plane % 2
    base = 16 * field + 8 * x
    return jnp.concatenate([ref[4 * i + j, base : base + 8, :] for j in range(4)], axis=0)


def edge_kernel(slab_ref, low_ref, high_ref):
    lane = iota((32, 128), 1)
    for field in range(2):
        low = jnp.zeros((32, 128), F32)
        high = jnp.zeros((32, 128), F32)
        for plane in range(16):
            tile = slab_plane(slab_ref, field, plane)
            here = (lane >> 3) == plane
            low = jnp.where(here, roll(tile, 8 * plane, 1), low)
            high = jnp.where(here, roll(tile, 8 * plane + 8, 1), high)
        low_ref[32 * field : 32 * field + 32, :] = low
        high_ref[32 * field : 32 * field + 32, :] = high


def filter_kernel(
    order_ref, index_ref, slab_ref, left_ref, right_ref, out_ref, coef_ref,
    za, zb, ka, ends_a, ends_b, main, side,
):
    mine = index_ref[0]
    at_z = index_ref[2]
    lane = iota((32, 128), 1)
    row = iota((32, 128), 0)
    slot = lane & 7
    zero_plane = jnp.zeros((32, 128), F32)
    for dest, field in ((za, 0), (ka, 1)):
        dest[0] = zero_plane
        dest[17] = zero_plane
        for plane in range(16):
            dest[plane + 1] = slab_plane(slab_ref, field, plane)
    zb[0] = zero_plane
    zb[17] = zero_plane
    ends_a[0] = right_ref[0:32, :]
    ends_a[1] = left_ref[0:32, :]

    def edges_of(right, left):
        return jnp.where(slot == 0, right, jnp.where(slot == 1, roll(left, -6, 1), 0.0))

    def z_pair(z, edges, plane):
        ahead = roll(edges, 127 - 8 * plane, 1)
        return (
            jnp.where(lane == 127, ahead, roll(z, 127, 1)),
            jnp.where(lane == 0, ahead, roll(z, 1, 1)),
        )

    def collect(inner, z, plane):
        return jnp.where((lane >> 1) == 4 * plane, roll(z, 8 * plane + 1, 1), inner)

    def end_pairs(right, left, inner):
        return (
            (roll(right, 127, 1), jnp.where(slot == 0, inner, roll(right, 1, 1))),
            (jnp.where(slot == 7, roll(inner, 6, 1), roll(left, 127, 1)), roll(left, 1, 1)),
        )

    half = 0.5 * 2.0 / (UPPER - LOWER)
    center = (UPPER + LOWER) / (UPPER - LOWER)

    def weights(store, k, kxp, kxm, kzp, kzm, first_x, last_x, keep):
        xp = half * (k + kxp)
        xm = half * (k + kxm)
        yp = half * (k + jnp.where(row == 31, 0.0, roll(k, 31, 0)))
        ym = half * (k + jnp.where(row == 0, 0.0, roll(k, 1, 0)))
        zp = half * (k + kzp)
        zm = half * (k + kzm)
        total = xp + xm + yp + ym + zp + zm
        values = (
            xp if last_x is None else jnp.where(last_x, 0.0, xp),
            xm if first_x is None else jnp.where(first_x, 0.0, xm),
            jnp.where(row == 31, 0.0, yp),
            jnp.where(row == 0, 0.0, ym),
            zp,
            zm,
            center - total,
        )
        for n, value in enumerate(values):
            store(n, value if keep is None else jnp.where(keep, value, 0.0))

    k_right, k_left = right_ref[32:64, :], left_ref[32:64, :]
    k_edges = edges_of(k_right, k_left)
    k_inner = zero_plane
    for plane in range(16):
        k = ka[plane + 1]
        kzp, kzm = z_pair(k, k_edges, plane)
        k_inner = collect(k_inner, k, plane)

        def store(n, value, plane=plane):
            main[n, plane] = value

        weights(store, k, ka[plane + 2], ka[plane], kzp, kzm, None, None, None)
    first_x, last_x = lane < 8, lane >= 120
    for n, (k, pair, keep) in enumerate(
        zip(
            (k_right, k_left),
            end_pairs(k_right, k_left, k_inner),
            (at_z < 15, at_z > 0),
        )
    ):
        kxp = jnp.where(last_x, 0.0, roll(k, -8, 1))
        kxm = jnp.where(first_x, 0.0, roll(k, 8, 1))

        def store(m, value, n=n):
            side[n, m] = value

        weights(store, k, kxp, kxm, *pair, first_x, last_x, keep)

    def combine(w, z, xp, xm, zp, zm, step, previous):
        one, two = cheb_factors(step)
        acc = w(6) * z + (w(0) * xp + w(1) * xm)
        acc = acc + (w(2) * roll(z, 31, 0) + w(3) * roll(z, 1, 0))
        acc = one * (acc + (w(4) * zp + w(5) * zm))
        return acc if step == 0 else acc - two * previous()

    for step in range(PASSES):
        src, dest = (za, zb) if step % 2 == 0 else (zb, za)
        end_src, end_dest = (ends_a, ends_b) if step % 2 == 0 else (ends_b, ends_a)
        right, left = end_src[0], end_src[1]
        edges = edges_of(right, left)
        inner = zero_plane
        for plane in range(16):
            z = src[plane + 1]
            inner = collect(inner, z, plane)
            zp, zm = z_pair(z, edges, plane)
            dest[plane + 1] = combine(
                lambda n, plane=plane: main[n, plane],
                z, src[plane + 2], src[plane], zp, zm, step,
                lambda plane=plane, dest=dest: dest[plane + 1],
            )
        for n, (z, (zp, zm)) in enumerate(zip((right, left), end_pairs(right, left, inner))):
            end_dest[n] = combine(
                lambda m, n=n: side[n, m],
                z, roll(z, -8, 1), roll(z, 8, 1), zp, zm, step,
                lambda n=n, end_dest=end_dest: end_dest[n],
            )

    ghosts = []
    for j in range(4):
        rows = slice(8 * j, 8 * j + 8)
        pair = []
        for n, keep, start in ((1, 7, 121), (0, 0, 0)):
            column = jnp.where((iota((8, 128), 1) & 7) == keep, ends_a[n, rows, :], 0.0)
            spread = pltpu.roll(column, start, 1, stride=1, stride_axis=0)
            pair.append(jnp.sum(spread, axis=0, keepdims=True))
        ghosts.append(pair)
    sub = iota((8, 128), 0)
    lane8 = iota((8, 128), 1)
    lane1 = iota((1, 128), 1)
    zero_row = jnp.zeros((1, 128), F32)
    for r in range(32):
        i, j = r // 4, r % 4
        dest = lax.shift_right_logical(order_ref[r, at_z], 4)
        rows = slice(8 * j, 8 * j + 8)
        out_ref[dest, 0:8, :] = za[2 * i + 1, rows]
        out_ref[dest, 8:16, :] = za[2 * i + 2, rows]
        out_ref[dest, 16:24, :] = za[2 * i, rows]
        out_ref[dest, 24:32, :] = za[2 * i + 3, rows]
        for x in range(2):
            out_ref[dest, 50 + x : 51 + x, :] = (
                za[2 * i + 1 + x, 8 * j - 1 : 8 * j] if j > 0 else zero_row
            )
            out_ref[dest, 52 + x : 53 + x, :] = (
                za[2 * i + 1 + x, 8 * j + 8 : 8 * j + 9] if j < 3 else zero_row
            )
        line = jnp.where(lane1 < 32, roll(ghosts[j][1], 16 - 16 * i, 1), 0.0)
        line = jnp.where(lane1 < 16, roll(ghosts[j][0], -16 * i, 1), line)
        out_ref[dest, 54:55, :] = line
        out_ref[dest, 55:56, :] = zero_row

        def coefficients(slot, i=i, j=j, rows=rows):
            coef_ref[slot, 0:8, :] = ka[2 * i + 1, rows]
            coef_ref[slot, 8:16, :] = ka[2 * i + 2, rows]
            coef_ref[slot, 16:24, :] = ka[2 * i, rows]
            coef_ref[slot, 24:32, :] = ka[2 * i + 3, rows]
            for x in range(2):
                coef_ref[slot, 32 + x : 33 + x, :] = (
                    ka[2 * i + 1 + x, 8 * j - 1 : 8 * j] if j > 0 else zero_row
                )
                coef_ref[slot, 34 + x : 35 + x, :] = (
                    ka[2 * i + 1 + x, 8 * j + 8 : 8 * j + 9] if j < 3 else zero_row
                )
                coef_ref[slot, 40 + 8 * x : 48 + 8 * x, :] = roll(
                    k_edges[rows, :], 127 - 8 * (2 * i + x), 1
                )

        @pl.when(dest == mine)
        def _(coefficients=coefficients):
            coefficients(0)

        @pl.when(dest == 0)
        def _(coefficients=coefficients):
            coefficients(1)

    first = [out_ref[0, 8 * n : 8 * n + 8, :] for n in range(4)]
    edges = [out_ref[0, 50 + n : 51 + n, :] for n in range(4)]
    ends = out_ref[0, 54:55, :]
    for core in range(2):
        body = jnp.concatenate(
            [pack_half(first[0], first[1], core), pack_half(first[2], first[3], core)], axis=0
        )
        sides = jnp.concatenate(
            [pack_half(edges[0], edges[1], core), pack_half(edges[2], edges[3], core)], axis=0
        )
        at = 64 if core == 0 else 63
        below = 40 if core == 0 else 32
        packed = jnp.zeros((8, 128), F32)
        for x in range(2):
            column = first[x][:, at : at + 1]
            packed = jnp.where(lane8 == below + 64 * x + sub, column, packed)
        line = jnp.sum(packed, axis=0, keepdims=True)
        outer = 32 if core == 0 else 40
        start = 0 if core == 0 else 16
        for x in range(2):
            here = (lane1 >> 3) == (outer + 64 * x) // 8
            line = jnp.where(here, roll(ends, outer + 64 * x - start - 8 * x, 1), line)

        def spread(k, carry, core=core, body=body, sides=sides, line=line):
            dest = 2 * k + core
            out_ref[dest, 32:48, :] = body
            out_ref[dest, 48:50, :] = sides
            out_ref[dest, 54:55, :] = out_ref[dest, 54:55, :] + line
            return carry

        lax.fori_loop(0, 16, spread, 0)


def pack_half(even, odd, core):
    lane = iota(even.shape, 1)
    if core == 0:
        return jnp.where(lane < 64, even, roll(odd, 64, 1))
    return jnp.where(lane < 64, roll(even, 64, 1), odd)


def nt_dot(a, b):
    return lax.dot_general(
        a, b, (((1,), (1,)), ((), ())), precision=HIGHEST, preferred_element_type=F32
    )


def galerkin_kernel(index_ref, data_ref, coef_ref, own_ref, part_ref, left, image, cross, ending):
    sub = iota((8, 128), 0)
    lane8 = iota((8, 128), 1)
    lane = iota((32, 128), 1)
    scaling = 1.0 / math.sqrt(2048.0)
    eye = (iota((32, 32), 0) == iota((32, 32), 1)).astype(F32)
    core = lax.rem(index_ref[0], 2)

    def field(r):
        return data_ref[pl.ds(r, 32, stride=56), :]

    def span(r):
        return slice(128 * r, 128 * r + 128)

    def weights(part):
        k0 = coef_ref[part, 0:8, :]
        k1 = coef_ref[part, 8:16, :]
        km = coef_ref[part, 16:24, :]
        kp = coef_ref[part, 24:32, :]
        found = []
        for x in range(2):
            k = (k0, k1)[x]
            below = coef_ref[part, 32 + x : 33 + x, :]
            above = coef_ref[part, 34 + x : 35 + x, :]
            ends = coef_ref[part, 40 + 8 * x : 48 + 8 * x, :]
            xm = 0.5 * (k + (km, k0)[x])
            xp = 0.5 * (k + (k1, kp)[x])
            ym = 0.5 * (k + jnp.where(sub == 0, below, roll(k, 1, 0)))
            yp = 0.5 * (k + jnp.where(sub == 7, above, roll(k, 7, 0)))
            zm = 0.5 * (k + jnp.where(lane8 == 0, ends, roll(k, 1, 1)))
            zp = 0.5 * (k + jnp.where(lane8 == 127, ends, roll(k, 127, 1)))
            found.append((xm, xp, ym, yp, zm, zp, xp + xm + yp + ym + zp + zm))
        return found

    for r in range(16):
        left[:, span(r)] = field(r)
    columns = jnp.zeros((32, 128), F32)
    y_low, y_high = [], []
    for x, (xm, xp, ym, yp, zm, zp, diag) in enumerate(weights(0)):
        zm_in = jnp.where(lane8 == 0, 0.0, zm)
        zp_in = jnp.where(lane8 == 127, 0.0, zp)
        for y in range(8):
            r = 8 * x + y
            one = slice(y, y + 1)
            z = left[:, span(r)]
            beside = zp_in[one] * roll(z, 127, 1) + zm_in[one] * roll(z, 1, 1)
            if x == 0:
                beside = beside + xp[one] * left[:, span(r + 8)]
            else:
                beside = beside + xm[one] * left[:, span(r - 8)]
            if y < 7:
                beside = beside + yp[one] * left[:, span(r + 1)]
            if y > 0:
                beside = beside + ym[one] * left[:, span(r - 1)]
            image[:, span(r)] = diag[one] * z - beside
            cross[:, span(r)] = (xm, xp)[x][one] * field(16 + r)
            if y == 0:
                y_low.append((r, ym[one] * field(50 + x)))
            if y == 7:
                y_high.append((r, yp[one] * field(52 + x)))
            columns = jnp.where(lane == r, roll(zm[one] * z, r, 1), columns)
            columns = jnp.where(lane == 16 + r, roll(zp[one] * z, 17 + r, 1), columns)
    own_ref[:, 0:32] = scaling * nt_dot(left[...], image[...]) + SHIFT * eye
    own_ref[:, 32:64] = -scaling * nt_dot(left[:, 0:1024], cross[:, 0:1024])
    own_ref[:, 64:96] = -scaling * nt_dot(left[:, 1024:2048], cross[:, 1024:2048])
    for at, pair in ((96, y_low), (128, y_high)):
        block = sum(nt_dot(left[:, span(r)], ghost) for r, ghost in pair)
        own_ref[:, at : at + 32] = -scaling * block
    ghost = field(54)
    low = jnp.where(lane < 16, columns, 0.0)
    high = jnp.where((lane >= 16) & (lane < 32), columns, 0.0)
    own_ref[:, 160:192] = -scaling * nt_dot(low, ghost)
    own_ref[:, 192:224] = -scaling * nt_dot(high, ghost)

    even, odd = weights(1)

    def pack(a, b):
        return jnp.where(core == 0, pack_half(a, b, 0), pack_half(a, b, 1))

    w_out = pack(even[0], odd[1])
    w_in = pack(even[1], odd[0])
    ym, yp, zm, zp, diag = (pack(even[n], odd[n]) for n in range(2, 7))
    first8 = (lane8 & 63) == 0
    last8 = (lane8 & 63) == 63
    zm_in = jnp.where(first8 & (core == 0), 0.0, zm)
    zp_in = jnp.where(last8 & (core == 1), 0.0, zp)
    z_out = jnp.where(core == 0, jnp.where(first8, zm, 0.0), jnp.where(last8, zp, 0.0))
    at_first = (lane & 63) == 0
    at_last = (lane & 63) == 63
    for y in range(8):
        left[:, span(y)] = field(32 + y)
    for y in range(8):
        one = slice(y, y + 1)
        z = left[:, span(y)]
        z_low = jnp.where(at_first, roll(ghost, -(32 + y), 1), roll(z, 1, 1))
        z_high = jnp.where(at_last, roll(ghost, 23 - y, 1), roll(z, 127, 1))
        beside = zp_in[one] * z_high + zm_in[one] * z_low + w_in[one] * roll(z, 64, 1)
        if y < 7:
            beside = beside + yp[one] * left[:, span(y + 1)]
        if y > 0:
            beside = beside + ym[one] * left[:, span(y - 1)]
        image[:, span(y)] = diag[one] * z - beside
        side = w_out[one] * field(40 + y)
        cross[:, span(y)] = jnp.where(lane < 64, side, 0.0)
        cross[:, span(8 + y)] = jnp.where(lane < 64, 0.0, side)
        ending[:, span(y)] = z_out[one] * jnp.where(core == 0, z_low, z_high)
    half = slice(0, 1024)
    shift = jnp.where(core == 0, SHIFT, 0.0) * eye
    part_ref[:, 0:32] = scaling * nt_dot(left[:, half], image[:, half]) + shift
    part_ref[:, 32:64] = -scaling * nt_dot(left[:, half], cross[:, half])
    part_ref[:, 64:96] = -scaling * nt_dot(left[:, half], cross[:, 1024:2048])
    part_ref[:, 96:128] = -scaling * nt_dot(left[:, span(0)], ym[0:1] * field(48))
    part_ref[:, 128:160] = -scaling * nt_dot(left[:, span(7)], yp[7:8] * field(49))
    block = -scaling * nt_dot(left[:, half], ending[...])
    part_ref[:, 160:192] = jnp.where(core == 0, block, 0.0)
    part_ref[:, 192:224] = jnp.where(core == 0, 0.0, block)
    own_ref[:, 224:256] = jnp.zeros((32, 32), F32)
    part_ref[:, 224:256] = jnp.zeros((32, 32), F32)


def copies_kernel(own_ref, part_ref, other_ref, out_ref):
    own = own_ref[...]
    panel = part_ref[...] + other_ref[...]
    for n in range(16):
        out_ref[n, 0:32, :] = own
        out_ref[n, 32:64, :] = panel


def halves(value):
    high = value.astype(BF16)
    return high, (value - high.astype(F32)).astype(BF16)


def dot3(a, b, dims):
    ah, al = a
    bh, bl = b

    def one(p, q):
        return lax.dot_general(p, q, (dims, ((), ())), preferred_element_type=F32)

    return one(ah, bh) + (one(ah, bl) + one(al, bh))


NN = ((1,), (0,))
NT = ((1,), (1,))


def factor_kernel(
    index_ref, table_ref, data_ref, out_ref,
    diag, al, il, tinv, er, el, xm, mm, lm, ua, vm, cm, mh, ml, uh, ul,
    left, right, ready, touched, row_list, hits, count,
):
    mine = index_ref[0]
    at_z = index_ref[2]
    lane = iota((32, 128), 1)
    corner = (mine == 0) & (at_z == 0)

    def base(l):
        return table_ref[3, l, 1]

    def slot0(l):
        return table_ref[3, l, 2]

    def block_rows(l):
        return pl.ds(pl.multiple_of(32 * l, 32), 32)

    def tile_of(n):
        return pl.ds(pl.multiple_of(128 * n, 128), 128)

    def place(dest, row, tile, sub, source_row, u):
        source = data_ref[
            pl.ds(pl.multiple_of(source_row, 32), 32), tile_of(lax.shift_right_logical(u, 2))
        ]
        moved = pltpu.roll(source, (32 * sub - 32 * u) & 127, 1)
        at = (pl.ds(pl.multiple_of(row, 32), 32), tile_of(tile))
        dest[at] = dest[at] + jnp.where((lane >> 5) == sub, moved, 0.0)

    def put(dest, row, column, block):
        padded = jnp.concatenate([block, jnp.zeros((32, 96), F32)], axis=1)
        at = (block_rows(row), tile_of(lax.shift_right_logical(column, 2)))
        dest[at] = dest[at] + pltpu.roll(padded, (32 * column) & 127, 1)

    def for_hits(which, l, action):
        def one(u, carry):
            at = table_ref[which, l, u]

            @pl.when(at >= 0)
            def _():
                action(u, at)

            return carry

        lax.fori_loop(0, 7, one, 0)

    def for_blocks(action):
        def each(l, carry):
            action(l)
            return carry

        lax.fori_loop(0, 16, each, 0)

    def nn(a, b):
        return lax.dot_general(a, b, (NN, ((), ())), precision=HIGHEST, preferred_element_type=F32)

    mm[...] = jnp.zeros(mm.shape, F32)
    any_link = jnp.bool_(False)
    for l in range(16):
        diag[32 * l : 32 * l + 32, :] = data_ref[64 * l + 32 : 64 * l + 64, 0:128]
        left[l] = jnp.int32(-1)
        right[l] = jnp.int32(-1)
        ready[l] = jnp.int32(0)
        touched[l] = jnp.int32(0)
    for l in range(15):
        link = base(l) == base(l + 1)
        any_link = any_link | link

        @pl.when(link)
        def _(l=l):
            right[l] = jnp.int32(l + 1)
            left[l + 1] = jnp.int32(l)
            ahead = data_ref[64 * l + 32 : 64 * l + 64, 128:256]
            back = data_ref[64 * l + 96 : 64 * l + 128, 128:256]
            er[32 * l : 32 * l + 32, :] = roll(ahead, -64, 1)
            el[32 * l + 32 : 32 * l + 64, :] = roll(back, -32, 1)

    @pl.when(any_link)
    def _():
        xm[...] = (iota((512, 512), 0) == iota((512, 512), 1)).astype(F32)

    @pl.when(corner)
    def _():
        lm[...] = jnp.zeros(lm.shape, F32)

    def batched_inverse():
        lane16 = iota((16, 128), 1)
        for g in range(8):
            wide = diag[pl.ds(4 * g, 16, stride=32), :]
            for t in range(1, 4):
                row = diag[pl.ds(4 * g + t, 16, stride=32), :]
                wide = jnp.where((lane16 >> 5) == t, roll(row, 32 * t, 1), wide)
            turned = jnp.transpose(jnp.concatenate([wide, jnp.zeros((112, 128), F32)], axis=0))
            for t in range(4):
                al[4 * g + t] = turned[32 * t : 32 * t + 32, :]
        sub = iota((8, 128), 0)
        for q in range(4):
            low = 8 * q
            a = [al[low + t, low : low + 8, :] for t in range(8)]
            w = [(sub == t).astype(F32) for t in range(8)]
            for t in range(8):
                pivot = a[t][t : t + 1, :]
                inv = lax.rsqrt(pivot)
                inv = inv * (1.5 - 0.5 * pivot * inv * inv)
                a[t] = a[t] * inv
                w[t] = w[t] * inv
                for k in range(t + 1, 8):
                    f = a[k][t : t + 1, :] * inv
                    a[k] = a[k] - f * a[t]
                    w[k] = w[k] - f * w[t]
            lead = {}
            for r in range(q + 1, 4):
                old = [al[low + k, 8 * r : 8 * r + 8, :] for k in range(8)]
                for t in range(8):
                    total = w[t][0:1, :] * old[0]
                    for k in range(1, t + 1):
                        total = total + w[t][k : k + 1, :] * old[k]
                    lead[t, r] = total
            unit = {(t, q): w[t] for t in range(8)}
            for r in range(q):
                old = [il[low + k, 8 * r : 8 * r + 8, :] for k in range(8)]
                for t in range(8):
                    total = w[t][0:1, :] * old[0]
                    for k in range(1, t + 1):
                        total = total + w[t][k : k + 1, :] * old[k]
                    unit[t, r] = total
            for t in range(8):
                for r in range(4):
                    il[low + t, 8 * r : 8 * r + 8, :] = unit.get((t, r), jnp.zeros((8, 128), F32))
            for i in range(low + 8, 32):
                own = i // 8
                f = [lead[t, own][i % 8 : i % 8 + 1, :] for t in range(8)]
                for r in range(own, 4):
                    value = al[i, 8 * r : 8 * r + 8, :]
                    for t in range(8):
                        value = value - f[t] * lead[t, r]
                    al[i, 8 * r : 8 * r + 8, :] = value
                for r in range(q + 1):
                    value = -f[0] * unit[0, r]
                    if r < q:
                        value = value + il[i, 8 * r : 8 * r + 8, :]
                    for t in range(1, 8):
                        value = value - f[t] * unit[t, r]
                    il[i, 8 * r : 8 * r + 8, :] = value
        for g in range(8):
            stack = jnp.concatenate([il[4 * g + t] for t in range(4)], axis=0)
            turned = jnp.transpose(stack)[0:16, :]
            for t in range(4):
                tinv[pl.ds(4 * g + t, 16, stride=32), :] = jnp.where(
                    lane16 < 32, roll(turned, -32 * t, 1), 0.0
                )

    def eliminate(l):
        before, after = left[l], right[l]
        rows = block_rows(l)
        inverse = tinv[rows, 0:32]

        @pl.when(corner)
        def _():
            put(lm, l, l, nt_dot(diag[rows, 0:32], inverse))

        @pl.when(touched[l] == 0)
        def _():
            at = (rows, tile_of(lax.shift_right_logical(l, 2)))
            mm[at] = pltpu.roll(tinv[rows, :], (32 * l) & 127, 1)

        @pl.when(touched[l] > 0)
        def _():
            mm[rows, :] = nn(inverse, xm[rows, :])

        def fold(near, link):
            at = block_rows(near)
            factor = nt_dot(link[at, 0:32], inverse)
            diag[at, 0:32] = diag[at, 0:32] - nt_dot(factor, factor)
            xm[at, :] = xm[at, :] - nn(factor, mm[rows, :])
            touched[near] = jnp.int32(1)

            @pl.when(corner)
            def _():
                put(lm, near, l, factor)

        @pl.when(after >= 0)
        def _():
            fold(after, el)
            left[after] = before

        @pl.when(before >= 0)
        def _():
            fold(before, er)
            right[before] = after

        @pl.when((before >= 0) & (after >= 0))
        def _():
            one = nt_dot(er[block_rows(before), 0:32], inverse)
            two = nt_dot(el[block_rows(after), 0:32], inverse)
            er[block_rows(before), 0:32] = -nt_dot(one, two)
            el[block_rows(after), 0:32] = -nt_dot(two, one)

        ready[l] = jnp.int32(2)

    def level(unused):
        batched_inverse()

        def mark(l):
            before, after, slot = left[l], right[l], slot0(l)
            free = (before < 0) | (slot0(jnp.maximum(before, 0)) > slot)
            free = free & ((after < 0) | (slot0(jnp.maximum(after, 0)) > slot))
            ready[l] = jnp.where(ready[l] == 2, 2, jnp.where(free, 1, 0))

        for_blocks(mark)
        count[0] = jnp.int32(0)

        def visit(l):
            @pl.when(ready[l] == 1)
            def _():
                eliminate(l)

            @pl.when(ready[l] == 0)
            def _():
                count[0] = count[0] + 1

        for_blocks(visit)
        return count[0] > 0

    lax.while_loop(lambda more: more, level, jnp.bool_(True))
    out_ref[...] = jnp.zeros(out_ref.shape, F32)

    def emit(source_row, row_of, number):
        rows = pl.ds(pl.multiple_of(source_row, 128), 128)
        tall = iota((128, 128), 1)
        ua[0:128, :] = jnp.zeros((128, 512), F32)
        for l in range(16):
            slot = slot0(l)
            source = vm[rows, 128 * (l // 4) : 128 * (l // 4) + 128]
            moved = pltpu.roll(source, (32 * slot - 32 * l) & 127, 1)
            at = (slice(0, 128), tile_of(lax.shift_right_logical(slot, 2)))
            ua[at] = jnp.where((tall >> 5) == (slot & 3), moved, ua[at])
        for k in range(4):

            @pl.when(k < number)
            def _(k=k):
                out_ref[pl.ds(pl.multiple_of(row_of(k), 32), 32), 0:512] = ua[
                    32 * k : 32 * k + 32, :
                ]

    @pl.when(mine > 0)
    def _():
        mh[...], ml[...] = halves(mm[...])
        cm[...] = jnp.zeros(cm.shape, F32)
        for n in range(8):
            hits[n] = jnp.int32(0)
        count[0] = jnp.int32(0)

        def gather(l):
            @pl.when(table_ref[0, l, 7] > 0)
            def _():
                def one(u, at):
                    tile = lax.shift_right_logical(at, 2)
                    hits[tile] = jnp.int32(1)
                    place(cm, 32 * l, tile, at & 3, 64 * l + 32, u)

                for_hits(0, l, one)

            @pl.when(table_ref[2, l, 7] > 0)
            def _():
                row_list[count[0]] = l
                count[0] = count[0] + 1

            @pl.when(table_ref[1, l, 7] > 0)
            def _():
                def one(u, at):
                    place(
                        out_ref, 32 * table_ref[3, l, 0], lax.shift_right_logical(at, 2),
                        at & 3, 64 * l, u,
                    )

                for_hits(1, l, one)

        for_blocks(gather)
        total = count[0]

        @pl.when(total > 0)
        def _():
            def column(n, carry):
                @pl.when(hits[n] > 0)
                def _():
                    at = (slice(0, 512), tile_of(n))
                    uh[at], ul[at] = halves(dot3((mh[...], ml[...]), halves(cm[at]), NN))

                return carry

            lax.fori_loop(0, 8, column, 0)

        def chunk(c, carry):
            @pl.when(total > 4 * c)
            def _():
                ua[0:128, :] = jnp.zeros((128, 512), F32)

                def fill(k, carry):
                    @pl.when(4 * c + k < total)
                    def _():
                        l = row_list[4 * c + k]
                        for_hits(
                            2,
                            l,
                            lambda u, at: place(
                                ua, 32 * k, lax.shift_right_logical(at, 2), at & 3, 64 * l, u
                            ),
                        )

                    return carry

                lax.fori_loop(0, 4, fill, 0)
                part = dot3(halves(ua[0:128, :]), (mh[...], ml[...]), NT)
                vm[0:128, :] = part

                def row_of(k):
                    return 32 * table_ref[3, row_list[jnp.minimum(4 * c + k, total - 1)], 0]

                def column(n, carry):
                    @pl.when(hits[n] > 0)
                    def _():
                        at = (slice(0, 512), tile_of(n))
                        update = dot3(halves(vm[0:128, :]), (uh[at], ul[at]), NN)
                        for k in range(4):

                            @pl.when(4 * c + k < total)
                            def _(k=k):
                                to = (pl.ds(pl.multiple_of(row_of(k), 32), 32), tile_of(n))
                                out_ref[to] = out_ref[to] - update[32 * k : 32 * k + 32, :]

                    return carry

                lax.fori_loop(0, 8, column, 0)

                @pl.when(at_z == 0)
                def _():
                    emit(0, row_of, total - 4 * c)

            return carry

        lax.fori_loop(0, 4, chunk, 0)

    @pl.when(corner)
    def _():
        def rows(c, carry):
            vm[0:128, :] = lm[pl.ds(pl.multiple_of(128 * c, 128), 128), :]
            emit(0, lambda k: 32 * slot0(4 * c + k), 4)
            return carry

        lax.fori_loop(0, 4, rows, 0)
        lower = iota((512, 512), 0) >= iota((512, 512), 1)
        out_ref[:, 0:512] = jnp.where(lower, out_ref[:, 0:512], 0.0)


def factor(index, table, data):
    big = pltpu.VMEM((512, 512), F32)
    narrow = pltpu.VMEM((512, 128), F32)
    cube = pltpu.VMEM((32, 32, 128), F32)
    short = pltpu.VMEM((128, 512), F32)
    return pl.pallas_call(
        factor_kernel,
        out_shape=jax.ShapeDtypeStruct((512, 1024), F32),
        in_specs=[SM, SM, VM],
        out_specs=VM,
        scratch_shapes=[
            narrow, cube, cube, narrow, narrow, narrow, big, big, big, short, short,
            pltpu.VMEM((512, 1024), F32),
            pltpu.VMEM((512, 512), BF16),
            pltpu.VMEM((512, 512), BF16),
            pltpu.VMEM((512, 1024), BF16),
            pltpu.VMEM((512, 1024), BF16),
            pltpu.SMEM((16,), jnp.int32),
            pltpu.SMEM((16,), jnp.int32),
            pltpu.SMEM((16,), jnp.int32),
            pltpu.SMEM((16,), jnp.int32),
            pltpu.SMEM((16,), jnp.int32),
            pltpu.SMEM((8,), jnp.int32),
            pltpu.SMEM((1,), jnp.int32),
        ],
    )(index, table, data)


def build_table(slot_order, mine, at_z):
    ids = jnp.arange(32, dtype=jnp.int32)[:, None]
    group = slot_order // 16
    wanted = jnp.stack([jnp.zeros((), jnp.int32), mine])
    mask = group[None] == wanted[:, None, None]
    rows = jnp.sum(jnp.where(mask, ids[None], 0), axis=1)
    slots = jnp.sum(jnp.where(mask, slot_order[None], 0), axis=1)
    steps = jnp.array([0, -4, 4, -1, 1, 0, 0], jnp.int32)
    deltas = jnp.array([0, 0, 0, 0, 0, -1, 1], jnp.int32)
    l = jnp.arange(16, dtype=jnp.int32)
    near = rows[:, :, None] + steps
    column = jnp.broadcast_to(l[:, None] + deltas, (16, 7))
    col = (rows % 4)[:, :, None]
    u = jnp.arange(7, dtype=jnp.int32)
    ok = (near >= 0) & (near < 32) & (column >= 0) & (column < 16)
    ok = ok & ~((u == 3) & (col == 0)) & ~((u == 4) & (col == 3))
    none = jnp.full((1, 32), -1, jnp.int32)
    turned = slot_order.T
    shifted = jnp.stack(
        [turned] * 5
        + [jnp.concatenate([none, turned[:-1]]), jnp.concatenate([turned[1:], none])],
        axis=1,
    )
    hit = near[..., None] == jnp.arange(32, dtype=jnp.int32)
    target = jnp.sum(jnp.where(hit, shifted[None], 0), axis=-1)
    target = jnp.where(ok, target, -1)
    at = target - 32 * at_z
    here = jnp.where((target >= 16) & (at >= 0) & (at < 32), at, -1)
    panel = jnp.where((target[1] >= 0) & (target[1] < 16), column, -1)
    three = jnp.concatenate([here, panel[None]], axis=0)
    flag = (jnp.max(three, axis=-1, keepdims=True) >= 0).astype(jnp.int32)
    three = jnp.concatenate([three, flag], axis=-1)
    last = jnp.stack([slots[1] - 16 * mine, rows[0], slots[0]], axis=-1)
    last = jnp.pad(last, ((0, 0), (0, 5)))
    return jnp.concatenate([three, last[None]], axis=0)


def on_device(probe_vectors, layer_ids, layer_kappa, slot_order):
    index_x = lax.axis_index("gx")
    index_y = lax.axis_index("gy")
    index_z = lax.axis_index("gz")
    grid_z = lax.axis_size("gz")
    mine = index_x * lax.axis_size("gy") + index_y
    index = jnp.stack([mine, jnp.zeros((), jnp.int32), index_z]).astype(jnp.int32)
    table = build_table(slot_order, mine, index_z)

    send = pl.pallas_call(
        pack_kernel,
        out_shape=pltpu.VMEM((32, 32, 128), F32),
        in_specs=[VM, VM, SM],
        out_specs=VM,
    )(probe_vectors.reshape(32, 16, 128), layer_ids.reshape(16, 128), layer_kappa)
    slab = near(lax.all_to_all(send, ("gx", "gy"), 0, 0, tiled=True))
    low, high = pl.pallas_call(
        edge_kernel,
        out_shape=[pltpu.VMEM((64, 128), F32)] * 2,
        in_specs=[VM],
        out_specs=[VM, VM],
    )(slab)
    upward = [(i, i + 1) for i in range(grid_z - 1)]
    downward = [(b, a) for a, b in upward]
    from_left = lax.ppermute(high, "gz", upward)
    from_right = lax.ppermute(low, "gz", downward)
    planes = pltpu.VMEM((18, 32, 128), F32)
    pieces, coef = pl.pallas_call(
        filter_kernel,
        out_shape=[pltpu.VMEM((32, 56, 128), F32), pltpu.VMEM((2, 56, 128), F32)],
        in_specs=[SM, SM, VM, VM, VM],
        out_specs=[VM, VM],
        scratch_shapes=[planes] * 3
        + [pltpu.VMEM((2, 32, 128), F32)] * 2
        + [pltpu.VMEM((7, 16, 32, 128), F32), pltpu.VMEM((2, 7, 32, 128), F32)],
    )(slot_order, index, slab, near(from_left), near(from_right))
    owned = lax.all_to_all(pieces, ("gx", "gy"), 0, 0, tiled=True)
    own, part = pl.pallas_call(
        galerkin_kernel,
        out_shape=[pltpu.VMEM((32, 256), F32)] * 2,
        in_specs=[SM, VM, VM],
        out_specs=[VM, VM],
        scratch_shapes=[pltpu.VMEM((32, 2048), F32)] * 3 + [pltpu.VMEM((32, 1024), F32)],
    )(index, near(owned.reshape(32 * 56, 128)), near(coef))
    pairs = [(k, k ^ 1) for k in range(lax.axis_size("gy"))]
    other = lax.ppermute(part, "gy", pairs)
    spread = pl.pallas_call(
        copies_kernel,
        out_shape=pltpu.VMEM((16, 64, 256), F32),
        in_specs=[VM, VM, VM],
        out_specs=VM,
    )(near(own), near(part), near(other))
    spread = lax.all_to_all(spread, "gz", 0, 0, tiled=True)
    return factor(index, table, near(spread.reshape(1024, 256)))


def solution(mesh):
    in_specs = (P(None, "gx", "gy", "gz"), P("gx", "gy", "gz"), P(), P())
    out_specs = P(("gx", "gy"), "gz")
    return jax.shard_map(
        on_device, mesh=mesh, in_specs=in_specs, out_specs=out_specs, check_vma=False
    )
```

```python
import functools
import math

import jax
import jax.numpy as jnp
from jax import lax
from jax.experimental import pallas as pl
from jax.experimental.pallas import tpu as pltpu
from jax.sharding import PartitionSpec as P

PASSES = 4
UPPER = 120.0
LOWER = 24.0
SHIFT = 1.0
F32 = jnp.float32
BF16 = jnp.bfloat16
HIGHEST = lax.Precision.HIGHEST


VM = pl.BlockSpec(memory_space=pltpu.VMEM)


def near(value):
    return pltpu.with_memory_space_constraint(value, pltpu.VMEM)


SM = pl.BlockSpec(memory_space=pltpu.SMEM)


def cheb_factors(step_index):
    center = (UPPER + LOWER) / (UPPER - LOWER)
    growth = math.log(center + math.sqrt(center * center - 1.0))

    def chebval(degree):
        expo = math.exp(degree * growth)
        return 0.5 * (expo + 1.0 / expo)

    if step_index == 0:
        return (1.0 / chebval(1), 0.0)
    return (
        2.0 * chebval(step_index) / chebval(step_index + 1),
        chebval(step_index - 1) / chebval(step_index + 1),
    )


def position():
    return lax.axis_index("gx") * 4 + lax.axis_index("gy"), lax.axis_index("gz")


def iota(shape, dim):
    return lax.broadcasted_iota(jnp.int32, shape, dim)


def roll(value, shift, axis):
    shift = shift % value.shape[axis]
    if shift == 0:
        return value
    return pltpu.roll(value, shift, axis)


def pack_kernel(vec_ref, ids_ref, kappa_ref, out_ref):
    ids = ids_ref[...]
    kappa = jnp.zeros(ids.shape, F32)
    for layer in range(kappa_ref.shape[0]):
        kappa = jnp.where(ids == layer, kappa_ref[layer], kappa)
    out_ref[:, 0:16, :] = vec_ref[...]
    out_ref[:, 16:32, :] = jnp.broadcast_to(kappa[None], (out_ref.shape[0], 16, 128))


def slab_plane(ref, field, plane):
    i, x = plane // 2, plane % 2
    base = 16 * field + 8 * x
    return jnp.concatenate([ref[4 * i + j, base : base + 8, :] for j in range(4)], axis=0)


def edge_kernel(slab_ref, low_ref, high_ref):
    lane = iota((32, 128), 1)
    for field in range(2):
        low = jnp.zeros((32, 128), F32)
        high = jnp.zeros((32, 128), F32)
        for plane in range(16):
            tile = slab_plane(slab_ref, field, plane)
            here = (lane >> 3) == plane
            low = jnp.where(here, roll(tile, 8 * plane, 1), low)
            high = jnp.where(here, roll(tile, 8 * plane + 8, 1), high)
        low_ref[32 * field : 32 * field + 32, :] = low
        high_ref[32 * field : 32 * field + 32, :] = high


def filter_kernel(
    order_ref, slab_ref, left_ref, right_ref, out_ref, coef_ref,
    za, zb, ka, ends_a, ends_b, main, side,
):
    mine, at_z = position()
    lane = iota((32, 128), 1)
    row = iota((32, 128), 0)
    slot = lane & 7
    zero_plane = jnp.zeros((32, 128), F32)
    for dest, field in ((za, 0), (ka, 1)):
        dest[0] = zero_plane
        dest[17] = zero_plane
        for plane in range(16):
            dest[plane + 1] = slab_plane(slab_ref, field, plane)
    zb[0] = zero_plane
    zb[17] = zero_plane
    ends_a[0] = right_ref[0:32, :]
    ends_a[1] = left_ref[0:32, :]

    def edges_of(right, left):
        return jnp.where(slot == 0, right, jnp.where(slot == 1, roll(left, -6, 1), 0.0))

    def z_pair(z, edges, plane):
        ahead = roll(edges, 127 - 8 * plane, 1)
        return (
            jnp.where(lane == 127, ahead, roll(z, 127, 1)),
            jnp.where(lane == 0, ahead, roll(z, 1, 1)),
        )

    def collect(inner, z, plane):
        return jnp.where((lane >> 1) == 4 * plane, roll(z, 8 * plane + 1, 1), inner)

    def end_pairs(right, left, inner):
        return (
            (roll(right, 127, 1), jnp.where(slot == 0, inner, roll(right, 1, 1))),
            (jnp.where(slot == 7, roll(inner, 6, 1), roll(left, 127, 1)), roll(left, 1, 1)),
        )

    half = 0.5 * 2.0 / (UPPER - LOWER)
    center = (UPPER + LOWER) / (UPPER - LOWER)

    def weights(store, k, kxp, kxm, kzp, kzm, first_x, last_x, keep):
        xp = half * (k + kxp)
        xm = half * (k + kxm)
        yp = half * (k + jnp.where(row == 31, 0.0, roll(k, 31, 0)))
        ym = half * (k + jnp.where(row == 0, 0.0, roll(k, 1, 0)))
        zp = half * (k + kzp)
        zm = half * (k + kzm)
        total = xp + xm + yp + ym + zp + zm
        values = (
            xp if last_x is None else jnp.where(last_x, 0.0, xp),
            xm if first_x is None else jnp.where(first_x, 0.0, xm),
            jnp.where(row == 31, 0.0, yp),
            jnp.where(row == 0, 0.0, ym),
            zp,
            zm,
            center - total,
        )
        for n, value in enumerate(values):
            store(n, value if keep is None else jnp.where(keep, value, 0.0))

    k_right, k_left = right_ref[32:64, :], left_ref[32:64, :]
    k_edges = edges_of(k_right, k_left)
    k_inner = zero_plane
    for plane in range(16):
        k = ka[plane + 1]
        kzp, kzm = z_pair(k, k_edges, plane)
        k_inner = collect(k_inner, k, plane)

        def store(n, value, plane=plane):
            main[n, plane] = value

        weights(store, k, ka[plane + 2], ka[plane], kzp, kzm, None, None, None)
    first_x, last_x = lane < 8, lane >= 120
    for n, (k, pair, keep) in enumerate(
        zip(
            (k_right, k_left),
            end_pairs(k_right, k_left, k_inner),
            (at_z < 15, at_z > 0),
        )
    ):
        kxp = jnp.where(last_x, 0.0, roll(k, -8, 1))
        kxm = jnp.where(first_x, 0.0, roll(k, 8, 1))

        def store(m, value, n=n):
            side[n, m] = value

        weights(store, k, kxp, kxm, *pair, first_x, last_x, keep)

    def combine(w, z, xp, xm, zp, zm, step, previous):
        one, two = cheb_factors(step)
        acc = w(6) * z + (w(0) * xp + w(1) * xm)
        acc = acc + (w(2) * roll(z, 31, 0) + w(3) * roll(z, 1, 0))
        acc = one * (acc + (w(4) * zp + w(5) * zm))
        return acc if step == 0 else acc - two * previous()

    for step in range(PASSES):
        src, dest = (za, zb) if step % 2 == 0 else (zb, za)
        end_src, end_dest = (ends_a, ends_b) if step % 2 == 0 else (ends_b, ends_a)
        right, left = end_src[0], end_src[1]
        edges = edges_of(right, left)
        inner = zero_plane
        for plane in range(16):
            z = src[plane + 1]
            inner = collect(inner, z, plane)
            zp, zm = z_pair(z, edges, plane)
            dest[plane + 1] = combine(
                lambda n, plane=plane: main[n, plane],
                z, src[plane + 2], src[plane], zp, zm, step,
                lambda plane=plane, dest=dest: dest[plane + 1],
            )
        for n, (z, (zp, zm)) in enumerate(zip((right, left), end_pairs(right, left, inner))):
            end_dest[n] = combine(
                lambda m, n=n: side[n, m],
                z, roll(z, -8, 1), roll(z, 8, 1), zp, zm, step,
                lambda n=n, end_dest=end_dest: end_dest[n],
            )

    ghosts = []
    for j in range(4):
        rows = slice(8 * j, 8 * j + 8)
        pair = []
        for n, keep, start in ((1, 7, 121), (0, 0, 0)):
            column = jnp.where((iota((8, 128), 1) & 7) == keep, ends_a[n, rows, :], 0.0)
            spread = pltpu.roll(column, start, 1, stride=1, stride_axis=0)
            pair.append(jnp.sum(spread, axis=0, keepdims=True))
        ghosts.append(pair)
    sub = iota((8, 128), 0)
    lane8 = iota((8, 128), 1)
    lane1 = iota((1, 128), 1)
    zero_row = jnp.zeros((1, 128), F32)
    for r in range(32):
        i, j = r // 4, r % 4
        dest = lax.shift_right_logical(order_ref[at_z, r], 4)
        rows = slice(8 * j, 8 * j + 8)
        out_ref[dest, 0:8, :] = za[2 * i + 1, rows]
        out_ref[dest, 8:16, :] = za[2 * i + 2, rows]
        out_ref[dest, 16:24, :] = za[2 * i, rows]
        out_ref[dest, 24:32, :] = za[2 * i + 3, rows]
        for x in range(2):
            out_ref[dest, 50 + x : 51 + x, :] = (
                za[2 * i + 1 + x, 8 * j - 1 : 8 * j] if j > 0 else zero_row
            )
            out_ref[dest, 52 + x : 53 + x, :] = (
                za[2 * i + 1 + x, 8 * j + 8 : 8 * j + 9] if j < 3 else zero_row
            )
        line = jnp.where(lane1 < 32, roll(ghosts[j][1], 16 - 16 * i, 1), 0.0)
        line = jnp.where(lane1 < 16, roll(ghosts[j][0], -16 * i, 1), line)
        out_ref[dest, 54:55, :] = line
        out_ref[dest, 55:56, :] = zero_row

        def coefficients(slot, i=i, j=j, rows=rows):
            coef_ref[slot, 0:8, :] = ka[2 * i + 1, rows]
            coef_ref[slot, 8:16, :] = ka[2 * i + 2, rows]
            coef_ref[slot, 16:24, :] = ka[2 * i, rows]
            coef_ref[slot, 24:32, :] = ka[2 * i + 3, rows]
            for x in range(2):
                coef_ref[slot, 32 + x : 33 + x, :] = (
                    ka[2 * i + 1 + x, 8 * j - 1 : 8 * j] if j > 0 else zero_row
                )
                coef_ref[slot, 34 + x : 35 + x, :] = (
                    ka[2 * i + 1 + x, 8 * j + 8 : 8 * j + 9] if j < 3 else zero_row
                )
                coef_ref[slot, 40 + 8 * x : 48 + 8 * x, :] = roll(
                    k_edges[rows, :], 127 - 8 * (2 * i + x), 1
                )

        @pl.when(dest == mine)
        def _(coefficients=coefficients):
            coefficients(0)

        @pl.when(dest == 0)
        def _(coefficients=coefficients):
            coefficients(1)

    first = [out_ref[0, 8 * n : 8 * n + 8, :] for n in range(4)]
    edges = [out_ref[0, 50 + n : 51 + n, :] for n in range(4)]
    ends = out_ref[0, 54:55, :]
    for core in range(2):
        body = jnp.concatenate(
            [pack_half(first[0], first[1], core), pack_half(first[2], first[3], core)], axis=0
        )
        sides = jnp.concatenate(
            [pack_half(edges[0], edges[1], core), pack_half(edges[2], edges[3], core)], axis=0
        )
        at = 64 if core == 0 else 63
        below = 40 if core == 0 else 32
        packed = jnp.zeros((8, 128), F32)
        for x in range(2):
            column = first[x][:, at : at + 1]
            packed = jnp.where(lane8 == below + 64 * x + sub, column, packed)
        line = jnp.sum(packed, axis=0, keepdims=True)
        outer = 32 if core == 0 else 40
        start = 0 if core == 0 else 16
        for x in range(2):
            here = (lane1 >> 3) == (outer + 64 * x) // 8
            line = jnp.where(here, roll(ends, outer + 64 * x - start - 8 * x, 1), line)

        def spread(k, carry, core=core, body=body, sides=sides, line=line):
            dest = 2 * k + core
            out_ref[dest, 32:48, :] = body
            out_ref[dest, 48:50, :] = sides
            out_ref[dest, 54:55, :] = out_ref[dest, 54:55, :] + line
            return carry

        lax.fori_loop(0, 16, spread, 0)


def pack_half(even, odd, core):
    lane = iota(even.shape, 1)
    if core == 0:
        return jnp.where(lane < 64, even, roll(odd, 64, 1))
    return jnp.where(lane < 64, roll(even, 64, 1), odd)


def nt_dot(a, b):
    return lax.dot_general(
        a, b, (((1,), (1,)), ((), ())), precision=HIGHEST, preferred_element_type=F32
    )


def galerkin_kernel(table_ref, data_ref, coef_ref, own_ref, part_ref, left, image, cross, ending):
    sub = iota((8, 128), 0)
    lane8 = iota((8, 128), 1)
    lane = iota((32, 128), 1)
    scaling = 1.0 / math.sqrt(2048.0)
    eye = (iota((32, 32), 0) == iota((32, 32), 1)).astype(F32)
    core = lax.rem(lax.axis_index("gy"), 2)

    def field(r):
        return data_ref[pl.ds(r, 32, stride=56), :]

    def span(r):
        return slice(128 * r, 128 * r + 128)

    def weights(part):
        k0 = coef_ref[part, 0:8, :]
        k1 = coef_ref[part, 8:16, :]
        km = coef_ref[part, 16:24, :]
        kp = coef_ref[part, 24:32, :]
        found = []
        for x in range(2):
            k = (k0, k1)[x]
            below = coef_ref[part, 32 + x : 33 + x, :]
            above = coef_ref[part, 34 + x : 35 + x, :]
            ends = coef_ref[part, 40 + 8 * x : 48 + 8 * x, :]
            xm = 0.5 * (k + (km, k0)[x])
            xp = 0.5 * (k + (k1, kp)[x])
            ym = 0.5 * (k + jnp.where(sub == 0, below, roll(k, 1, 0)))
            yp = 0.5 * (k + jnp.where(sub == 7, above, roll(k, 7, 0)))
            zm = 0.5 * (k + jnp.where(lane8 == 0, ends, roll(k, 1, 1)))
            zp = 0.5 * (k + jnp.where(lane8 == 127, ends, roll(k, 127, 1)))
            found.append((xm, xp, ym, yp, zm, zp, xp + xm + yp + ym + zp + zm))
        return found

    for r in range(16):
        left[:, span(r)] = field(r)
    columns = jnp.zeros((32, 128), F32)
    y_low, y_high = [], []
    for x, (xm, xp, ym, yp, zm, zp, diag) in enumerate(weights(0)):
        zm_in = jnp.where(lane8 == 0, 0.0, zm)
        zp_in = jnp.where(lane8 == 127, 0.0, zp)
        for y in range(8):
            r = 8 * x + y
            one = slice(y, y + 1)
            z = left[:, span(r)]
            beside = zp_in[one] * roll(z, 127, 1) + zm_in[one] * roll(z, 1, 1)
            if x == 0:
                beside = beside + xp[one] * left[:, span(r + 8)]
            else:
                beside = beside + xm[one] * left[:, span(r - 8)]
            if y < 7:
                beside = beside + yp[one] * left[:, span(r + 1)]
            if y > 0:
                beside = beside + ym[one] * left[:, span(r - 1)]
            image[:, span(r)] = diag[one] * z - beside
            cross[:, span(r)] = (xm, xp)[x][one] * field(16 + r)
            if y == 0:
                y_low.append((r, ym[one] * field(50 + x)))
            if y == 7:
                y_high.append((r, yp[one] * field(52 + x)))
            columns = jnp.where(lane == r, roll(zm[one] * z, r, 1), columns)
            columns = jnp.where(lane == 16 + r, roll(zp[one] * z, 17 + r, 1), columns)
    own_ref[:, 0:32] = scaling * nt_dot(left[...], image[...]) + SHIFT * eye
    own_ref[:, 32:64] = -scaling * nt_dot(left[:, 0:1024], cross[:, 0:1024])
    own_ref[:, 64:96] = -scaling * nt_dot(left[:, 1024:2048], cross[:, 1024:2048])
    for at, pair in ((96, y_low), (128, y_high)):
        block = sum(nt_dot(left[:, span(r)], ghost) for r, ghost in pair)
        own_ref[:, at : at + 32] = -scaling * block
    ghost = field(54)
    low = jnp.where(lane < 16, columns, 0.0)
    high = jnp.where((lane >= 16) & (lane < 32), columns, 0.0)
    own_ref[:, 160:192] = -scaling * nt_dot(low, ghost)
    own_ref[:, 192:224] = -scaling * nt_dot(high, ghost)

    even, odd = weights(1)

    def pack(a, b):
        return jnp.where(core == 0, pack_half(a, b, 0), pack_half(a, b, 1))

    w_out = pack(even[0], odd[1])
    w_in = pack(even[1], odd[0])
    ym, yp, zm, zp, diag = (pack(even[n], odd[n]) for n in range(2, 7))
    first8 = (lane8 & 63) == 0
    last8 = (lane8 & 63) == 63
    zm_in = jnp.where(first8 & (core == 0), 0.0, zm)
    zp_in = jnp.where(last8 & (core == 1), 0.0, zp)
    z_out = jnp.where(core == 0, jnp.where(first8, zm, 0.0), jnp.where(last8, zp, 0.0))
    at_first = (lane & 63) == 0
    at_last = (lane & 63) == 63
    for y in range(8):
        left[:, span(y)] = field(32 + y)
    for y in range(8):
        one = slice(y, y + 1)
        z = left[:, span(y)]
        z_low = jnp.where(at_first, roll(ghost, -(32 + y), 1), roll(z, 1, 1))
        z_high = jnp.where(at_last, roll(ghost, 23 - y, 1), roll(z, 127, 1))
        beside = zp_in[one] * z_high + zm_in[one] * z_low + w_in[one] * roll(z, 64, 1)
        if y < 7:
            beside = beside + yp[one] * left[:, span(y + 1)]
        if y > 0:
            beside = beside + ym[one] * left[:, span(y - 1)]
        image[:, span(y)] = diag[one] * z - beside
        side = w_out[one] * field(40 + y)
        cross[:, span(y)] = jnp.where(lane < 64, side, 0.0)
        cross[:, span(8 + y)] = jnp.where(lane < 64, 0.0, side)
        ending[:, span(y)] = z_out[one] * jnp.where(core == 0, z_low, z_high)
    half = slice(0, 1024)
    shift = jnp.where(core == 0, SHIFT, 0.0) * eye
    part_ref[:, 0:32] = scaling * nt_dot(left[:, half], image[:, half]) + shift
    part_ref[:, 32:64] = -scaling * nt_dot(left[:, half], cross[:, half])
    part_ref[:, 64:96] = -scaling * nt_dot(left[:, half], cross[:, 1024:2048])
    part_ref[:, 96:128] = -scaling * nt_dot(left[:, span(0)], ym[0:1] * field(48))
    part_ref[:, 128:160] = -scaling * nt_dot(left[:, span(7)], yp[7:8] * field(49))
    block = -scaling * nt_dot(left[:, half], ending[...])
    part_ref[:, 160:192] = jnp.where(core == 0, block, 0.0)
    part_ref[:, 192:224] = jnp.where(core == 0, 0.0, block)
    own_ref[:, 224:256] = jnp.zeros((32, 32), F32)
    part_ref[:, 224:256] = jnp.zeros((32, 32), F32)


def copies_kernel(own_ref, part_ref, other_ref, out_ref):
    own = own_ref[...]
    panel = part_ref[...] + other_ref[...]
    for n in range(16):
        out_ref[n, 0:32, :] = own
        out_ref[n, 32:64, :] = panel


def halves(value):
    high = value.astype(BF16)
    return high, (value - high.astype(F32)).astype(BF16)


def dot3(a, b, dims):
    ah, al = a
    bh, bl = b

    def one(p, q):
        return lax.dot_general(p, q, (dims, ((), ())), preferred_element_type=F32)

    return one(ah, bh) + (one(ah, bl) + one(al, bh))


NN = ((1,), (0,))
NT = ((1,), (1,))


def factor_kernel(
    table_ref, data_ref, out_ref,
    diag, al, il, tinv, er, el, xm, mm, lm, ua, vm, cm, mh, ml, uh, ul,
    left, right, ready, touched, row_list, col_list, col_at, count,
):
    mine, at_z = position()
    lane = iota((32, 128), 1)
    corner = (mine == 0) & (at_z == 0)

    def base(l):
        return table_ref[3, l, 1]

    def slot0(l):
        return table_ref[3, l, 2]

    def block_rows(l):
        return pl.ds(pl.multiple_of(32 * l, 32), 32)

    def tile_of(n):
        return pl.ds(pl.multiple_of(128 * n, 128), 128)

    def place(dest, row, tile, sub, source_row, u):
        source = data_ref[
            pl.ds(pl.multiple_of(source_row, 32), 32), 128 * (u // 4) : 128 * (u // 4) + 128
        ]
        moved = pltpu.roll(source, (32 * sub - 32 * u) & 127, 1)
        at = (pl.ds(pl.multiple_of(row, 32), 32), tile_of(tile))
        dest[at] = dest[at] + jnp.where((lane >> 5) == sub, moved, 0.0)

    def put(dest, row, column, block):
        padded = jnp.concatenate([block, jnp.zeros((32, 96), F32)], axis=1)
        at = (block_rows(row), tile_of(lax.shift_right_logical(column, 2)))
        dest[at] = dest[at] + pltpu.roll(padded, (32 * column) & 127, 1)

    def for_hits(which, l, action):
        for u in range(7):
            at = table_ref[which, l, u]

            @pl.when(at >= 0)
            def _(u=u, at=at):
                action(u, at)

    def for_blocks(action):
        def each(l, carry):
            action(l)
            return carry

        lax.fori_loop(0, 16, each, 0)

    def nn(a, b):
        return lax.dot_general(a, b, (NN, ((), ())), precision=HIGHEST, preferred_element_type=F32)

    mh[...] = jnp.zeros(mh.shape, BF16)
    ml[...] = jnp.zeros(ml.shape, BF16)
    any_link = jnp.bool_(False)
    for l in range(16):
        diag[32 * l : 32 * l + 32, :] = data_ref[64 * l + 32 : 64 * l + 64, 0:128]
        left[l] = jnp.int32(-1)
        right[l] = jnp.int32(-1)
        ready[l] = jnp.int32(0)
        touched[l] = jnp.int32(0)
    for l in range(15):
        link = base(l) == base(l + 1)
        any_link = any_link | link

        @pl.when(link)
        def _(l=l):
            right[l] = jnp.int32(l + 1)
            left[l + 1] = jnp.int32(l)
            ahead = data_ref[64 * l + 32 : 64 * l + 64, 128:256]
            back = data_ref[64 * l + 96 : 64 * l + 128, 128:256]
            er[32 * l : 32 * l + 32, :] = roll(ahead, -64, 1)
            el[32 * l + 32 : 32 * l + 64, :] = roll(back, -32, 1)

    @pl.when(any_link)
    def _():
        xm[...] = (iota((512, 512), 0) == iota((512, 512), 1)).astype(F32)

    @pl.when(corner)
    def _():
        lm[...] = jnp.zeros(lm.shape, F32)

    def batched_inverse():
        lane16 = iota((16, 128), 1)
        for g in range(8):
            wide = diag[pl.ds(4 * g, 16, stride=32), :]
            for t in range(1, 4):
                row = diag[pl.ds(4 * g + t, 16, stride=32), :]
                wide = jnp.where((lane16 >> 5) == t, roll(row, 32 * t, 1), wide)
            turned = jnp.transpose(jnp.concatenate([wide, jnp.zeros((112, 128), F32)], axis=0))
            for t in range(4):
                al[4 * g + t] = turned[32 * t : 32 * t + 32, :]
        sub = iota((8, 128), 0)
        for q in range(4):
            low = 8 * q
            a = [al[low + t, low : low + 8, :] for t in range(8)]
            w = [(sub == t).astype(F32) for t in range(8)]
            for t in range(8):
                pivot = a[t][t : t + 1, :]
                inv = lax.rsqrt(pivot)
                inv = inv * (1.5 - 0.5 * pivot * inv * inv)
                a[t] = a[t] * inv
                w[t] = w[t] * inv
                for k in range(t + 1, 8):
                    f = a[k][t : t + 1, :] * inv
                    a[k] = a[k] - f * a[t]
                    w[k] = w[k] - f * w[t]
            lead = {}
            for r in range(q + 1, 4):
                old = [al[low + k, 8 * r : 8 * r + 8, :] for k in range(8)]
                for t in range(8):
                    total = w[t][0:1, :] * old[0]
                    for k in range(1, t + 1):
                        total = total + w[t][k : k + 1, :] * old[k]
                    lead[t, r] = total
            unit = {(t, q): w[t] for t in range(8)}
            for r in range(q):
                old = [il[low + k, 8 * r : 8 * r + 8, :] for k in range(8)]
                for t in range(8):
                    total = w[t][0:1, :] * old[0]
                    for k in range(1, t + 1):
                        total = total + w[t][k : k + 1, :] * old[k]
                    unit[t, r] = total
            for t in range(8):
                for r in range(4):
                    il[low + t, 8 * r : 8 * r + 8, :] = unit.get((t, r), jnp.zeros((8, 128), F32))
            for i in range(low + 8, 32):
                own = i // 8
                f = [lead[t, own][i % 8 : i % 8 + 1, :] for t in range(8)]
                for r in range(own, 4):
                    value = al[i, 8 * r : 8 * r + 8, :]
                    for t in range(8):
                        value = value - f[t] * lead[t, r]
                    al[i, 8 * r : 8 * r + 8, :] = value
                for r in range(q + 1):
                    value = -f[0] * unit[0, r]
                    if r < q:
                        value = value + il[i, 8 * r : 8 * r + 8, :]
                    for t in range(1, 8):
                        value = value - f[t] * unit[t, r]
                    il[i, 8 * r : 8 * r + 8, :] = value
        for g in range(8):
            stack = jnp.concatenate([il[4 * g + t] for t in range(4)], axis=0)
            turned = jnp.transpose(stack)[0:16, :]
            for t in range(4):
                tinv[pl.ds(4 * g + t, 16, stride=32), :] = jnp.where(
                    lane16 < 32, roll(turned, -32 * t, 1), 0.0
                )

    def eliminate(l):
        before, after = left[l], right[l]
        rows = block_rows(l)
        inverse = tinv[rows, 0:32]

        @pl.when(corner)
        def _():
            put(lm, l, l, nt_dot(diag[rows, 0:32], inverse))

        @pl.when(touched[l] == 0)
        def _():
            at = (rows, tile_of(lax.shift_right_logical(l, 2)))
            moved = pltpu.roll(tinv[rows, :], (32 * l) & 127, 1)
            mh[at], ml[at] = halves(moved)

            @pl.when((before >= 0) | (after >= 0))
            def _():
                mm[rows, :] = jnp.zeros((32, 512), F32)
                mm[at] = moved

        @pl.when(touched[l] > 0)
        def _():
            strip = nn(inverse, xm[rows, :])
            mm[rows, :] = strip
            mh[rows, :], ml[rows, :] = halves(strip)

        def fold(near, link):
            at = block_rows(near)
            factor = nt_dot(link[at, 0:32], inverse)
            diag[at, 0:32] = diag[at, 0:32] - nt_dot(factor, factor)
            xm[at, :] = xm[at, :] - nn(factor, mm[rows, :])
            touched[near] = jnp.int32(1)

            @pl.when(corner)
            def _():
                put(lm, near, l, factor)

        @pl.when(after >= 0)
        def _():
            fold(after, el)
            left[after] = before

        @pl.when(before >= 0)
        def _():
            fold(before, er)
            right[before] = after

        @pl.when((before >= 0) & (after >= 0))
        def _():
            one = nt_dot(er[block_rows(before), 0:32], inverse)
            two = nt_dot(el[block_rows(after), 0:32], inverse)
            er[block_rows(before), 0:32] = -nt_dot(one, two)
            el[block_rows(after), 0:32] = -nt_dot(two, one)

        ready[l] = jnp.int32(2)

    simple = jnp.logical_not(any_link | corner)

    def level(unused):
        batched_inverse()

        def mark(l):
            before, after, slot = left[l], right[l], slot0(l)
            free = (before < 0) | (slot0(jnp.maximum(before, 0)) > slot)
            free = free & ((after < 0) | (slot0(jnp.maximum(after, 0)) > slot))
            ready[l] = jnp.where(ready[l] == 2, 2, jnp.where(free, 1, 0))

        count[0] = jnp.int32(0)

        def visit(l):
            @pl.when(ready[l] == 1)
            def _():
                eliminate(l)

            @pl.when(ready[l] == 0)
            def _():
                count[0] = count[0] + 1

        @pl.when(simple)
        def _():
            for l in range(16):
                rows = slice(32 * l, 32 * l + 32)
                at = (rows, slice(128 * (l // 4), 128 * (l // 4) + 128))
                mh[at], ml[at] = halves(roll(tinv[rows, :], 32 * (l % 4), 1))

        @pl.when(jnp.logical_not(simple))
        def _():
            for_blocks(mark)
            for_blocks(visit)

        return count[0] > 0

    lax.while_loop(lambda more: more, level, jnp.bool_(True))
    out_ref[...] = jnp.zeros(out_ref.shape, F32)

    def emit(source_row, row_of, number):
        rows = pl.ds(pl.multiple_of(source_row, 128), 128)
        tall = iota((128, 128), 1)
        ua[0:128, :] = jnp.zeros((128, 512), F32)
        for l in range(16):
            slot = slot0(l)
            source = vm[rows, 128 * (l // 4) : 128 * (l // 4) + 128]
            moved = pltpu.roll(source, (32 * slot - 32 * l) & 127, 1)
            at = (slice(0, 128), tile_of(lax.shift_right_logical(slot, 2)))
            ua[at] = jnp.where((tall >> 5) == (slot & 3), moved, ua[at])
        for k in range(4):

            @pl.when(k < number)
            def _(k=k):
                out_ref[pl.ds(pl.multiple_of(row_of(k), 32), 32), 0:512] = ua[
                    32 * k : 32 * k + 32, :
                ]

    @pl.when(mine > 0)
    def _():
        for n in range(32):
            col_at[n] = jnp.int32(-1)
        count[0] = jnp.int32(0)
        count[1] = jnp.int32(0)

        def gather(l):
            @pl.when(table_ref[0, l, 7] > 0)
            def _():
                def one(u, at):
                    @pl.when(col_at[at] < 0)
                    def _():
                        new = count[1]
                        col_at[at] = new
                        col_list[new] = at
                        count[1] = new + 1

                        @pl.when((new & 3) == 0)
                        def _():
                            cm[:, tile_of(lax.shift_right_logical(new, 2))] = jnp.zeros(
                                (512, 128), F32
                            )

                    packed = col_at[at]
                    place(
                        cm, 32 * l, lax.shift_right_logical(packed, 2), packed & 3,
                        64 * l + 32, u,
                    )

                for_hits(0, l, one)

            @pl.when(table_ref[2, l, 7] > 0)
            def _():
                row_list[count[0]] = l
                count[0] = count[0] + 1

            @pl.when(table_ref[1, l, 7] > 0)
            def _():
                def one(u, at):
                    place(
                        out_ref, 32 * table_ref[3, l, 0], lax.shift_right_logical(at, 2),
                        at & 3, 64 * l, u,
                    )

                for_hits(1, l, one)

        for_blocks(gather)
        total = count[0]
        columns = count[1]
        tiles = lax.shift_right_logical(columns + 3, 2)

        def chunk(c, carry):
            @pl.when(total > 4 * c)
            def _():
                ua[0:128, :] = jnp.zeros((128, 512), F32)

                def fill(k, carry):
                    @pl.when(4 * c + k < total)
                    def _():
                        l = row_list[4 * c + k]
                        for_hits(
                            2,
                            l,
                            lambda u, at: place(
                                ua, 32 * k, lax.shift_right_logical(at, 2), at & 3, 64 * l, u
                            ),
                        )

                    return carry

                lax.fori_loop(0, 4, fill, 0)
                part = dot3(halves(ua[0:128, :]), (mh[...], ml[...]), NT)
                vm[0:128, :] = part
                solved = dot3(halves(part), (mh[...], ml[...]), NN)
                uh[...], ul[...] = halves(solved)

                def row_of(k):
                    return 32 * table_ref[3, row_list[jnp.minimum(4 * c + k, total - 1)], 0]

                def column(n, carry):
                    at = (slice(0, 512), tile_of(n))
                    update = dot3((uh[...], ul[...]), halves(cm[at]), NN)
                    tall = iota((128, 128), 1) >> 5
                    for q in range(4):

                        @pl.when(4 * n + q < columns)
                        def _(q=q):
                            to = col_list[4 * n + q]
                            moved = pltpu.roll(update, (32 * to - 32 * q) & 127, 1)
                            moved = jnp.where(tall == (to & 3), moved, 0.0)
                            tile = tile_of(lax.shift_right_logical(to, 2))
                            for k in range(4):

                                @pl.when(4 * c + k < total)
                                def _(k=k):
                                    rows = pl.ds(pl.multiple_of(row_of(k), 32), 32)
                                    out_ref[rows, tile] = (
                                        out_ref[rows, tile] - moved[32 * k : 32 * k + 32, :]
                                    )

                    return carry

                lax.fori_loop(0, tiles, column, 0)

                @pl.when(at_z == 0)
                def _():
                    emit(0, row_of, total - 4 * c)

            return carry

        lax.fori_loop(0, 4, chunk, 0)

    @pl.when(corner)
    def _():
        def rows(c, carry):
            vm[0:128, :] = lm[pl.ds(pl.multiple_of(128 * c, 128), 128), :]
            emit(0, lambda k: 32 * slot0(4 * c + k), 4)
            return carry

        lax.fori_loop(0, 4, rows, 0)
        lower = iota((512, 512), 0) >= iota((512, 512), 1)
        out_ref[:, 0:512] = jnp.where(lower, out_ref[:, 0:512], 0.0)


def factor(table, data):
    big = pltpu.VMEM((512, 512), F32)
    narrow = pltpu.VMEM((512, 128), F32)
    cube = pltpu.VMEM((32, 32, 128), F32)
    short = pltpu.VMEM((128, 512), F32)
    return pl.pallas_call(
        factor_kernel,
        out_shape=jax.ShapeDtypeStruct((512, 1024), F32),
        in_specs=[SM, VM],
        out_specs=VM,
        scratch_shapes=[
            narrow, cube, cube, narrow, narrow, narrow, big, big, big, short, short,
            pltpu.VMEM((512, 1024), F32),
            pltpu.VMEM((512, 512), BF16),
            pltpu.VMEM((512, 512), BF16),
            pltpu.VMEM((128, 512), BF16),
            pltpu.VMEM((128, 512), BF16),
            pltpu.SMEM((16,), jnp.int32),
            pltpu.SMEM((16,), jnp.int32),
            pltpu.SMEM((16,), jnp.int32),
            pltpu.SMEM((16,), jnp.int32),
            pltpu.SMEM((16,), jnp.int32),
            pltpu.SMEM((32,), jnp.int32),
            pltpu.SMEM((32,), jnp.int32),
            pltpu.SMEM((2,), jnp.int32),
        ],
    )(table, data)


def build_table(slot_order, mine, at_z):
    ids = jnp.arange(32, dtype=jnp.int32)[:, None]
    group = slot_order // 16
    wanted = jnp.stack([jnp.zeros((), jnp.int32), mine])
    mask = group[None] == wanted[:, None, None]
    rows = jnp.sum(jnp.where(mask, ids[None], 0), axis=1)
    slots = jnp.sum(jnp.where(mask, slot_order[None], 0), axis=1)
    steps = jnp.array([0, -4, 4, -1, 1, 0, 0], jnp.int32)
    deltas = jnp.array([0, 0, 0, 0, 0, -1, 1], jnp.int32)
    l = jnp.arange(16, dtype=jnp.int32)
    near = rows[:, :, None] + steps
    column = jnp.broadcast_to(l[:, None] + deltas, (16, 7))
    col = (rows % 4)[:, :, None]
    u = jnp.arange(7, dtype=jnp.int32)
    ok = (near >= 0) & (near < 32) & (column >= 0) & (column < 16)
    ok = ok & ~((u == 3) & (col == 0)) & ~((u == 4) & (col == 3))
    none = jnp.full((1, 32), -1, jnp.int32)
    turned = slot_order.T
    shifted = jnp.stack(
        [turned] * 5
        + [jnp.concatenate([none, turned[:-1]]), jnp.concatenate([turned[1:], none])],
        axis=1,
    )
    hit = near[..., None] == jnp.arange(32, dtype=jnp.int32)
    target = jnp.sum(jnp.where(hit, shifted[None], 0), axis=-1)
    target = jnp.where(ok, target, -1)
    at = target - 32 * at_z
    here = jnp.where((target >= 16) & (at >= 0) & (at < 32), at, -1)
    panel = jnp.where((target[1] >= 0) & (target[1] < 16), column, -1)
    three = jnp.concatenate([here, panel[None]], axis=0)
    flag = (jnp.max(three, axis=-1, keepdims=True) >= 0).astype(jnp.int32)
    three = jnp.concatenate([three, flag], axis=-1)
    last = jnp.stack([slots[1] - 16 * mine, rows[0], slots[0]], axis=-1)
    last = jnp.pad(last, ((0, 0), (0, 5)))
    return jnp.concatenate([three, last[None]], axis=0)


def on_device(probe_vectors, layer_ids, layer_kappa, slot_order):
    index_x = lax.axis_index("gx")
    index_y = lax.axis_index("gy")
    index_z = lax.axis_index("gz")
    grid_z = lax.axis_size("gz")
    mine = index_x * lax.axis_size("gy") + index_y
    table = build_table(slot_order, mine, index_z)

    send = pl.pallas_call(
        pack_kernel,
        out_shape=pltpu.VMEM((32, 32, 128), F32),
        in_specs=[VM, VM, SM],
        out_specs=VM,
    )(probe_vectors.reshape(32, 16, 128), layer_ids.reshape(16, 128), layer_kappa)
    slab = near(lax.all_to_all(send, ("gx", "gy"), 0, 0, tiled=True))
    low, high = pl.pallas_call(
        edge_kernel,
        out_shape=[pltpu.VMEM((64, 128), F32)] * 2,
        in_specs=[VM],
        out_specs=[VM, VM],
    )(slab)
    upward = [(i, i + 1) for i in range(grid_z - 1)]
    downward = [(b, a) for a, b in upward]
    from_left = lax.ppermute(high, "gz", upward)
    from_right = lax.ppermute(low, "gz", downward)
    planes = pltpu.VMEM((18, 32, 128), F32)
    pieces, coef = pl.pallas_call(
        filter_kernel,
        out_shape=[pltpu.VMEM((32, 56, 128), F32), pltpu.VMEM((2, 56, 128), F32)],
        in_specs=[SM, VM, VM, VM],
        out_specs=[VM, VM],
        scratch_shapes=[planes] * 3
        + [pltpu.VMEM((2, 32, 128), F32)] * 2
        + [pltpu.VMEM((7, 16, 32, 128), F32), pltpu.VMEM((2, 7, 32, 128), F32)],
    )(slot_order.T, slab, near(from_left), near(from_right))
    owned = lax.all_to_all(pieces, ("gx", "gy"), 0, 0, tiled=True)
    own, part = pl.pallas_call(
        galerkin_kernel,
        out_shape=[pltpu.VMEM((32, 256), F32)] * 2,
        in_specs=[SM, VM, VM],
        out_specs=[VM, VM],
        scratch_shapes=[pltpu.VMEM((32, 2048), F32)] * 3 + [pltpu.VMEM((32, 1024), F32)],
    )(table, near(owned.reshape(32 * 56, 128)), near(coef))
    pairs = [(k, k ^ 1) for k in range(lax.axis_size("gy"))]
    other = lax.ppermute(part, "gy", pairs)
    spread = pl.pallas_call(
        copies_kernel,
        out_shape=pltpu.VMEM((16, 64, 256), F32),
        in_specs=[VM, VM, VM],
        out_specs=VM,
    )(near(own), near(part), near(other))
    spread = lax.all_to_all(spread, "gz", 0, 0, tiled=True)
    return factor(table, near(spread.reshape(1024, 256)))


def solution(mesh):
    in_specs = (P(None, "gx", "gy", "gz"), P("gx", "gy", "gz"), P(), P())
    out_specs = P(("gx", "gy"), "gz")
    return jax.shard_map(
        on_device, mesh=mesh, in_specs=in_specs, out_specs=out_specs, check_vma=False
    )
```

```python
import functools
import math

import jax
import jax.numpy as jnp
from jax import lax
from jax.experimental import pallas as pl
from jax.experimental.pallas import tpu as pltpu
from jax.sharding import PartitionSpec as P

PASSES = 4
UPPER = 120.0
LOWER = 24.0
SHIFT = 1.0
F32 = jnp.float32
BF16 = jnp.bfloat16
HIGHEST = lax.Precision.HIGHEST


VM = pl.BlockSpec(memory_space=pltpu.VMEM)


def near(value):
    return pltpu.with_memory_space_constraint(value, pltpu.VMEM)


SM = pl.BlockSpec(memory_space=pltpu.SMEM)


def cheb_factors(step_index):
    center = (UPPER + LOWER) / (UPPER - LOWER)
    growth = math.log(center + math.sqrt(center * center - 1.0))

    def chebval(degree):
        expo = math.exp(degree * growth)
        return 0.5 * (expo + 1.0 / expo)

    if step_index == 0:
        return (1.0 / chebval(1), 0.0)
    return (
        2.0 * chebval(step_index) / chebval(step_index + 1),
        chebval(step_index - 1) / chebval(step_index + 1),
    )


def position():
    return lax.axis_index("gx") * 4 + lax.axis_index("gy"), lax.axis_index("gz")


def iota(shape, dim):
    return lax.broadcasted_iota(jnp.int32, shape, dim)


def roll(value, shift, axis):
    shift = shift % value.shape[axis]
    if shift == 0:
        return value
    return pltpu.roll(value, shift, axis)


def pack_kernel(vec_ref, ids_ref, kappa_ref, out_ref):
    ids = ids_ref[...]
    kappa = jnp.zeros(ids.shape, F32)
    for layer in range(kappa_ref.shape[0]):
        kappa = jnp.where(ids == layer, kappa_ref[layer], kappa)
    out_ref[:, 0:16, :] = vec_ref[...]
    for dest in range(out_ref.shape[0]):
        core = dest % 2
        out_ref[dest, 16:24, :] = kappa[8 * core : 8 * core + 8, :]


def slab_plane(ref, swap_ref, field, plane):
    i, x = plane // 2, plane % 2
    if field == 0:
        tiles = [ref[4 * i + j, 8 * x : 8 * x + 8, :] for j in range(4)]
    else:
        held = lax.rem(lax.axis_index("gy"), 2) == x
        tiles = [
            jnp.where(held, ref[4 * i + j, 16:24, :], swap_ref[4 * i + j]) for j in range(4)
        ]
    return jnp.concatenate(tiles, axis=0)


def edge_kernel(slab_ref, swap_ref, low_ref, high_ref):
    lane = iota((32, 128), 1)
    for field in range(2):
        low = jnp.zeros((32, 128), F32)
        high = jnp.zeros((32, 128), F32)
        for plane in range(16):
            tile = slab_plane(slab_ref, swap_ref, field, plane)
            here = (lane >> 3) == plane
            low = jnp.where(here, roll(tile, 8 * plane, 1), low)
            high = jnp.where(here, roll(tile, 8 * plane + 8, 1), high)
        low_ref[32 * field : 32 * field + 32, :] = low
        high_ref[32 * field : 32 * field + 32, :] = high


def filter_kernel(
    order_ref, slab_ref, swap_ref, left_ref, right_ref, out_ref, coef_ref,
    za, zb, ka, ends_a, ends_b, main, side,
):
    mine, at_z = position()
    lane = iota((32, 128), 1)
    row = iota((32, 128), 0)
    slot = lane & 7
    zero_plane = jnp.zeros((32, 128), F32)
    for dest, field in ((za, 0), (ka, 1)):
        dest[0] = zero_plane
        dest[17] = zero_plane
        for plane in range(16):
            dest[plane + 1] = slab_plane(slab_ref, swap_ref, field, plane)
    zb[0] = zero_plane
    zb[17] = zero_plane
    ends_a[0] = right_ref[0:32, :]
    ends_a[1] = left_ref[0:32, :]

    def edges_of(right, left):
        return jnp.where(slot == 0, right, jnp.where(slot == 1, roll(left, -6, 1), 0.0))

    def z_pair(z, edges, plane):
        ahead = roll(edges, 127 - 8 * plane, 1)
        return (
            jnp.where(lane == 127, ahead, roll(z, 127, 1)),
            jnp.where(lane == 0, ahead, roll(z, 1, 1)),
        )

    def collect(inner, z, plane):
        return jnp.where((lane >> 1) == 4 * plane, roll(z, 8 * plane + 1, 1), inner)

    def end_pairs(right, left, inner):
        return (
            (roll(right, 127, 1), jnp.where(slot == 0, inner, roll(right, 1, 1))),
            (jnp.where(slot == 7, roll(inner, 6, 1), roll(left, 127, 1)), roll(left, 1, 1)),
        )

    half = 0.5 * 2.0 / (UPPER - LOWER)
    center = (UPPER + LOWER) / (UPPER - LOWER)

    def weights(store, k, kxp, kxm, kzp, kzm, first_x, last_x, keep):
        xp = half * (k + kxp)
        xm = half * (k + kxm)
        yp = half * (k + jnp.where(row == 31, 0.0, roll(k, 31, 0)))
        ym = half * (k + jnp.where(row == 0, 0.0, roll(k, 1, 0)))
        zp = half * (k + kzp)
        zm = half * (k + kzm)
        total = xp + xm + yp + ym + zp + zm
        values = (
            xp if last_x is None else jnp.where(last_x, 0.0, xp),
            xm if first_x is None else jnp.where(first_x, 0.0, xm),
            jnp.where(row == 31, 0.0, yp),
            jnp.where(row == 0, 0.0, ym),
            zp,
            zm,
            center - total,
        )
        for n, value in enumerate(values):
            store(n, value if keep is None else jnp.where(keep, value, 0.0))

    k_right, k_left = right_ref[32:64, :], left_ref[32:64, :]
    k_edges = edges_of(k_right, k_left)
    k_inner = zero_plane
    for plane in range(16):
        k = ka[plane + 1]
        kzp, kzm = z_pair(k, k_edges, plane)
        k_inner = collect(k_inner, k, plane)

        def store(n, value, plane=plane):
            main[n, plane] = value

        weights(store, k, ka[plane + 2], ka[plane], kzp, kzm, None, None, None)
    first_x, last_x = lane < 8, lane >= 120
    for n, (k, pair, keep) in enumerate(
        zip(
            (k_right, k_left),
            end_pairs(k_right, k_left, k_inner),
            (at_z < 15, at_z > 0),
        )
    ):
        kxp = jnp.where(last_x, 0.0, roll(k, -8, 1))
        kxm = jnp.where(first_x, 0.0, roll(k, 8, 1))

        def store(m, value, n=n):
            side[n, m] = value

        weights(store, k, kxp, kxm, *pair, first_x, last_x, keep)

    def combine(w, z, xp, xm, zp, zm, step, previous):
        one, two = cheb_factors(step)
        acc = w(6) * z + (w(0) * xp + w(1) * xm)
        acc = acc + (w(2) * roll(z, 31, 0) + w(3) * roll(z, 1, 0))
        acc = one * (acc + (w(4) * zp + w(5) * zm))
        return acc if step == 0 else acc - two * previous()

    for step in range(PASSES):
        src, dest = (za, zb) if step % 2 == 0 else (zb, za)
        end_src, end_dest = (ends_a, ends_b) if step % 2 == 0 else (ends_b, ends_a)
        right, left = end_src[0], end_src[1]
        edges = edges_of(right, left)
        inner = zero_plane
        for plane in range(16):
            z = src[plane + 1]
            inner = collect(inner, z, plane)
            zp, zm = z_pair(z, edges, plane)
            dest[plane + 1] = combine(
                lambda n, plane=plane: main[n, plane],
                z, src[plane + 2], src[plane], zp, zm, step,
                lambda plane=plane, dest=dest: dest[plane + 1],
            )
        for n, (z, (zp, zm)) in enumerate(zip((right, left), end_pairs(right, left, inner))):
            end_dest[n] = combine(
                lambda m, n=n: side[n, m],
                z, roll(z, -8, 1), roll(z, 8, 1), zp, zm, step,
                lambda n=n, end_dest=end_dest: end_dest[n],
            )

    ghosts = []
    for j in range(4):
        rows = slice(8 * j, 8 * j + 8)
        pair = []
        for n, keep, start in ((1, 7, 121), (0, 0, 0)):
            column = jnp.where((iota((8, 128), 1) & 7) == keep, ends_a[n, rows, :], 0.0)
            spread = pltpu.roll(column, start, 1, stride=1, stride_axis=0)
            pair.append(jnp.sum(spread, axis=0, keepdims=True))
        ghosts.append(pair)
    sub = iota((8, 128), 0)
    lane8 = iota((8, 128), 1)
    lane1 = iota((1, 128), 1)
    zero_row = jnp.zeros((1, 128), F32)
    for r in range(32):
        i, j = r // 4, r % 4
        dest = lax.shift_right_logical(order_ref[at_z, r], 4)
        rows = slice(8 * j, 8 * j + 8)
        out_ref[dest, 0:8, :] = za[2 * i + 1, rows]
        out_ref[dest, 8:16, :] = za[2 * i + 2, rows]
        out_ref[dest, 16:24, :] = za[2 * i, rows]
        out_ref[dest, 24:32, :] = za[2 * i + 3, rows]
        for x in range(2):
            out_ref[dest, 50 + x : 51 + x, :] = (
                za[2 * i + 1 + x, 8 * j - 1 : 8 * j] if j > 0 else zero_row
            )
            out_ref[dest, 52 + x : 53 + x, :] = (
                za[2 * i + 1 + x, 8 * j + 8 : 8 * j + 9] if j < 3 else zero_row
            )
        line = jnp.where(lane1 < 32, roll(ghosts[j][1], 16 - 16 * i, 1), 0.0)
        line = jnp.where(lane1 < 16, roll(ghosts[j][0], -16 * i, 1), line)
        out_ref[dest, 54:55, :] = line
        out_ref[dest, 55:56, :] = zero_row

        def coefficients(slot, i=i, j=j, rows=rows):
            coef_ref[slot, 0:8, :] = ka[2 * i + 1, rows]
            coef_ref[slot, 8:16, :] = ka[2 * i + 2, rows]
            coef_ref[slot, 16:24, :] = ka[2 * i, rows]
            coef_ref[slot, 24:32, :] = ka[2 * i + 3, rows]
            for x in range(2):
                coef_ref[slot, 32 + x : 33 + x, :] = (
                    ka[2 * i + 1 + x, 8 * j - 1 : 8 * j] if j > 0 else zero_row
                )
                coef_ref[slot, 34 + x : 35 + x, :] = (
                    ka[2 * i + 1 + x, 8 * j + 8 : 8 * j + 9] if j < 3 else zero_row
                )
                coef_ref[slot, 40 + 8 * x : 48 + 8 * x, :] = roll(
                    k_edges[rows, :], 127 - 8 * (2 * i + x), 1
                )

        @pl.when(dest == mine)
        def _(coefficients=coefficients):
            coefficients(0)

        @pl.when(dest == 0)
        def _(coefficients=coefficients):
            coefficients(1)

    first = [out_ref[0, 8 * n : 8 * n + 8, :] for n in range(4)]
    edges = [out_ref[0, 50 + n : 51 + n, :] for n in range(4)]
    ends = out_ref[0, 54:55, :]
    for core in range(2):
        body = jnp.concatenate(
            [pack_half(first[0], first[1], core), pack_half(first[2], first[3], core)], axis=0
        )
        sides = jnp.concatenate(
            [pack_half(edges[0], edges[1], core), pack_half(edges[2], edges[3], core)], axis=0
        )
        at = 64 if core == 0 else 63
        below = 40 if core == 0 else 32
        packed = jnp.zeros((8, 128), F32)
        for x in range(2):
            column = first[x][:, at : at + 1]
            packed = jnp.where(lane8 == below + 64 * x + sub, column, packed)
        line = jnp.sum(packed, axis=0, keepdims=True)
        outer = 32 if core == 0 else 40
        start = 0 if core == 0 else 16
        for x in range(2):
            here = (lane1 >> 3) == (outer + 64 * x) // 8
            line = jnp.where(here, roll(ends, outer + 64 * x - start - 8 * x, 1), line)

        def spread(k, carry, core=core, body=body, sides=sides, line=line):
            dest = 2 * k + core
            out_ref[dest, 32:48, :] = body
            out_ref[dest, 48:50, :] = sides
            out_ref[dest, 54:55, :] = out_ref[dest, 54:55, :] + line
            return carry

        lax.fori_loop(0, 16, spread, 0)


def pack_half(even, odd, core):
    lane = iota(even.shape, 1)
    if core == 0:
        return jnp.where(lane < 64, even, roll(odd, 64, 1))
    return jnp.where(lane < 64, roll(even, 64, 1), odd)


def nt_dot(a, b):
    return lax.dot_general(
        a, b, (((1,), (1,)), ((), ())), precision=HIGHEST, preferred_element_type=F32
    )


def galerkin_kernel(table_ref, data_ref, coef_ref, own_ref, part_ref, left, image, cross, ending):
    sub = iota((8, 128), 0)
    lane8 = iota((8, 128), 1)
    lane = iota((32, 128), 1)
    scaling = 1.0 / math.sqrt(2048.0)
    eye = (iota((32, 32), 0) == iota((32, 32), 1)).astype(F32)
    core = lax.rem(lax.axis_index("gy"), 2)

    def field(r):
        return data_ref[pl.ds(r, 32, stride=56), :]

    def span(r):
        return slice(128 * r, 128 * r + 128)

    def weights(part):
        k0 = coef_ref[part, 0:8, :]
        k1 = coef_ref[part, 8:16, :]
        km = coef_ref[part, 16:24, :]
        kp = coef_ref[part, 24:32, :]
        found = []
        for x in range(2):
            k = (k0, k1)[x]
            below = coef_ref[part, 32 + x : 33 + x, :]
            above = coef_ref[part, 34 + x : 35 + x, :]
            ends = coef_ref[part, 40 + 8 * x : 48 + 8 * x, :]
            xm = 0.5 * (k + (km, k0)[x])
            xp = 0.5 * (k + (k1, kp)[x])
            ym = 0.5 * (k + jnp.where(sub == 0, below, roll(k, 1, 0)))
            yp = 0.5 * (k + jnp.where(sub == 7, above, roll(k, 7, 0)))
            zm = 0.5 * (k + jnp.where(lane8 == 0, ends, roll(k, 1, 1)))
            zp = 0.5 * (k + jnp.where(lane8 == 127, ends, roll(k, 127, 1)))
            found.append((xm, xp, ym, yp, zm, zp, xp + xm + yp + ym + zp + zm))
        return found

    for r in range(16):
        left[:, span(r)] = field(r)
    columns = jnp.zeros((32, 128), F32)
    y_low, y_high = [], []
    for x, (xm, xp, ym, yp, zm, zp, diag) in enumerate(weights(0)):
        zm_in = jnp.where(lane8 == 0, 0.0, zm)
        zp_in = jnp.where(lane8 == 127, 0.0, zp)
        for y in range(8):
            r = 8 * x + y
            one = slice(y, y + 1)
            z = left[:, span(r)]
            beside = zp_in[one] * roll(z, 127, 1) + zm_in[one] * roll(z, 1, 1)
            if x == 0:
                beside = beside + xp[one] * left[:, span(r + 8)]
            else:
                beside = beside + xm[one] * left[:, span(r - 8)]
            if y < 7:
                beside = beside + yp[one] * left[:, span(r + 1)]
            if y > 0:
                beside = beside + ym[one] * left[:, span(r - 1)]
            image[:, span(r)] = diag[one] * z - beside
            cross[:, span(r)] = (xm, xp)[x][one] * field(16 + r)
            if y == 0:
                y_low.append((r, ym[one] * field(50 + x)))
            if y == 7:
                y_high.append((r, yp[one] * field(52 + x)))
            columns = jnp.where(lane == r, roll(zm[one] * z, r, 1), columns)
            columns = jnp.where(lane == 16 + r, roll(zp[one] * z, 17 + r, 1), columns)
    own_ref[:, 0:32] = scaling * nt_dot(left[...], image[...]) + SHIFT * eye
    own_ref[:, 32:64] = -scaling * nt_dot(left[:, 0:1024], cross[:, 0:1024])
    own_ref[:, 64:96] = -scaling * nt_dot(left[:, 1024:2048], cross[:, 1024:2048])
    for at, pair in ((96, y_low), (128, y_high)):
        block = sum(nt_dot(left[:, span(r)], ghost) for r, ghost in pair)
        own_ref[:, at : at + 32] = -scaling * block
    ghost = field(54)
    low = jnp.where(lane < 16, columns, 0.0)
    high = jnp.where((lane >= 16) & (lane < 32), columns, 0.0)
    own_ref[:, 160:192] = -scaling * nt_dot(low, ghost)
    own_ref[:, 192:224] = -scaling * nt_dot(high, ghost)

    even, odd = weights(1)

    def pack(a, b):
        return jnp.where(core == 0, pack_half(a, b, 0), pack_half(a, b, 1))

    w_out = pack(even[0], odd[1])
    w_in = pack(even[1], odd[0])
    ym, yp, zm, zp, diag = (pack(even[n], odd[n]) for n in range(2, 7))
    first8 = (lane8 & 63) == 0
    last8 = (lane8 & 63) == 63
    zm_in = jnp.where(first8 & (core == 0), 0.0, zm)
    zp_in = jnp.where(last8 & (core == 1), 0.0, zp)
    z_out = jnp.where(core == 0, jnp.where(first8, zm, 0.0), jnp.where(last8, zp, 0.0))
    at_first = (lane & 63) == 0
    at_last = (lane & 63) == 63
    for y in range(8):
        left[:, span(y)] = field(32 + y)
    for y in range(8):
        one = slice(y, y + 1)
        z = left[:, span(y)]
        z_low = jnp.where(at_first, roll(ghost, -(32 + y), 1), roll(z, 1, 1))
        z_high = jnp.where(at_last, roll(ghost, 23 - y, 1), roll(z, 127, 1))
        beside = zp_in[one] * z_high + zm_in[one] * z_low + w_in[one] * roll(z, 64, 1)
        if y < 7:
            beside = beside + yp[one] * left[:, span(y + 1)]
        if y > 0:
            beside = beside + ym[one] * left[:, span(y - 1)]
        image[:, span(y)] = diag[one] * z - beside
        side = w_out[one] * field(40 + y)
        cross[:, span(y)] = jnp.where(lane < 64, side, 0.0)
        cross[:, span(8 + y)] = jnp.where(lane < 64, 0.0, side)
        ending[:, span(y)] = z_out[one] * jnp.where(core == 0, z_low, z_high)
    half = slice(0, 1024)
    shift = jnp.where(core == 0, SHIFT, 0.0) * eye
    part_ref[:, 0:32] = scaling * nt_dot(left[:, half], image[:, half]) + shift
    part_ref[:, 32:64] = -scaling * nt_dot(left[:, half], cross[:, half])
    part_ref[:, 64:96] = -scaling * nt_dot(left[:, half], cross[:, 1024:2048])
    part_ref[:, 96:128] = -scaling * nt_dot(left[:, span(0)], ym[0:1] * field(48))
    part_ref[:, 128:160] = -scaling * nt_dot(left[:, span(7)], yp[7:8] * field(49))
    block = -scaling * nt_dot(left[:, half], ending[...])
    part_ref[:, 160:192] = jnp.where(core == 0, block, 0.0)
    part_ref[:, 192:224] = jnp.where(core == 0, 0.0, block)
    own_ref[:, 224:256] = jnp.zeros((32, 32), F32)
    part_ref[:, 224:256] = jnp.zeros((32, 32), F32)


def copies_kernel(own_ref, part_ref, other_ref, out_ref):
    own = own_ref[...]
    panel = part_ref[...] + other_ref[...]
    for n in range(16):
        out_ref[n, 0:32, :] = own
        out_ref[n, 32:64, :] = panel


def halves(value):
    high = value.astype(BF16)
    return high, (value - high.astype(F32)).astype(BF16)


def dot3(a, b, dims):
    ah, al = a
    bh, bl = b

    def one(p, q):
        return lax.dot_general(p, q, (dims, ((), ())), preferred_element_type=F32)

    return one(ah, bh) + (one(ah, bl) + one(al, bh))


NN = ((1,), (0,))
NT = ((1,), (1,))


def factor_kernel(
    table_ref, data_ref, out_ref,
    diag, al, il, tinv, er, el, xm, mm, lm, ua, vm, cm, mh, ml, uh, ul,
    left, right, ready, touched, row_list, col_list, col_at, count,
):
    mine, at_z = position()
    lane = iota((32, 128), 1)
    corner = (mine == 0) & (at_z == 0)

    def base(l):
        return table_ref[3, l, 1]

    def slot0(l):
        return table_ref[3, l, 2]

    def block_rows(l):
        return pl.ds(pl.multiple_of(32 * l, 32), 32)

    def tile_of(n):
        return pl.ds(pl.multiple_of(128 * n, 128), 128)

    def place(dest, row, tile, sub, source_row, u):
        source = data_ref[
            pl.ds(pl.multiple_of(source_row, 32), 32), 128 * (u // 4) : 128 * (u // 4) + 128
        ]
        moved = pltpu.roll(source, (32 * sub - 32 * u) & 127, 1)
        at = (pl.ds(pl.multiple_of(row, 32), 32), tile_of(tile))
        dest[at] = dest[at] + jnp.where((lane >> 5) == sub, moved, 0.0)

    def put(dest, row, column, block):
        padded = jnp.concatenate([block, jnp.zeros((32, 96), F32)], axis=1)
        at = (block_rows(row), tile_of(lax.shift_right_logical(column, 2)))
        dest[at] = dest[at] + pltpu.roll(padded, (32 * column) & 127, 1)

    def for_hits(which, l, action):
        for u in range(7):
            at = table_ref[which, l, u]

            @pl.when(at >= 0)
            def _(u=u, at=at):
                action(u, at)

    def for_blocks(action):
        def each(l, carry):
            action(l)
            return carry

        lax.fori_loop(0, 16, each, 0)

    def nn(a, b):
        return lax.dot_general(a, b, (NN, ((), ())), precision=HIGHEST, preferred_element_type=F32)

    mh[...] = jnp.zeros(mh.shape, BF16)
    ml[...] = jnp.zeros(ml.shape, BF16)
    any_link = jnp.bool_(False)
    for l in range(16):
        diag[32 * l : 32 * l + 32, :] = data_ref[64 * l + 32 : 64 * l + 64, 0:128]
        left[l] = jnp.int32(-1)
        right[l] = jnp.int32(-1)
        ready[l] = jnp.int32(0)
        touched[l] = jnp.int32(0)
    for l in range(15):
        link = base(l) == base(l + 1)
        any_link = any_link | link

        @pl.when(link)
        def _(l=l):
            right[l] = jnp.int32(l + 1)
            left[l + 1] = jnp.int32(l)
            ahead = data_ref[64 * l + 32 : 64 * l + 64, 128:256]
            back = data_ref[64 * l + 96 : 64 * l + 128, 128:256]
            er[32 * l : 32 * l + 32, :] = roll(ahead, -64, 1)
            el[32 * l + 32 : 32 * l + 64, :] = roll(back, -32, 1)

    @pl.when(any_link)
    def _():
        xm[...] = (iota((512, 512), 0) == iota((512, 512), 1)).astype(F32)

    @pl.when(corner)
    def _():
        lm[...] = jnp.zeros(lm.shape, F32)

    def batched_inverse():
        lane16 = iota((16, 128), 1)
        for g in range(8):
            wide = diag[pl.ds(4 * g, 16, stride=32), :]
            for t in range(1, 4):
                row = diag[pl.ds(4 * g + t, 16, stride=32), :]
                wide = jnp.where((lane16 >> 5) == t, roll(row, 32 * t, 1), wide)
            turned = jnp.transpose(jnp.concatenate([wide, jnp.zeros((112, 128), F32)], axis=0))
            for t in range(4):
                al[4 * g + t] = turned[32 * t : 32 * t + 32, :]
        sub = iota((8, 128), 0)
        for q in range(4):
            low = 8 * q
            a = [al[low + t, low : low + 8, :] for t in range(8)]
            w = [(sub == t).astype(F32) for t in range(8)]
            for t in range(8):
                pivot = a[t][t : t + 1, :]
                inv = lax.rsqrt(pivot)
                inv = inv * (1.5 - 0.5 * pivot * inv * inv)
                a[t] = a[t] * inv
                w[t] = w[t] * inv
                for k in range(t + 1, 8):
                    f = a[k][t : t + 1, :] * inv
                    a[k] = a[k] - f * a[t]
                    w[k] = w[k] - f * w[t]
            lead = {}
            for r in range(q + 1, 4):
                old = [al[low + k, 8 * r : 8 * r + 8, :] for k in range(8)]
                for t in range(8):
                    total = w[t][0:1, :] * old[0]
                    for k in range(1, t + 1):
                        total = total + w[t][k : k + 1, :] * old[k]
                    lead[t, r] = total
            unit = {(t, q): w[t] for t in range(8)}
            for r in range(q):
                old = [il[low + k, 8 * r : 8 * r + 8, :] for k in range(8)]
                for t in range(8):
                    total = w[t][0:1, :] * old[0]
                    for k in range(1, t + 1):
                        total = total + w[t][k : k + 1, :] * old[k]
                    unit[t, r] = total
            for t in range(8):
                for r in range(4):
                    il[low + t, 8 * r : 8 * r + 8, :] = unit.get((t, r), jnp.zeros((8, 128), F32))
            for i in range(low + 8, 32):
                own = i // 8
                f = [lead[t, own][i % 8 : i % 8 + 1, :] for t in range(8)]
                for r in range(own, 4):
                    value = al[i, 8 * r : 8 * r + 8, :]
                    for t in range(8):
                        value = value - f[t] * lead[t, r]
                    al[i, 8 * r : 8 * r + 8, :] = value
                for r in range(q + 1):
                    value = -f[0] * unit[0, r]
                    if r < q:
                        value = value + il[i, 8 * r : 8 * r + 8, :]
                    for t in range(1, 8):
                        value = value - f[t] * unit[t, r]
                    il[i, 8 * r : 8 * r + 8, :] = value
        for g in range(8):
            stack = jnp.concatenate([il[4 * g + t] for t in range(4)], axis=0)
            turned = jnp.transpose(stack)[0:16, :]
            for t in range(4):
                tinv[pl.ds(4 * g + t, 16, stride=32), :] = jnp.where(
                    lane16 < 32, roll(turned, -32 * t, 1), 0.0
                )

    def eliminate(l):
        before, after = left[l], right[l]
        rows = block_rows(l)
        inverse = tinv[rows, 0:32]

        @pl.when(corner)
        def _():
            put(lm, l, l, nt_dot(diag[rows, 0:32], inverse))

        @pl.when(touched[l] == 0)
        def _():
            at = (rows, tile_of(lax.shift_right_logical(l, 2)))
            moved = pltpu.roll(tinv[rows, :], (32 * l) & 127, 1)
            mh[at], ml[at] = halves(moved)

            @pl.when((before >= 0) | (after >= 0))
            def _():
                mm[rows, :] = jnp.zeros((32, 512), F32)
                mm[at] = moved

        @pl.when(touched[l] > 0)
        def _():
            strip = nn(inverse, xm[rows, :])
            mm[rows, :] = strip
            mh[rows, :], ml[rows, :] = halves(strip)

        def fold(near, link):
            at = block_rows(near)
            factor = nt_dot(link[at, 0:32], inverse)
            diag[at, 0:32] = diag[at, 0:32] - nt_dot(factor, factor)
            xm[at, :] = xm[at, :] - nn(factor, mm[rows, :])
            touched[near] = jnp.int32(1)

            @pl.when(corner)
            def _():
                put(lm, near, l, factor)

        @pl.when(after >= 0)
        def _():
            fold(after, el)
            left[after] = before

        @pl.when(before >= 0)
        def _():
            fold(before, er)
            right[before] = after

        @pl.when((before >= 0) & (after >= 0))
        def _():
            one = nt_dot(er[block_rows(before), 0:32], inverse)
            two = nt_dot(el[block_rows(after), 0:32], inverse)
            er[block_rows(before), 0:32] = -nt_dot(one, two)
            el[block_rows(after), 0:32] = -nt_dot(two, one)

        ready[l] = jnp.int32(2)

    simple = jnp.logical_not(any_link | corner)

    def level(unused):
        batched_inverse()

        def mark(l):
            before, after, slot = left[l], right[l], slot0(l)
            free = (before < 0) | (slot0(jnp.maximum(before, 0)) > slot)
            free = free & ((after < 0) | (slot0(jnp.maximum(after, 0)) > slot))
            ready[l] = jnp.where(ready[l] == 2, 2, jnp.where(free, 1, 0))

        count[0] = jnp.int32(0)

        def visit(l):
            @pl.when(ready[l] == 1)
            def _():
                eliminate(l)

            @pl.when(ready[l] == 0)
            def _():
                count[0] = count[0] + 1

        @pl.when(simple)
        def _():
            for l in range(16):
                rows = slice(32 * l, 32 * l + 32)
                at = (rows, slice(128 * (l // 4), 128 * (l // 4) + 128))
                mh[at], ml[at] = halves(roll(tinv[rows, :], 32 * (l % 4), 1))

        @pl.when(jnp.logical_not(simple))
        def _():
            for_blocks(mark)
            for_blocks(visit)

        return count[0] > 0

    lax.while_loop(lambda more: more, level, jnp.bool_(True))
    out_ref[...] = jnp.zeros(out_ref.shape, F32)

    def emit(source_row, row_of, number):
        rows = pl.ds(pl.multiple_of(source_row, 128), 128)
        tall = iota((128, 128), 1)
        ua[0:128, :] = jnp.zeros((128, 512), F32)
        for l in range(16):
            slot = slot0(l)
            source = vm[rows, 128 * (l // 4) : 128 * (l // 4) + 128]
            moved = pltpu.roll(source, (32 * slot - 32 * l) & 127, 1)
            at = (slice(0, 128), tile_of(lax.shift_right_logical(slot, 2)))
            ua[at] = jnp.where((tall >> 5) == (slot & 3), moved, ua[at])
        for k in range(4):

            @pl.when(k < number)
            def _(k=k):
                out_ref[pl.ds(pl.multiple_of(row_of(k), 32), 32), 0:512] = ua[
                    32 * k : 32 * k + 32, :
                ]

    @pl.when(mine > 0)
    def _():
        for n in range(32):
            col_at[n] = jnp.int32(-1)
        count[0] = jnp.int32(0)
        count[1] = jnp.int32(0)

        def gather(l):
            @pl.when(table_ref[0, l, 7] > 0)
            def _():
                def one(u, at):
                    @pl.when(col_at[at] < 0)
                    def _():
                        new = count[1]
                        col_at[at] = new
                        col_list[new] = at
                        count[1] = new + 1

                        @pl.when((new & 3) == 0)
                        def _():
                            cm[:, tile_of(lax.shift_right_logical(new, 2))] = jnp.zeros(
                                (512, 128), F32
                            )

                    packed = col_at[at]
                    place(
                        cm, 32 * l, lax.shift_right_logical(packed, 2), packed & 3,
                        64 * l + 32, u,
                    )

                for_hits(0, l, one)

            @pl.when(table_ref[2, l, 7] > 0)
            def _():
                row_list[count[0]] = l
                count[0] = count[0] + 1

            @pl.when(table_ref[1, l, 7] > 0)
            def _():
                def one(u, at):
                    place(
                        out_ref, 32 * table_ref[3, l, 0], lax.shift_right_logical(at, 2),
                        at & 3, 64 * l, u,
                    )

                for_hits(1, l, one)

        for_blocks(gather)
        total = count[0]
        columns = count[1]
        tiles = lax.shift_right_logical(columns + 3, 2)

        def chunk(c, carry):
            @pl.when(total > 4 * c)
            def _():
                ua[0:128, :] = jnp.zeros((128, 512), F32)

                def fill(k, carry):
                    @pl.when(4 * c + k < total)
                    def _():
                        l = row_list[4 * c + k]
                        for_hits(
                            2,
                            l,
                            lambda u, at: place(
                                ua, 32 * k, lax.shift_right_logical(at, 2), at & 3, 64 * l, u
                            ),
                        )

                    return carry

                lax.fori_loop(0, 4, fill, 0)
                part = dot3(halves(ua[0:128, :]), (mh[...], ml[...]), NT)
                vm[0:128, :] = part
                solved = dot3(halves(part), (mh[...], ml[...]), NN)
                uh[...], ul[...] = halves(solved)

                def row_of(k):
                    return 32 * table_ref[3, row_list[jnp.minimum(4 * c + k, total - 1)], 0]

                def column(n, carry):
                    at = (slice(0, 512), tile_of(n))
                    update = dot3((uh[...], ul[...]), halves(cm[at]), NN)
                    tall = iota((128, 128), 1) >> 5
                    for q in range(4):

                        @pl.when(4 * n + q < columns)
                        def _(q=q):
                            to = col_list[4 * n + q]
                            moved = pltpu.roll(update, (32 * to - 32 * q) & 127, 1)
                            moved = jnp.where(tall == (to & 3), moved, 0.0)
                            tile = tile_of(lax.shift_right_logical(to, 2))
                            for k in range(4):

                                @pl.when(4 * c + k < total)
                                def _(k=k):
                                    rows = pl.ds(pl.multiple_of(row_of(k), 32), 32)
                                    out_ref[rows, tile] = (
                                        out_ref[rows, tile] - moved[32 * k : 32 * k + 32, :]
                                    )

                    return carry

                lax.fori_loop(0, tiles, column, 0)

                @pl.when(at_z == 0)
                def _():
                    emit(0, row_of, total - 4 * c)

            return carry

        lax.fori_loop(0, 4, chunk, 0)

    @pl.when(corner)
    def _():
        def rows(c, carry):
            vm[0:128, :] = lm[pl.ds(pl.multiple_of(128 * c, 128), 128), :]
            emit(0, lambda k: 32 * slot0(4 * c + k), 4)
            return carry

        lax.fori_loop(0, 4, rows, 0)
        lower = iota((512, 512), 0) >= iota((512, 512), 1)
        out_ref[:, 0:512] = jnp.where(lower, out_ref[:, 0:512], 0.0)


def factor(table, data):
    big = pltpu.VMEM((512, 512), F32)
    narrow = pltpu.VMEM((512, 128), F32)
    cube = pltpu.VMEM((32, 32, 128), F32)
    short = pltpu.VMEM((128, 512), F32)
    return pl.pallas_call(
        factor_kernel,
        out_shape=jax.ShapeDtypeStruct((512, 1024), F32),
        in_specs=[SM, VM],
        out_specs=VM,
        scratch_shapes=[
            narrow, cube, cube, narrow, narrow, narrow, big, big, big, short, short,
            pltpu.VMEM((512, 1024), F32),
            pltpu.VMEM((512, 512), BF16),
            pltpu.VMEM((512, 512), BF16),
            pltpu.VMEM((128, 512), BF16),
            pltpu.VMEM((128, 512), BF16),
            pltpu.SMEM((16,), jnp.int32),
            pltpu.SMEM((16,), jnp.int32),
            pltpu.SMEM((16,), jnp.int32),
            pltpu.SMEM((16,), jnp.int32),
            pltpu.SMEM((16,), jnp.int32),
            pltpu.SMEM((32,), jnp.int32),
            pltpu.SMEM((32,), jnp.int32),
            pltpu.SMEM((2,), jnp.int32),
        ],
    )(table, data)


def build_table(slot_order, mine, at_z):
    ids = jnp.arange(32, dtype=jnp.int32)[:, None]
    group = slot_order // 16
    wanted = jnp.stack([jnp.zeros((), jnp.int32), mine])
    mask = group[None] == wanted[:, None, None]
    rows = jnp.sum(jnp.where(mask, ids[None], 0), axis=1)
    slots = jnp.sum(jnp.where(mask, slot_order[None], 0), axis=1)
    steps = jnp.array([0, -4, 4, -1, 1, 0, 0], jnp.int32)
    deltas = jnp.array([0, 0, 0, 0, 0, -1, 1], jnp.int32)
    l = jnp.arange(16, dtype=jnp.int32)
    near = rows[:, :, None] + steps
    column = jnp.broadcast_to(l[:, None] + deltas, (16, 7))
    col = (rows % 4)[:, :, None]
    u = jnp.arange(7, dtype=jnp.int32)
    ok = (near >= 0) & (near < 32) & (column >= 0) & (column < 16)
    ok = ok & ~((u == 3) & (col == 0)) & ~((u == 4) & (col == 3))
    none = jnp.full((1, 32), -1, jnp.int32)
    turned = slot_order.T
    shifted = jnp.stack(
        [turned] * 5
        + [jnp.concatenate([none, turned[:-1]]), jnp.concatenate([turned[1:], none])],
        axis=1,
    )
    hit = near[..., None] == jnp.arange(32, dtype=jnp.int32)
    target = jnp.sum(jnp.where(hit, shifted[None], 0), axis=-1)
    target = jnp.where(ok, target, -1)
    at = target - 32 * at_z
    here = jnp.where((target >= 16) & (at >= 0) & (at < 32), at, -1)
    panel = jnp.where((target[1] >= 0) & (target[1] < 16), column, -1)
    three = jnp.concatenate([here, panel[None]], axis=0)
    flag = (jnp.max(three, axis=-1, keepdims=True) >= 0).astype(jnp.int32)
    three = jnp.concatenate([three, flag], axis=-1)
    last = jnp.stack([slots[1] - 16 * mine, rows[0], slots[0]], axis=-1)
    last = jnp.pad(last, ((0, 0), (0, 5)))
    return jnp.concatenate([three, last[None]], axis=0)


def on_device(probe_vectors, layer_ids, layer_kappa, slot_order):
    index_x = lax.axis_index("gx")
    index_y = lax.axis_index("gy")
    index_z = lax.axis_index("gz")
    grid_z = lax.axis_size("gz")
    mine = index_x * lax.axis_size("gy") + index_y
    table = build_table(slot_order, mine, index_z)

    send = pl.pallas_call(
        pack_kernel,
        out_shape=pltpu.VMEM((32, 24, 128), F32),
        in_specs=[VM, VM, SM],
        out_specs=VM,
    )(probe_vectors.reshape(32, 16, 128), layer_ids.reshape(16, 128), layer_kappa)
    pairs = [(k, k ^ 1) for k in range(lax.axis_size("gy"))]
    slab = lax.all_to_all(send, ("gx", "gy"), 0, 0, tiled=True)
    swap = near(lax.ppermute(slab[:, 16:24, :], "gy", pairs))
    slab = near(slab)
    low, high = pl.pallas_call(
        edge_kernel,
        out_shape=[pltpu.VMEM((64, 128), F32)] * 2,
        in_specs=[VM, VM],
        out_specs=[VM, VM],
    )(slab, swap)
    upward = [(i, i + 1) for i in range(grid_z - 1)]
    downward = [(b, a) for a, b in upward]
    from_left = lax.ppermute(high, "gz", upward)
    from_right = lax.ppermute(low, "gz", downward)
    planes = pltpu.VMEM((18, 32, 128), F32)
    pieces, coef = pl.pallas_call(
        filter_kernel,
        out_shape=[pltpu.VMEM((32, 56, 128), F32), pltpu.VMEM((2, 56, 128), F32)],
        in_specs=[SM, VM, VM, VM, VM],
        out_specs=[VM, VM],
        scratch_shapes=[planes] * 3
        + [pltpu.VMEM((2, 32, 128), F32)] * 2
        + [pltpu.VMEM((7, 16, 32, 128), F32), pltpu.VMEM((2, 7, 32, 128), F32)],
    )(slot_order.T, slab, swap, near(from_left), near(from_right))
    owned = lax.all_to_all(pieces, ("gx", "gy"), 0, 0, tiled=True)
    own, part = pl.pallas_call(
        galerkin_kernel,
        out_shape=[pltpu.VMEM((32, 256), F32)] * 2,
        in_specs=[SM, VM, VM],
        out_specs=[VM, VM],
        scratch_shapes=[pltpu.VMEM((32, 2048), F32)] * 3 + [pltpu.VMEM((32, 1024), F32)],
    )(table, near(owned.reshape(32 * 56, 128)), near(coef))
    other = lax.ppermute(part, "gy", pairs)
    spread = pl.pallas_call(
        copies_kernel,
        out_shape=pltpu.VMEM((16, 64, 256), F32),
        in_specs=[VM, VM, VM],
        out_specs=VM,
    )(near(own), near(part), near(other))
    spread = lax.all_to_all(spread, "gz", 0, 0, tiled=True)
    return factor(table, near(spread.reshape(1024, 256)))


def solution(mesh):
    in_specs = (P(None, "gx", "gy", "gz"), P("gx", "gy", "gz"), P(), P())
    out_specs = P(("gx", "gy"), "gz")
    return jax.shard_map(
        on_device, mesh=mesh, in_specs=in_specs, out_specs=out_specs, check_vma=False
    )
```

```python
import functools
import math

import jax
import jax.numpy as jnp
from jax import lax
from jax.experimental import pallas as pl
from jax.experimental.pallas import tpu as pltpu
from jax.sharding import PartitionSpec as P

PASSES = 4
UPPER = 120.0
LOWER = 24.0
SHIFT = 1.0
F32 = jnp.float32
BF16 = jnp.bfloat16
HIGHEST = lax.Precision.HIGHEST


VM = pl.BlockSpec(memory_space=pltpu.VMEM)


def near(value):
    return pltpu.with_memory_space_constraint(value, pltpu.VMEM)


SM = pl.BlockSpec(memory_space=pltpu.SMEM)


def cheb_factors(step_index):
    center = (UPPER + LOWER) / (UPPER - LOWER)
    growth = math.log(center + math.sqrt(center * center - 1.0))

    def chebval(degree):
        expo = math.exp(degree * growth)
        return 0.5 * (expo + 1.0 / expo)

    if step_index == 0:
        return (1.0 / chebval(1), 0.0)
    return (
        2.0 * chebval(step_index) / chebval(step_index + 1),
        chebval(step_index - 1) / chebval(step_index + 1),
    )


def position():
    return lax.axis_index("gx") * 4 + lax.axis_index("gy"), lax.axis_index("gz")


def iota(shape, dim):
    return lax.broadcasted_iota(jnp.int32, shape, dim)


def roll(value, shift, axis):
    shift = shift % value.shape[axis]
    if shift == 0:
        return value
    return pltpu.roll(value, shift, axis)


def pack_kernel(vec_ref, ids_ref, kappa_ref, out_ref):
    ids = ids_ref[...]
    kappa = jnp.zeros(ids.shape, F32)
    for layer in range(kappa_ref.shape[0]):
        kappa = jnp.where(ids == layer, kappa_ref[layer], kappa)
    out_ref[:, 0:16, :] = vec_ref[...]
    for dest in range(out_ref.shape[0]):
        core = dest % 2
        out_ref[dest, 16:24, :] = kappa[8 * core : 8 * core + 8, :]


def slab_plane(ref, swap_ref, field, plane):
    i, x = plane // 2, plane % 2
    if field == 0:
        tiles = [ref[4 * i + j, 8 * x : 8 * x + 8, :] for j in range(4)]
    else:
        held = lax.rem(lax.axis_index("gy"), 2) == x
        tiles = [
            jnp.where(held, ref[4 * i + j, 16:24, :], swap_ref[4 * i + j]) for j in range(4)
        ]
    return jnp.concatenate(tiles, axis=0)


def edge_kernel(slab_ref, swap_ref, low_ref, high_ref):
    lane = iota((32, 128), 1)
    for field in range(2):
        low = jnp.zeros((32, 128), F32)
        high = jnp.zeros((32, 128), F32)
        for plane in range(16):
            tile = slab_plane(slab_ref, swap_ref, field, plane)
            here = (lane >> 3) == plane
            low = jnp.where(here, roll(tile, 8 * plane, 1), low)
            high = jnp.where(here, roll(tile, 8 * plane + 8, 1), high)
        low_ref[32 * field : 32 * field + 32, :] = low
        high_ref[32 * field : 32 * field + 32, :] = high


def filter_kernel(
    order_ref, slab_ref, swap_ref, left_ref, right_ref, out_ref, coef_ref,
    za, zb, ka, ends_a, ends_b, main, side,
):
    mine, at_z = position()
    lane = iota((32, 128), 1)
    row = iota((32, 128), 0)
    slot = lane & 7
    zero_plane = jnp.zeros((32, 128), F32)
    for dest, field in ((za, 0), (ka, 1)):
        dest[0] = zero_plane
        dest[17] = zero_plane
        for plane in range(16):
            dest[plane + 1] = slab_plane(slab_ref, swap_ref, field, plane)
    zb[0] = zero_plane
    zb[17] = zero_plane
    ends_a[0] = right_ref[0:32, :]
    ends_a[1] = left_ref[0:32, :]

    def edges_of(right, left):
        return jnp.where(slot == 0, right, jnp.where(slot == 1, roll(left, -6, 1), 0.0))

    def z_pair(z, edges, plane):
        ahead = roll(edges, 127 - 8 * plane, 1)
        return (
            jnp.where(lane == 127, ahead, roll(z, 127, 1)),
            jnp.where(lane == 0, ahead, roll(z, 1, 1)),
        )

    def collect(inner, z, plane):
        return jnp.where((lane >> 1) == 4 * plane, roll(z, 8 * plane + 1, 1), inner)

    def end_pairs(right, left, inner):
        return (
            (roll(right, 127, 1), jnp.where(slot == 0, inner, roll(right, 1, 1))),
            (jnp.where(slot == 7, roll(inner, 6, 1), roll(left, 127, 1)), roll(left, 1, 1)),
        )

    half = 0.5 * 2.0 / (UPPER - LOWER)
    center = (UPPER + LOWER) / (UPPER - LOWER)

    def weights(store, k, kxp, kxm, kzp, kzm, first_x, last_x, keep):
        xp = half * (k + kxp)
        xm = half * (k + kxm)
        yp = half * (k + jnp.where(row == 31, 0.0, roll(k, 31, 0)))
        ym = half * (k + jnp.where(row == 0, 0.0, roll(k, 1, 0)))
        zp = half * (k + kzp)
        zm = half * (k + kzm)
        total = xp + xm + yp + ym + zp + zm
        values = (
            xp if last_x is None else jnp.where(last_x, 0.0, xp),
            xm if first_x is None else jnp.where(first_x, 0.0, xm),
            jnp.where(row == 31, 0.0, yp),
            jnp.where(row == 0, 0.0, ym),
            zp,
            zm,
            center - total,
        )
        for n, value in enumerate(values):
            store(n, value if keep is None else jnp.where(keep, value, 0.0))

    k_right, k_left = right_ref[32:64, :], left_ref[32:64, :]
    k_edges = edges_of(k_right, k_left)
    k_inner = zero_plane
    for plane in range(16):
        k = ka[plane + 1]
        kzp, kzm = z_pair(k, k_edges, plane)
        k_inner = collect(k_inner, k, plane)

        def store(n, value, plane=plane):
            main[n, plane] = value

        weights(store, k, ka[plane + 2], ka[plane], kzp, kzm, None, None, None)
    first_x, last_x = lane < 8, lane >= 120
    for n, (k, pair, keep) in enumerate(
        zip(
            (k_right, k_left),
            end_pairs(k_right, k_left, k_inner),
            (at_z < 15, at_z > 0),
        )
    ):
        kxp = jnp.where(last_x, 0.0, roll(k, -8, 1))
        kxm = jnp.where(first_x, 0.0, roll(k, 8, 1))

        def store(m, value, n=n):
            side[n, m] = value

        weights(store, k, kxp, kxm, *pair, first_x, last_x, keep)

    def combine(w, z, xp, xm, zp, zm, step, previous):
        one, two = cheb_factors(step)
        acc = w(6) * z + (w(0) * xp + w(1) * xm)
        acc = acc + (w(2) * roll(z, 31, 0) + w(3) * roll(z, 1, 0))
        acc = one * (acc + (w(4) * zp + w(5) * zm))
        return acc if step == 0 else acc - two * previous()

    for step in range(PASSES):
        src, dest = (za, zb) if step % 2 == 0 else (zb, za)
        end_src, end_dest = (ends_a, ends_b) if step % 2 == 0 else (ends_b, ends_a)
        right, left = end_src[0], end_src[1]
        edges = edges_of(right, left)
        inner = zero_plane
        for plane in range(16):
            z = src[plane + 1]
            inner = collect(inner, z, plane)
            zp, zm = z_pair(z, edges, plane)
            dest[plane + 1] = combine(
                lambda n, plane=plane: main[n, plane],
                z, src[plane + 2], src[plane], zp, zm, step,
                lambda plane=plane, dest=dest: dest[plane + 1],
            )
        for n, (z, (zp, zm)) in enumerate(zip((right, left), end_pairs(right, left, inner))):
            end_dest[n] = combine(
                lambda m, n=n: side[n, m],
                z, roll(z, -8, 1), roll(z, 8, 1), zp, zm, step,
                lambda n=n, end_dest=end_dest: end_dest[n],
            )

    ghosts = []
    for j in range(4):
        rows = slice(8 * j, 8 * j + 8)
        pair = []
        for n, keep, start in ((1, 7, 121), (0, 0, 0)):
            column = jnp.where((iota((8, 128), 1) & 7) == keep, ends_a[n, rows, :], 0.0)
            spread = pltpu.roll(column, start, 1, stride=1, stride_axis=0)
            pair.append(jnp.sum(spread, axis=0, keepdims=True))
        ghosts.append(pair)
    sub = iota((8, 128), 0)
    lane8 = iota((8, 128), 1)
    lane1 = iota((1, 128), 1)
    zero_row = jnp.zeros((1, 128), F32)
    for r in range(32):
        i, j = r // 4, r % 4
        dest = lax.shift_right_logical(order_ref[at_z, r], 4)
        rows = slice(8 * j, 8 * j + 8)
        out_ref[dest, 0:8, :] = za[2 * i + 1, rows]
        out_ref[dest, 8:16, :] = za[2 * i + 2, rows]
        out_ref[dest, 16:24, :] = za[2 * i, rows]
        out_ref[dest, 24:32, :] = za[2 * i + 3, rows]
        for x in range(2):
            out_ref[dest, 50 + x : 51 + x, :] = (
                za[2 * i + 1 + x, 8 * j - 1 : 8 * j] if j > 0 else zero_row
            )
            out_ref[dest, 52 + x : 53 + x, :] = (
                za[2 * i + 1 + x, 8 * j + 8 : 8 * j + 9] if j < 3 else zero_row
            )
        line = jnp.where(lane1 < 32, roll(ghosts[j][1], 16 - 16 * i, 1), 0.0)
        line = jnp.where(lane1 < 16, roll(ghosts[j][0], -16 * i, 1), line)
        out_ref[dest, 54:55, :] = line
        out_ref[dest, 55:56, :] = zero_row

        def coefficients(slot, i=i, j=j, rows=rows):
            coef_ref[slot, 0:8, :] = ka[2 * i + 1, rows]
            coef_ref[slot, 8:16, :] = ka[2 * i + 2, rows]
            coef_ref[slot, 16:24, :] = ka[2 * i, rows]
            coef_ref[slot, 24:32, :] = ka[2 * i + 3, rows]
            for x in range(2):
                coef_ref[slot, 32 + x : 33 + x, :] = (
                    ka[2 * i + 1 + x, 8 * j - 1 : 8 * j] if j > 0 else zero_row
                )
                coef_ref[slot, 34 + x : 35 + x, :] = (
                    ka[2 * i + 1 + x, 8 * j + 8 : 8 * j + 9] if j < 3 else zero_row
                )
                coef_ref[slot, 40 + 8 * x : 48 + 8 * x, :] = roll(
                    k_edges[rows, :], 127 - 8 * (2 * i + x), 1
                )

        @pl.when(dest == mine)
        def _(coefficients=coefficients):
            coefficients(0)

        @pl.when(dest == 0)
        def _(coefficients=coefficients):
            coefficients(1)

    first = [out_ref[0, 8 * n : 8 * n + 8, :] for n in range(4)]
    edges = [out_ref[0, 50 + n : 51 + n, :] for n in range(4)]
    ends = out_ref[0, 54:55, :]
    for core in range(2):
        body = jnp.concatenate(
            [pack_half(first[0], first[1], core), pack_half(first[2], first[3], core)], axis=0
        )
        sides = jnp.concatenate(
            [pack_half(edges[0], edges[1], core), pack_half(edges[2], edges[3], core)], axis=0
        )
        at = 64 if core == 0 else 63
        below = 40 if core == 0 else 32
        packed = jnp.zeros((8, 128), F32)
        for x in range(2):
            column = first[x][:, at : at + 1]
            packed = jnp.where(lane8 == below + 64 * x + sub, column, packed)
        line = jnp.sum(packed, axis=0, keepdims=True)
        outer = 32 if core == 0 else 40
        start = 0 if core == 0 else 16
        for x in range(2):
            here = (lane1 >> 3) == (outer + 64 * x) // 8
            line = jnp.where(here, roll(ends, outer + 64 * x - start - 8 * x, 1), line)

        def spread(k, carry, core=core, body=body, sides=sides, line=line):
            dest = 2 * k + core
            out_ref[dest, 32:48, :] = body
            out_ref[dest, 48:50, :] = sides
            out_ref[dest, 54:55, :] = out_ref[dest, 54:55, :] + line
            return carry

        lax.fori_loop(0, 16, spread, 0)


def pack_half(even, odd, core):
    lane = iota(even.shape, 1)
    if core == 0:
        return jnp.where(lane < 64, even, roll(odd, 64, 1))
    return jnp.where(lane < 64, roll(even, 64, 1), odd)


def nt_dot(a, b):
    return lax.dot_general(
        a, b, (((1,), (1,)), ((), ())), precision=HIGHEST, preferred_element_type=F32
    )


def galerkin_kernel(table_ref, data_ref, coef_ref, own_ref, part_ref, left, image, cross, ending):
    sub = iota((8, 128), 0)
    lane8 = iota((8, 128), 1)
    lane = iota((32, 128), 1)
    scaling = 1.0 / math.sqrt(2048.0)
    eye = (iota((32, 32), 0) == iota((32, 32), 1)).astype(F32)
    core = lax.rem(lax.axis_index("gy"), 2)

    def field(r):
        return data_ref[pl.ds(r, 32, stride=56), :]

    def span(r):
        return slice(128 * r, 128 * r + 128)

    def weights(part):
        k0 = coef_ref[part, 0:8, :]
        k1 = coef_ref[part, 8:16, :]
        km = coef_ref[part, 16:24, :]
        kp = coef_ref[part, 24:32, :]
        found = []
        for x in range(2):
            k = (k0, k1)[x]
            below = coef_ref[part, 32 + x : 33 + x, :]
            above = coef_ref[part, 34 + x : 35 + x, :]
            ends = coef_ref[part, 40 + 8 * x : 48 + 8 * x, :]
            xm = 0.5 * (k + (km, k0)[x])
            xp = 0.5 * (k + (k1, kp)[x])
            ym = 0.5 * (k + jnp.where(sub == 0, below, roll(k, 1, 0)))
            yp = 0.5 * (k + jnp.where(sub == 7, above, roll(k, 7, 0)))
            zm = 0.5 * (k + jnp.where(lane8 == 0, ends, roll(k, 1, 1)))
            zp = 0.5 * (k + jnp.where(lane8 == 127, ends, roll(k, 127, 1)))
            found.append((xm, xp, ym, yp, zm, zp, xp + xm + yp + ym + zp + zm))
        return found

    for r in range(16):
        left[:, span(r)] = field(r)
    columns = jnp.zeros((32, 128), F32)
    y_low, y_high = [], []
    for x, (xm, xp, ym, yp, zm, zp, diag) in enumerate(weights(0)):
        zm_in = jnp.where(lane8 == 0, 0.0, zm)
        zp_in = jnp.where(lane8 == 127, 0.0, zp)
        for y in range(8):
            r = 8 * x + y
            one = slice(y, y + 1)
            z = left[:, span(r)]
            beside = zp_in[one] * roll(z, 127, 1) + zm_in[one] * roll(z, 1, 1)
            if x == 0:
                beside = beside + xp[one] * left[:, span(r + 8)]
            else:
                beside = beside + xm[one] * left[:, span(r - 8)]
            if y < 7:
                beside = beside + yp[one] * left[:, span(r + 1)]
            if y > 0:
                beside = beside + ym[one] * left[:, span(r - 1)]
            image[:, span(r)] = diag[one] * z - beside
            cross[:, span(r)] = (xm, xp)[x][one] * field(16 + r)
            if y == 0:
                y_low.append((r, ym[one] * field(50 + x)))
            if y == 7:
                y_high.append((r, yp[one] * field(52 + x)))
            columns = jnp.where(lane == r, roll(zm[one] * z, r, 1), columns)
            columns = jnp.where(lane == 16 + r, roll(zp[one] * z, 17 + r, 1), columns)
    own_ref[:, 0:32] = scaling * nt_dot(left[...], image[...]) + SHIFT * eye
    own_ref[:, 32:64] = -scaling * nt_dot(left[:, 0:1024], cross[:, 0:1024])
    own_ref[:, 64:96] = -scaling * nt_dot(left[:, 1024:2048], cross[:, 1024:2048])
    for at, pair in ((96, y_low), (128, y_high)):
        block = sum(nt_dot(left[:, span(r)], ghost) for r, ghost in pair)
        own_ref[:, at : at + 32] = -scaling * block
    ghost = field(54)
    low = jnp.where(lane < 16, columns, 0.0)
    high = jnp.where((lane >= 16) & (lane < 32), columns, 0.0)
    own_ref[:, 160:192] = -scaling * nt_dot(low, ghost)
    own_ref[:, 192:224] = -scaling * nt_dot(high, ghost)

    even, odd = weights(1)

    def pack(a, b):
        return jnp.where(core == 0, pack_half(a, b, 0), pack_half(a, b, 1))

    w_out = pack(even[0], odd[1])
    w_in = pack(even[1], odd[0])
    ym, yp, zm, zp, diag = (pack(even[n], odd[n]) for n in range(2, 7))
    first8 = (lane8 & 63) == 0
    last8 = (lane8 & 63) == 63
    zm_in = jnp.where(first8 & (core == 0), 0.0, zm)
    zp_in = jnp.where(last8 & (core == 1), 0.0, zp)
    z_out = jnp.where(core == 0, jnp.where(first8, zm, 0.0), jnp.where(last8, zp, 0.0))
    at_first = (lane & 63) == 0
    at_last = (lane & 63) == 63
    for y in range(8):
        left[:, span(y)] = field(32 + y)
    for y in range(8):
        one = slice(y, y + 1)
        z = left[:, span(y)]
        z_low = jnp.where(at_first, roll(ghost, -(32 + y), 1), roll(z, 1, 1))
        z_high = jnp.where(at_last, roll(ghost, 23 - y, 1), roll(z, 127, 1))
        beside = zp_in[one] * z_high + zm_in[one] * z_low + w_in[one] * roll(z, 64, 1)
        if y < 7:
            beside = beside + yp[one] * left[:, span(y + 1)]
        if y > 0:
            beside = beside + ym[one] * left[:, span(y - 1)]
        image[:, span(y)] = diag[one] * z - beside
        side = w_out[one] * field(40 + y)
        cross[:, span(y)] = jnp.where(lane < 64, side, 0.0)
        cross[:, span(8 + y)] = jnp.where(lane < 64, 0.0, side)
        ending[:, span(y)] = z_out[one] * jnp.where(core == 0, z_low, z_high)
    half = slice(0, 1024)
    shift = jnp.where(core == 0, SHIFT, 0.0) * eye
    part_ref[:, 0:32] = scaling * nt_dot(left[:, half], image[:, half]) + shift
    part_ref[:, 32:64] = -scaling * nt_dot(left[:, half], cross[:, half])
    part_ref[:, 64:96] = -scaling * nt_dot(left[:, half], cross[:, 1024:2048])
    part_ref[:, 96:128] = -scaling * nt_dot(left[:, span(0)], ym[0:1] * field(48))
    part_ref[:, 128:160] = -scaling * nt_dot(left[:, span(7)], yp[7:8] * field(49))
    block = -scaling * nt_dot(left[:, half], ending[...])
    part_ref[:, 160:192] = jnp.where(core == 0, block, 0.0)
    part_ref[:, 192:224] = jnp.where(core == 0, 0.0, block)
    own_ref[:, 224:256] = jnp.zeros((32, 32), F32)
    part_ref[:, 224:256] = jnp.zeros((32, 32), F32)


def copies_kernel(own_ref, part_ref, other_ref, out_ref):
    own = own_ref[...]
    panel = part_ref[...] + other_ref[...]
    for n in range(16):
        out_ref[n, 0:32, :] = own
        out_ref[n, 32:64, :] = panel


def halves(value):
    high = value.astype(BF16)
    return high, (value - high.astype(F32)).astype(BF16)


def dot3(a, b, dims):
    ah, al = a
    bh, bl = b

    def one(p, q):
        return lax.dot_general(p, q, (dims, ((), ())), preferred_element_type=F32)

    return one(ah, bh) + (one(ah, bl) + one(al, bh))


NN = ((1,), (0,))
NT = ((1,), (1,))


def factor_kernel(
    table_ref, data_ref, out_ref,
    diag, al, il, tinv, er, el, xm, mm, lm, ua, vm, cm, mh, ml, uh, ul,
    left, right, ready, touched, row_list, col_list, col_at, count,
):
    mine, at_z = position()
    lane = iota((32, 128), 1)
    corner = (mine == 0) & (at_z == 0)

    def base(l):
        return table_ref[3, l, 1]

    def slot0(l):
        return table_ref[3, l, 2]

    def block_rows(l):
        return pl.ds(pl.multiple_of(32 * l, 32), 32)

    def tile_of(n):
        return pl.ds(pl.multiple_of(128 * n, 128), 128)

    def place(dest, row, tile, sub, source_row, u):
        source = data_ref[
            pl.ds(pl.multiple_of(source_row, 32), 32), 128 * (u // 4) : 128 * (u // 4) + 128
        ]
        moved = pltpu.roll(source, (32 * sub - 32 * u) & 127, 1)
        at = (pl.ds(pl.multiple_of(row, 32), 32), tile_of(tile))
        dest[at] = dest[at] + jnp.where((lane >> 5) == sub, moved, 0.0)

    def put(dest, row, column, block):
        padded = jnp.concatenate([block, jnp.zeros((32, 96), F32)], axis=1)
        at = (block_rows(row), tile_of(lax.shift_right_logical(column, 2)))
        dest[at] = dest[at] + pltpu.roll(padded, (32 * column) & 127, 1)

    def for_hits(which, l, action):
        for u in range(7):
            at = table_ref[which, l, u]

            @pl.when(at >= 0)
            def _(u=u, at=at):
                action(u, at)

    def for_blocks(action):
        def each(l, carry):
            action(l)
            return carry

        lax.fori_loop(0, 16, each, 0)

    def nn(a, b):
        return lax.dot_general(a, b, (NN, ((), ())), precision=HIGHEST, preferred_element_type=F32)

    mh[...] = jnp.zeros(mh.shape, BF16)
    ml[...] = jnp.zeros(ml.shape, BF16)
    any_link = jnp.bool_(False)
    for l in range(16):
        diag[32 * l : 32 * l + 32, :] = data_ref[64 * l + 32 : 64 * l + 64, 0:128]
        left[l] = jnp.int32(-1)
        right[l] = jnp.int32(-1)
        ready[l] = jnp.int32(0)
        touched[l] = jnp.int32(0)
    for l in range(15):
        link = base(l) == base(l + 1)
        any_link = any_link | link

        @pl.when(link)
        def _(l=l):
            right[l] = jnp.int32(l + 1)
            left[l + 1] = jnp.int32(l)
            ahead = data_ref[64 * l + 32 : 64 * l + 64, 128:256]
            back = data_ref[64 * l + 96 : 64 * l + 128, 128:256]
            er[32 * l : 32 * l + 32, :] = roll(ahead, -64, 1)
            el[32 * l + 32 : 32 * l + 64, :] = roll(back, -32, 1)

    @pl.when(any_link)
    def _():
        xm[...] = (iota((512, 512), 0) == iota((512, 512), 1)).astype(F32)

    @pl.when(corner)
    def _():
        lm[...] = jnp.zeros(lm.shape, F32)

    def batched_inverse():
        lane16 = iota((16, 128), 1)
        for g in range(8):
            wide = diag[pl.ds(4 * g, 16, stride=32), :]
            for t in range(1, 4):
                row = diag[pl.ds(4 * g + t, 16, stride=32), :]
                wide = jnp.where((lane16 >> 5) == t, roll(row, 32 * t, 1), wide)
            turned = jnp.transpose(jnp.concatenate([wide, jnp.zeros((112, 128), F32)], axis=0))
            for t in range(4):
                al[4 * g + t] = turned[32 * t : 32 * t + 32, :]
        sub = iota((8, 128), 0)
        for q in range(4):
            low = 8 * q
            a = [al[low + t, low : low + 8, :] for t in range(8)]
            w = [(sub == t).astype(F32) for t in range(8)]
            for t in range(8):
                pivot = a[t][t : t + 1, :]
                inv = lax.rsqrt(pivot)
                inv = inv * (1.5 - 0.5 * pivot * inv * inv)
                a[t] = a[t] * inv
                w[t] = w[t] * inv
                for k in range(t + 1, 8):
                    f = a[k][t : t + 1, :] * inv
                    a[k] = a[k] - f * a[t]
                    w[k] = w[k] - f * w[t]
            lead = {}
            for r in range(q + 1, 4):
                old = [al[low + k, 8 * r : 8 * r + 8, :] for k in range(8)]
                for t in range(8):
                    total = w[t][0:1, :] * old[0]
                    for k in range(1, t + 1):
                        total = total + w[t][k : k + 1, :] * old[k]
                    lead[t, r] = total
            unit = {(t, q): w[t] for t in range(8)}
            for r in range(q):
                old = [il[low + k, 8 * r : 8 * r + 8, :] for k in range(8)]
                for t in range(8):
                    total = w[t][0:1, :] * old[0]
                    for k in range(1, t + 1):
                        total = total + w[t][k : k + 1, :] * old[k]
                    unit[t, r] = total
            for t in range(8):
                for r in range(4):
                    il[low + t, 8 * r : 8 * r + 8, :] = unit.get((t, r), jnp.zeros((8, 128), F32))
            for i in range(low + 8, 32):
                own = i // 8
                f = [lead[t, own][i % 8 : i % 8 + 1, :] for t in range(8)]
                for r in range(own, 4):
                    value = al[i, 8 * r : 8 * r + 8, :]
                    for t in range(8):
                        value = value - f[t] * lead[t, r]
                    al[i, 8 * r : 8 * r + 8, :] = value
                for r in range(q + 1):
                    value = -f[0] * unit[0, r]
                    if r < q:
                        value = value + il[i, 8 * r : 8 * r + 8, :]
                    for t in range(1, 8):
                        value = value - f[t] * unit[t, r]
                    il[i, 8 * r : 8 * r + 8, :] = value
        for g in range(8):
            stack = jnp.concatenate([il[4 * g + t] for t in range(4)], axis=0)
            turned = jnp.transpose(stack)[0:16, :]
            for t in range(4):
                tinv[pl.ds(4 * g + t, 16, stride=32), :] = jnp.where(
                    lane16 < 32, roll(turned, -32 * t, 1), 0.0
                )

    def eliminate(l):
        before, after = left[l], right[l]
        rows = block_rows(l)
        inverse = tinv[rows, 0:32]

        @pl.when(corner)
        def _():
            put(lm, l, l, nt_dot(diag[rows, 0:32], inverse))

        @pl.when(touched[l] == 0)
        def _():
            at = (rows, tile_of(lax.shift_right_logical(l, 2)))
            moved = pltpu.roll(tinv[rows, :], (32 * l) & 127, 1)
            mh[at], ml[at] = halves(moved)

            @pl.when((before >= 0) | (after >= 0))
            def _():
                mm[rows, :] = jnp.zeros((32, 512), F32)
                mm[at] = moved

        @pl.when(touched[l] > 0)
        def _():
            strip = nn(inverse, xm[rows, :])
            mm[rows, :] = strip
            mh[rows, :], ml[rows, :] = halves(strip)

        def fold(near, link):
            at = block_rows(near)
            factor = nt_dot(link[at, 0:32], inverse)
            diag[at, 0:32] = diag[at, 0:32] - nt_dot(factor, factor)
            xm[at, :] = xm[at, :] - nn(factor, mm[rows, :])
            touched[near] = jnp.int32(1)

            @pl.when(corner)
            def _():
                put(lm, near, l, factor)

        @pl.when(after >= 0)
        def _():
            fold(after, el)
            left[after] = before

        @pl.when(before >= 0)
        def _():
            fold(before, er)
            right[before] = after

        @pl.when((before >= 0) & (after >= 0))
        def _():
            one = nt_dot(er[block_rows(before), 0:32], inverse)
            two = nt_dot(el[block_rows(after), 0:32], inverse)
            er[block_rows(before), 0:32] = -nt_dot(one, two)
            el[block_rows(after), 0:32] = -nt_dot(two, one)

        ready[l] = jnp.int32(2)

    simple = jnp.logical_not(any_link | corner)

    def level(unused):
        batched_inverse()

        def mark(l):
            before, after, slot = left[l], right[l], slot0(l)
            free = (before < 0) | (slot0(jnp.maximum(before, 0)) > slot)
            free = free & ((after < 0) | (slot0(jnp.maximum(after, 0)) > slot))
            ready[l] = jnp.where(ready[l] == 2, 2, jnp.where(free, 1, 0))

        count[0] = jnp.int32(0)

        def visit(l):
            @pl.when(ready[l] == 1)
            def _():
                eliminate(l)

            @pl.when(ready[l] == 0)
            def _():
                count[0] = count[0] + 1

        @pl.when(simple)
        def _():
            for l in range(16):
                rows = slice(32 * l, 32 * l + 32)
                at = (rows, slice(128 * (l // 4), 128 * (l // 4) + 128))
                mh[at], ml[at] = halves(roll(tinv[rows, :], 32 * (l % 4), 1))

        @pl.when(jnp.logical_not(simple))
        def _():
            for_blocks(mark)
            for_blocks(visit)

        return count[0] > 0

    lax.while_loop(lambda more: more, level, jnp.bool_(True))
    out_ref[...] = jnp.zeros(out_ref.shape, F32)

    def emit(source_row, row_of, number):
        rows = pl.ds(pl.multiple_of(source_row, 128), 128)
        tall = iota((128, 128), 1)
        ua[0:128, :] = jnp.zeros((128, 512), F32)
        for l in range(16):
            slot = slot0(l)
            source = vm[rows, 128 * (l // 4) : 128 * (l // 4) + 128]
            moved = pltpu.roll(source, (32 * slot - 32 * l) & 127, 1)
            at = (slice(0, 128), tile_of(lax.shift_right_logical(slot, 2)))
            ua[at] = jnp.where((tall >> 5) == (slot & 3), moved, ua[at])
        for k in range(4):

            @pl.when(k < number)
            def _(k=k):
                out_ref[pl.ds(pl.multiple_of(row_of(k), 32), 32), 0:512] = ua[
                    32 * k : 32 * k + 32, :
                ]

    @pl.when(mine > 0)
    def _():
        @pl.when(at_z == lax.shift_right_logical(mine, 1))
        def _():
            for l in range(16):
                row = table_ref[3, l, 0]
                to = row + 16 * (mine & 1)
                moved = pltpu.roll(data_ref[64 * l : 64 * l + 32, 0:128], (32 * to) & 127, 1)
                at = (block_rows(row), tile_of(lax.shift_right_logical(to, 2)))
                out_ref[at] = jnp.where((lane >> 5) == (to & 3), moved, 0.0)

        for n in range(32):
            col_at[n] = jnp.int32(-1)
        count[0] = jnp.int32(0)
        count[1] = jnp.int32(0)

        def gather(l):
            @pl.when(table_ref[0, l, 7] > 0)
            def _():
                def one(u, at):
                    @pl.when(col_at[at] < 0)
                    def _():
                        new = count[1]
                        col_at[at] = new
                        col_list[new] = at
                        count[1] = new + 1

                        @pl.when((new & 3) == 0)
                        def _():
                            cm[:, tile_of(lax.shift_right_logical(new, 2))] = jnp.zeros(
                                (512, 128), F32
                            )

                    packed = col_at[at]
                    place(
                        cm, 32 * l, lax.shift_right_logical(packed, 2), packed & 3,
                        64 * l + 32, u,
                    )

                for_hits(0, l, one)

            @pl.when(table_ref[2, l, 7] > 0)
            def _():
                row_list[count[0]] = l
                count[0] = count[0] + 1

            @pl.when(table_ref[1, l, 7] > 0)
            def _():
                def one(u, at):
                    place(
                        out_ref, 32 * table_ref[3, l, 0], lax.shift_right_logical(at, 2),
                        at & 3, 64 * l, u,
                    )

                for_hits(1, l, one)

        for_blocks(gather)
        total = count[0]
        columns = count[1]
        tiles = lax.shift_right_logical(columns + 3, 2)

        def chunk(c, carry):
            @pl.when(total > 4 * c)
            def _():
                ua[0:128, :] = jnp.zeros((128, 512), F32)

                def fill(k, carry):
                    @pl.when(4 * c + k < total)
                    def _():
                        l = row_list[4 * c + k]
                        for_hits(
                            2,
                            l,
                            lambda u, at: place(
                                ua, 32 * k, lax.shift_right_logical(at, 2), at & 3, 64 * l, u
                            ),
                        )

                    return carry

                lax.fori_loop(0, 4, fill, 0)
                part = dot3(halves(ua[0:128, :]), (mh[...], ml[...]), NT)
                vm[0:128, :] = part
                solved = dot3(halves(part), (mh[...], ml[...]), NN)
                uh[...], ul[...] = halves(solved)

                def row_of(k):
                    return 32 * table_ref[3, row_list[jnp.minimum(4 * c + k, total - 1)], 0]

                def column(n, carry):
                    at = (slice(0, 512), tile_of(n))
                    update = dot3((uh[...], ul[...]), halves(cm[at]), NN)
                    tall = iota((128, 128), 1) >> 5
                    for q in range(4):

                        @pl.when(4 * n + q < columns)
                        def _(q=q):
                            to = col_list[4 * n + q]
                            moved = pltpu.roll(update, (32 * to - 32 * q) & 127, 1)
                            moved = jnp.where(tall == (to & 3), moved, 0.0)
                            tile = tile_of(lax.shift_right_logical(to, 2))
                            for k in range(4):

                                @pl.when(4 * c + k < total)
                                def _(k=k):
                                    rows = pl.ds(pl.multiple_of(row_of(k), 32), 32)
                                    out_ref[rows, tile] = (
                                        out_ref[rows, tile] - moved[32 * k : 32 * k + 32, :]
                                    )

                    return carry

                lax.fori_loop(0, tiles, column, 0)

                @pl.when(at_z == 0)
                def _():
                    emit(0, row_of, total - 4 * c)

            return carry

        lax.fori_loop(0, 4, chunk, 0)

    @pl.when(corner)
    def _():
        def rows(c, carry):
            vm[0:128, :] = lm[pl.ds(pl.multiple_of(128 * c, 128), 128), :]
            emit(0, lambda k: 32 * slot0(4 * c + k), 4)
            return carry

        lax.fori_loop(0, 4, rows, 0)
        lower = iota((512, 512), 0) >= iota((512, 512), 1)
        out_ref[:, 0:512] = jnp.where(lower, out_ref[:, 0:512], 0.0)


def factor(table, data):
    big = pltpu.VMEM((512, 512), F32)
    narrow = pltpu.VMEM((512, 128), F32)
    cube = pltpu.VMEM((32, 32, 128), F32)
    short = pltpu.VMEM((128, 512), F32)
    return pl.pallas_call(
        factor_kernel,
        out_shape=jax.ShapeDtypeStruct((512, 1024), F32),
        in_specs=[SM, VM],
        out_specs=VM,
        scratch_shapes=[
            narrow, cube, cube, narrow, narrow, narrow, big, big, big, short, short,
            pltpu.VMEM((512, 1024), F32),
            pltpu.VMEM((512, 512), BF16),
            pltpu.VMEM((512, 512), BF16),
            pltpu.VMEM((128, 512), BF16),
            pltpu.VMEM((128, 512), BF16),
            pltpu.SMEM((16,), jnp.int32),
            pltpu.SMEM((16,), jnp.int32),
            pltpu.SMEM((16,), jnp.int32),
            pltpu.SMEM((16,), jnp.int32),
            pltpu.SMEM((16,), jnp.int32),
            pltpu.SMEM((32,), jnp.int32),
            pltpu.SMEM((32,), jnp.int32),
            pltpu.SMEM((2,), jnp.int32),
        ],
    )(table, data)


def build_table(slot_order, mine, at_z):
    ids = jnp.arange(32, dtype=jnp.int32)[:, None]
    group = slot_order // 16
    wanted = jnp.stack([jnp.zeros((), jnp.int32), mine])
    mask = group[None] == wanted[:, None, None]
    rows = jnp.sum(jnp.where(mask, ids[None], 0), axis=1)
    slots = jnp.sum(jnp.where(mask, slot_order[None], 0), axis=1)
    steps = jnp.array([0, -4, 4, -1, 1, 0, 0], jnp.int32)
    deltas = jnp.array([0, 0, 0, 0, 0, -1, 1], jnp.int32)
    l = jnp.arange(16, dtype=jnp.int32)
    near = rows[:, :, None] + steps
    column = jnp.broadcast_to(l[:, None] + deltas, (16, 7))
    col = (rows % 4)[:, :, None]
    u = jnp.arange(7, dtype=jnp.int32)
    ok = (near >= 0) & (near < 32) & (column >= 0) & (column < 16)
    ok = ok & ~((u == 3) & (col == 0)) & ~((u == 4) & (col == 3))
    none = jnp.full((1, 32), -1, jnp.int32)
    turned = slot_order.T
    shifted = jnp.stack(
        [turned] * 5
        + [jnp.concatenate([none, turned[:-1]]), jnp.concatenate([turned[1:], none])],
        axis=1,
    )
    hit = near[..., None] == jnp.arange(32, dtype=jnp.int32)
    target = jnp.sum(jnp.where(hit, shifted[None], 0), axis=-1)
    target = jnp.where(ok, target, -1)
    at = target - 32 * at_z
    here = jnp.where((target >= 16) & (at >= 0) & (at < 32), at, -1)
    part = jnp.arange(2, dtype=jnp.int32)[:, None, None]
    here = jnp.where((part == 1) & (u == 0), -1, here)
    panel = jnp.where((target[1] >= 0) & (target[1] < 16), column, -1)
    three = jnp.concatenate([here, panel[None]], axis=0)
    flag = (jnp.max(three, axis=-1, keepdims=True) >= 0).astype(jnp.int32)
    three = jnp.concatenate([three, flag], axis=-1)
    last = jnp.stack([slots[1] - 16 * mine, rows[0], slots[0]], axis=-1)
    last = jnp.pad(last, ((0, 0), (0, 5)))
    return jnp.concatenate([three, last[None]], axis=0)


def on_device(probe_vectors, layer_ids, layer_kappa, slot_order):
    index_x = lax.axis_index("gx")
    index_y = lax.axis_index("gy")
    index_z = lax.axis_index("gz")
    grid_z = lax.axis_size("gz")
    mine = index_x * lax.axis_size("gy") + index_y
    table = build_table(slot_order, mine, index_z)

    send = pl.pallas_call(
        pack_kernel,
        out_shape=pltpu.VMEM((32, 24, 128), F32),
        in_specs=[VM, VM, SM],
        out_specs=VM,
    )(probe_vectors.reshape(32, 16, 128), layer_ids.reshape(16, 128), layer_kappa)
    pairs = [(k, k ^ 1) for k in range(lax.axis_size("gy"))]
    slab = lax.all_to_all(send, ("gx", "gy"), 0, 0, tiled=True)
    swap = near(lax.ppermute(slab[:, 16:24, :], "gy", pairs))
    slab = near(slab)
    low, high = pl.pallas_call(
        edge_kernel,
        out_shape=[pltpu.VMEM((64, 128), F32)] * 2,
        in_specs=[VM, VM],
        out_specs=[VM, VM],
    )(slab, swap)
    upward = [(i, i + 1) for i in range(grid_z - 1)]
    downward = [(b, a) for a, b in upward]
    from_left = lax.ppermute(high, "gz", upward)
    from_right = lax.ppermute(low, "gz", downward)
    planes = pltpu.VMEM((18, 32, 128), F32)
    pieces, coef = pl.pallas_call(
        filter_kernel,
        out_shape=[pltpu.VMEM((32, 56, 128), F32), pltpu.VMEM((2, 56, 128), F32)],
        in_specs=[SM, VM, VM, VM, VM],
        out_specs=[VM, VM],
        scratch_shapes=[planes] * 3
        + [pltpu.VMEM((2, 32, 128), F32)] * 2
        + [pltpu.VMEM((7, 16, 32, 128), F32), pltpu.VMEM((2, 7, 32, 128), F32)],
    )(slot_order.T, slab, swap, near(from_left), near(from_right))
    owned = lax.all_to_all(pieces, ("gx", "gy"), 0, 0, tiled=True)
    own, part = pl.pallas_call(
        galerkin_kernel,
        out_shape=[pltpu.VMEM((32, 256), F32)] * 2,
        in_specs=[SM, VM, VM],
        out_specs=[VM, VM],
        scratch_shapes=[pltpu.VMEM((32, 2048), F32)] * 3 + [pltpu.VMEM((32, 1024), F32)],
    )(table, near(owned.reshape(32 * 56, 128)), near(coef))
    other = lax.ppermute(part, "gy", pairs)
    spread = pl.pallas_call(
        copies_kernel,
        out_shape=pltpu.VMEM((16, 64, 256), F32),
        in_specs=[VM, VM, VM],
        out_specs=VM,
    )(near(own), near(part), near(other))
    spread = lax.all_to_all(spread, "gz", 0, 0, tiled=True)
    return factor(table, near(spread.reshape(1024, 256)))


def solution(mesh):
    in_specs = (P(None, "gx", "gy", "gz"), P("gx", "gy", "gz"), P(), P())
    out_specs = P(("gx", "gy"), "gz")
    return jax.shard_map(
        on_device, mesh=mesh, in_specs=in_specs, out_specs=out_specs, check_vma=False
    )
```

```python
import functools
import math

import jax
import jax.numpy as jnp
from jax import lax
from jax.experimental import pallas as pl
from jax.experimental.pallas import tpu as pltpu
from jax.sharding import PartitionSpec as P

PASSES = 4
UPPER = 120.0
LOWER = 24.0
SHIFT = 1.0
F32 = jnp.float32
BF16 = jnp.bfloat16
HIGHEST = lax.Precision.HIGHEST


VM = pl.BlockSpec(memory_space=pltpu.VMEM)


def near(value):
    return pltpu.with_memory_space_constraint(value, pltpu.VMEM)


SM = pl.BlockSpec(memory_space=pltpu.SMEM)


def cheb_factors(step_index):
    center = (UPPER + LOWER) / (UPPER - LOWER)
    growth = math.log(center + math.sqrt(center * center - 1.0))

    def chebval(degree):
        expo = math.exp(degree * growth)
        return 0.5 * (expo + 1.0 / expo)

    if step_index == 0:
        return (1.0 / chebval(1), 0.0)
    return (
        2.0 * chebval(step_index) / chebval(step_index + 1),
        chebval(step_index - 1) / chebval(step_index + 1),
    )


def position():
    return lax.axis_index("gx") * 4 + lax.axis_index("gy"), lax.axis_index("gz")


def iota(shape, dim):
    return lax.broadcasted_iota(jnp.int32, shape, dim)


def roll(value, shift, axis):
    shift = shift % value.shape[axis]
    if shift == 0:
        return value
    return pltpu.roll(value, shift, axis)


def pack_kernel(vec_ref, ids_ref, kappa_ref, out_ref):
    ids = ids_ref[...]
    kappa = jnp.zeros(ids.shape, F32)
    for layer in range(kappa_ref.shape[0]):
        kappa = jnp.where(ids == layer, kappa_ref[layer], kappa)
    out_ref[:, 0:16, :] = vec_ref[...]
    for dest in range(out_ref.shape[0]):
        core = dest % 2
        out_ref[dest, 16:24, :] = kappa[8 * core : 8 * core + 8, :]


def slab_plane(ref, swap_ref, field, plane):
    i, x = plane // 2, plane % 2
    if field == 0:
        tiles = [ref[4 * i + j, 8 * x : 8 * x + 8, :] for j in range(4)]
    else:
        held = lax.rem(lax.axis_index("gy"), 2) == x
        tiles = [
            jnp.where(held, ref[4 * i + j, 16:24, :], swap_ref[4 * i + j]) for j in range(4)
        ]
    return jnp.concatenate(tiles, axis=0)


def edge_kernel(slab_ref, swap_ref, low_ref, high_ref):
    lane = iota((32, 128), 1)
    for field in range(2):
        low = jnp.zeros((32, 128), F32)
        high = jnp.zeros((32, 128), F32)
        for plane in range(16):
            tile = slab_plane(slab_ref, swap_ref, field, plane)
            here = (lane >> 3) == plane
            low = jnp.where(here, roll(tile, 8 * plane, 1), low)
            high = jnp.where(here, roll(tile, 8 * plane + 8, 1), high)
        low_ref[32 * field : 32 * field + 32, :] = low
        high_ref[32 * field : 32 * field + 32, :] = high


def filter_kernel(
    order_ref, slab_ref, swap_ref, left_ref, right_ref, out_ref, coef_ref,
    za, zb, ka, ends_a, ends_b, main, side,
):
    mine, at_z = position()
    lane = iota((32, 128), 1)
    row = iota((32, 128), 0)
    slot = lane & 7
    zero_plane = jnp.zeros((32, 128), F32)
    for dest, field in ((za, 0), (ka, 1)):
        dest[0] = zero_plane
        dest[17] = zero_plane
        for plane in range(16):
            dest[plane + 1] = slab_plane(slab_ref, swap_ref, field, plane)
    zb[0] = zero_plane
    zb[17] = zero_plane
    ends_a[0] = right_ref[0:32, :]
    ends_a[1] = left_ref[0:32, :]

    def edges_of(right, left):
        return jnp.where(slot == 0, right, jnp.where(slot == 1, roll(left, -6, 1), 0.0))

    def z_pair(z, edges, plane):
        ahead = roll(edges, 127 - 8 * plane, 1)
        return (
            jnp.where(lane == 127, ahead, roll(z, 127, 1)),
            jnp.where(lane == 0, ahead, roll(z, 1, 1)),
        )

    def collect(inner, z, plane):
        return jnp.where((lane >> 1) == 4 * plane, roll(z, 8 * plane + 1, 1), inner)

    def end_pairs(right, left, inner):
        return (
            (roll(right, 127, 1), jnp.where(slot == 0, inner, roll(right, 1, 1))),
            (jnp.where(slot == 7, roll(inner, 6, 1), roll(left, 127, 1)), roll(left, 1, 1)),
        )

    half = 0.5 * 2.0 / (UPPER - LOWER)
    center = (UPPER + LOWER) / (UPPER - LOWER)

    def weights(store, k, kxp, kxm, kzp, kzm, first_x, last_x, keep):
        xp = half * (k + kxp)
        xm = half * (k + kxm)
        yp = half * (k + jnp.where(row == 31, 0.0, roll(k, 31, 0)))
        ym = half * (k + jnp.where(row == 0, 0.0, roll(k, 1, 0)))
        zp = half * (k + kzp)
        zm = half * (k + kzm)
        total = xp + xm + yp + ym + zp + zm
        values = (
            xp if last_x is None else jnp.where(last_x, 0.0, xp),
            xm if first_x is None else jnp.where(first_x, 0.0, xm),
            jnp.where(row == 31, 0.0, yp),
            jnp.where(row == 0, 0.0, ym),
            zp,
            zm,
            center - total,
        )
        for n, value in enumerate(values):
            store(n, value if keep is None else jnp.where(keep, value, 0.0))

    k_right, k_left = right_ref[32:64, :], left_ref[32:64, :]
    k_edges = edges_of(k_right, k_left)
    k_inner = zero_plane
    for plane in range(16):
        k = ka[plane + 1]
        kzp, kzm = z_pair(k, k_edges, plane)
        k_inner = collect(k_inner, k, plane)

        def store(n, value, plane=plane):
            main[n, plane] = value

        weights(store, k, ka[plane + 2], ka[plane], kzp, kzm, None, None, None)
    first_x, last_x = lane < 8, lane >= 120
    for n, (k, pair, keep) in enumerate(
        zip(
            (k_right, k_left),
            end_pairs(k_right, k_left, k_inner),
            (at_z < 15, at_z > 0),
        )
    ):
        kxp = jnp.where(last_x, 0.0, roll(k, -8, 1))
        kxm = jnp.where(first_x, 0.0, roll(k, 8, 1))

        def store(m, value, n=n):
            side[n, m] = value

        weights(store, k, kxp, kxm, *pair, first_x, last_x, keep)

    def combine(w, z, xp, xm, zp, zm, step, previous):
        one, two = cheb_factors(step)
        acc = w(6) * z + (w(0) * xp + w(1) * xm)
        acc = acc + (w(2) * roll(z, 31, 0) + w(3) * roll(z, 1, 0))
        acc = one * (acc + (w(4) * zp + w(5) * zm))
        return acc if step == 0 else acc - two * previous()

    for step in range(PASSES):
        src, dest = (za, zb) if step % 2 == 0 else (zb, za)
        end_src, end_dest = (ends_a, ends_b) if step % 2 == 0 else (ends_b, ends_a)
        right, left = end_src[0], end_src[1]
        edges = edges_of(right, left)
        inner = zero_plane
        for plane in range(16):
            z = src[plane + 1]
            inner = collect(inner, z, plane)
            zp, zm = z_pair(z, edges, plane)
            dest[plane + 1] = combine(
                lambda n, plane=plane: main[n, plane],
                z, src[plane + 2], src[plane], zp, zm, step,
                lambda plane=plane, dest=dest: dest[plane + 1],
            )
        for n, (z, (zp, zm)) in enumerate(zip((right, left), end_pairs(right, left, inner))):
            end_dest[n] = combine(
                lambda m, n=n: side[n, m],
                z, roll(z, -8, 1), roll(z, 8, 1), zp, zm, step,
                lambda n=n, end_dest=end_dest: end_dest[n],
            )

    ghosts = []
    for j in range(4):
        rows = slice(8 * j, 8 * j + 8)
        pair = []
        for n, keep, start in ((1, 7, 121), (0, 0, 0)):
            column = jnp.where((iota((8, 128), 1) & 7) == keep, ends_a[n, rows, :], 0.0)
            spread = pltpu.roll(column, start, 1, stride=1, stride_axis=0)
            pair.append(jnp.sum(spread, axis=0, keepdims=True))
        ghosts.append(pair)
    sub = iota((8, 128), 0)
    lane8 = iota((8, 128), 1)
    lane1 = iota((1, 128), 1)
    zero_row = jnp.zeros((1, 128), F32)
    for r in range(32):
        i, j = r // 4, r % 4
        dest = lax.shift_right_logical(order_ref[at_z, r], 4)
        rows = slice(8 * j, 8 * j + 8)
        out_ref[dest, 0:8, :] = za[2 * i + 1, rows]
        out_ref[dest, 8:16, :] = za[2 * i + 2, rows]
        out_ref[dest, 16:24, :] = za[2 * i, rows]
        out_ref[dest, 24:32, :] = za[2 * i + 3, rows]
        for x in range(2):
            out_ref[dest, 50 + x : 51 + x, :] = (
                za[2 * i + 1 + x, 8 * j - 1 : 8 * j] if j > 0 else zero_row
            )
            out_ref[dest, 52 + x : 53 + x, :] = (
                za[2 * i + 1 + x, 8 * j + 8 : 8 * j + 9] if j < 3 else zero_row
            )
        line = jnp.where(lane1 < 32, roll(ghosts[j][1], 16 - 16 * i, 1), 0.0)
        line = jnp.where(lane1 < 16, roll(ghosts[j][0], -16 * i, 1), line)
        out_ref[dest, 54:55, :] = line
        out_ref[dest, 55:56, :] = zero_row

        def coefficients(slot, i=i, j=j, rows=rows):
            coef_ref[slot, 0:8, :] = ka[2 * i + 1, rows]
            coef_ref[slot, 8:16, :] = ka[2 * i + 2, rows]
            coef_ref[slot, 16:24, :] = ka[2 * i, rows]
            coef_ref[slot, 24:32, :] = ka[2 * i + 3, rows]
            for x in range(2):
                coef_ref[slot, 32 + x : 33 + x, :] = (
                    ka[2 * i + 1 + x, 8 * j - 1 : 8 * j] if j > 0 else zero_row
                )
                coef_ref[slot, 34 + x : 35 + x, :] = (
                    ka[2 * i + 1 + x, 8 * j + 8 : 8 * j + 9] if j < 3 else zero_row
                )
                coef_ref[slot, 40 + 8 * x : 48 + 8 * x, :] = roll(
                    k_edges[rows, :], 127 - 8 * (2 * i + x), 1
                )

        @pl.when(dest == mine)
        def _(coefficients=coefficients):
            coefficients(0)

        @pl.when(dest == 0)
        def _(coefficients=coefficients):
            coefficients(1)

    first = [out_ref[0, 8 * n : 8 * n + 8, :] for n in range(4)]
    edges = [out_ref[0, 50 + n : 51 + n, :] for n in range(4)]
    ends = out_ref[0, 54:55, :]
    for core in range(2):
        body = jnp.concatenate(
            [pack_half(first[0], first[1], core), pack_half(first[2], first[3], core)], axis=0
        )
        sides = jnp.concatenate(
            [pack_half(edges[0], edges[1], core), pack_half(edges[2], edges[3], core)], axis=0
        )
        at = 64 if core == 0 else 63
        below = 40 if core == 0 else 32
        packed = jnp.zeros((8, 128), F32)
        for x in range(2):
            column = first[x][:, at : at + 1]
            packed = jnp.where(lane8 == below + 64 * x + sub, column, packed)
        line = jnp.sum(packed, axis=0, keepdims=True)
        outer = 32 if core == 0 else 40
        start = 0 if core == 0 else 16
        for x in range(2):
            here = (lane1 >> 3) == (outer + 64 * x) // 8
            line = jnp.where(here, roll(ends, outer + 64 * x - start - 8 * x, 1), line)

        def spread(k, carry, core=core, body=body, sides=sides, line=line):
            dest = 2 * k + core
            out_ref[dest, 32:48, :] = body
            out_ref[dest, 48:50, :] = sides
            out_ref[dest, 54:55, :] = out_ref[dest, 54:55, :] + line
            return carry

        lax.fori_loop(0, 16, spread, 0)


def pack_half(even, odd, core):
    lane = iota(even.shape, 1)
    if core == 0:
        return jnp.where(lane < 64, even, roll(odd, 64, 1))
    return jnp.where(lane < 64, roll(even, 64, 1), odd)


def nt_dot(a, b):
    return lax.dot_general(
        a, b, (((1,), (1,)), ((), ())), precision=HIGHEST, preferred_element_type=F32
    )


def galerkin_kernel(data_ref, coef_ref, own_ref, part_ref, left, image, cross, ending):
    sub = iota((8, 128), 0)
    lane8 = iota((8, 128), 1)
    lane = iota((32, 128), 1)
    scaling = 1.0 / math.sqrt(2048.0)
    eye = (iota((32, 32), 0) == iota((32, 32), 1)).astype(F32)
    core = lax.rem(lax.axis_index("gy"), 2)

    def field(r):
        return data_ref[pl.ds(r, 32, stride=56), :]

    def span(r):
        return slice(128 * r, 128 * r + 128)

    def weights(part):
        k0 = coef_ref[part, 0:8, :]
        k1 = coef_ref[part, 8:16, :]
        km = coef_ref[part, 16:24, :]
        kp = coef_ref[part, 24:32, :]
        found = []
        for x in range(2):
            k = (k0, k1)[x]
            below = coef_ref[part, 32 + x : 33 + x, :]
            above = coef_ref[part, 34 + x : 35 + x, :]
            ends = coef_ref[part, 40 + 8 * x : 48 + 8 * x, :]
            xm = 0.5 * (k + (km, k0)[x])
            xp = 0.5 * (k + (k1, kp)[x])
            ym = 0.5 * (k + jnp.where(sub == 0, below, roll(k, 1, 0)))
            yp = 0.5 * (k + jnp.where(sub == 7, above, roll(k, 7, 0)))
            zm = 0.5 * (k + jnp.where(lane8 == 0, ends, roll(k, 1, 1)))
            zp = 0.5 * (k + jnp.where(lane8 == 127, ends, roll(k, 127, 1)))
            found.append((xm, xp, ym, yp, zm, zp, xp + xm + yp + ym + zp + zm))
        return found

    for r in range(16):
        left[:, span(r)] = field(r)
    columns = jnp.zeros((32, 128), F32)
    y_low, y_high = [], []
    for x, (xm, xp, ym, yp, zm, zp, diag) in enumerate(weights(0)):
        zm_in = jnp.where(lane8 == 0, 0.0, zm)
        zp_in = jnp.where(lane8 == 127, 0.0, zp)
        for y in range(8):
            r = 8 * x + y
            one = slice(y, y + 1)
            z = left[:, span(r)]
            beside = zp_in[one] * roll(z, 127, 1) + zm_in[one] * roll(z, 1, 1)
            if x == 0:
                beside = beside + xp[one] * left[:, span(r + 8)]
            else:
                beside = beside + xm[one] * left[:, span(r - 8)]
            if y < 7:
                beside = beside + yp[one] * left[:, span(r + 1)]
            if y > 0:
                beside = beside + ym[one] * left[:, span(r - 1)]
            image[:, span(r)] = diag[one] * z - beside
            cross[:, span(r)] = (xm, xp)[x][one] * field(16 + r)
            if y == 0:
                y_low.append((r, ym[one] * field(50 + x)))
            if y == 7:
                y_high.append((r, yp[one] * field(52 + x)))
            columns = jnp.where(lane == r, roll(zm[one] * z, r, 1), columns)
            columns = jnp.where(lane == 16 + r, roll(zp[one] * z, 17 + r, 1), columns)
    own_ref[:, 0:32] = scaling * nt_dot(left[...], image[...]) + SHIFT * eye
    own_ref[:, 32:64] = -scaling * nt_dot(left[:, 0:1024], cross[:, 0:1024])
    own_ref[:, 64:96] = -scaling * nt_dot(left[:, 1024:2048], cross[:, 1024:2048])
    for at, pair in ((96, y_low), (128, y_high)):
        block = sum(nt_dot(left[:, span(r)], ghost) for r, ghost in pair)
        own_ref[:, at : at + 32] = -scaling * block
    ghost = field(54)
    low = jnp.where(lane < 16, columns, 0.0)
    high = jnp.where((lane >= 16) & (lane < 32), columns, 0.0)
    own_ref[:, 160:192] = -scaling * nt_dot(low, ghost)
    own_ref[:, 192:224] = -scaling * nt_dot(high, ghost)

    even, odd = weights(1)

    def pack(a, b):
        return jnp.where(core == 0, pack_half(a, b, 0), pack_half(a, b, 1))

    w_out = pack(even[0], odd[1])
    w_in = pack(even[1], odd[0])
    ym, yp, zm, zp, diag = (pack(even[n], odd[n]) for n in range(2, 7))
    first8 = (lane8 & 63) == 0
    last8 = (lane8 & 63) == 63
    zm_in = jnp.where(first8 & (core == 0), 0.0, zm)
    zp_in = jnp.where(last8 & (core == 1), 0.0, zp)
    z_out = jnp.where(core == 0, jnp.where(first8, zm, 0.0), jnp.where(last8, zp, 0.0))
    at_first = (lane & 63) == 0
    at_last = (lane & 63) == 63
    for y in range(8):
        left[:, span(y)] = field(32 + y)
    for y in range(8):
        one = slice(y, y + 1)
        z = left[:, span(y)]
        z_low = jnp.where(at_first, roll(ghost, -(32 + y), 1), roll(z, 1, 1))
        z_high = jnp.where(at_last, roll(ghost, 23 - y, 1), roll(z, 127, 1))
        beside = zp_in[one] * z_high + zm_in[one] * z_low + w_in[one] * roll(z, 64, 1)
        if y < 7:
            beside = beside + yp[one] * left[:, span(y + 1)]
        if y > 0:
            beside = beside + ym[one] * left[:, span(y - 1)]
        image[:, span(y)] = diag[one] * z - beside
        side = w_out[one] * field(40 + y)
        cross[:, span(y)] = jnp.where(lane < 64, side, 0.0)
        cross[:, span(8 + y)] = jnp.where(lane < 64, 0.0, side)
        ending[:, span(y)] = z_out[one] * jnp.where(core == 0, z_low, z_high)
    half = slice(0, 1024)
    shift = jnp.where(core == 0, SHIFT, 0.0) * eye
    part_ref[:, 0:32] = scaling * nt_dot(left[:, half], image[:, half]) + shift
    part_ref[:, 32:64] = -scaling * nt_dot(left[:, half], cross[:, half])
    part_ref[:, 64:96] = -scaling * nt_dot(left[:, half], cross[:, 1024:2048])
    part_ref[:, 96:128] = -scaling * nt_dot(left[:, span(0)], ym[0:1] * field(48))
    part_ref[:, 128:160] = -scaling * nt_dot(left[:, span(7)], yp[7:8] * field(49))
    block = -scaling * nt_dot(left[:, half], ending[...])
    part_ref[:, 160:192] = jnp.where(core == 0, block, 0.0)
    part_ref[:, 192:224] = jnp.where(core == 0, 0.0, block)
    own_ref[:, 224:256] = jnp.zeros((32, 32), F32)
    part_ref[:, 224:256] = jnp.zeros((32, 32), F32)


def copies_kernel(own_ref, part_ref, other_ref, out_ref):
    own = own_ref[...]
    panel = part_ref[...] + other_ref[...]
    for n in range(16):
        out_ref[n, 0:32, :] = own
        out_ref[n, 32:64, :] = panel


def halves(value):
    high = value.astype(BF16)
    return high, (value - high.astype(F32)).astype(BF16)


def dot3(a, b, dims):
    ah, al = a
    bh, bl = b

    def one(p, q):
        return lax.dot_general(p, q, (dims, ((), ())), preferred_element_type=F32)

    return one(ah, bh) + (one(ah, bl) + one(al, bh))


NN = ((1,), (0,))
NT = ((1,), (1,))


def factor_kernel(
    table_ref, data_ref, out_ref,
    diag, al, il, tinv, er, el, xm, mm, lm, ua, vm, cm, mh, ml, uh, ul,
    left, right, ready, touched, row_list, col_list, col_at, count,
):
    mine, at_z = position()
    lane = iota((32, 128), 1)
    corner = (mine == 0) & (at_z == 0)

    def base(l):
        return table_ref[3, l, 1]

    def slot0(l):
        return table_ref[3, l, 2]

    def block_rows(l):
        return pl.ds(pl.multiple_of(32 * l, 32), 32)

    def tile_of(n):
        return pl.ds(pl.multiple_of(128 * n, 128), 128)

    def place(dest, row, tile, sub, source_row, u):
        source = data_ref[
            pl.ds(pl.multiple_of(source_row, 32), 32), 128 * (u // 4) : 128 * (u // 4) + 128
        ]
        moved = pltpu.roll(source, (32 * sub - 32 * u) & 127, 1)
        at = (pl.ds(pl.multiple_of(row, 32), 32), tile_of(tile))
        dest[at] = dest[at] + jnp.where((lane >> 5) == sub, moved, 0.0)

    def put(dest, row, column, block):
        padded = jnp.concatenate([block, jnp.zeros((32, 96), F32)], axis=1)
        at = (block_rows(row), tile_of(lax.shift_right_logical(column, 2)))
        dest[at] = dest[at] + pltpu.roll(padded, (32 * column) & 127, 1)

    def for_hits(which, l, action):
        for u in range(7):
            at = table_ref[which, l, u]

            @pl.when(at >= 0)
            def _(u=u, at=at):
                action(u, at)

    def for_blocks(action):
        def each(l, carry):
            action(l)
            return carry

        lax.fori_loop(0, 16, each, 0)

    def nn(a, b):
        return lax.dot_general(a, b, (NN, ((), ())), precision=HIGHEST, preferred_element_type=F32)

    mh[...] = jnp.zeros(mh.shape, BF16)
    ml[...] = jnp.zeros(ml.shape, BF16)
    any_link = jnp.bool_(False)
    for l in range(16):
        diag[32 * l : 32 * l + 32, :] = data_ref[64 * l + 32 : 64 * l + 64, 0:128]
        left[l] = jnp.int32(-1)
        right[l] = jnp.int32(-1)
        ready[l] = jnp.int32(0)
        touched[l] = jnp.int32(0)
    for l in range(15):
        link = base(l) == base(l + 1)
        any_link = any_link | link

        @pl.when(link)
        def _(l=l):
            right[l] = jnp.int32(l + 1)
            left[l + 1] = jnp.int32(l)
            ahead = data_ref[64 * l + 32 : 64 * l + 64, 128:256]
            back = data_ref[64 * l + 96 : 64 * l + 128, 128:256]
            er[32 * l : 32 * l + 32, :] = roll(ahead, -64, 1)
            el[32 * l + 32 : 32 * l + 64, :] = roll(back, -32, 1)

    @pl.when(any_link)
    def _():
        xm[...] = (iota((512, 512), 0) == iota((512, 512), 1)).astype(F32)

    @pl.when(corner)
    def _():
        lm[...] = jnp.zeros(lm.shape, F32)

    def batched_inverse():
        lane16 = iota((16, 128), 1)
        for g in range(8):
            wide = diag[pl.ds(4 * g, 16, stride=32), :]
            for t in range(1, 4):
                row = diag[pl.ds(4 * g + t, 16, stride=32), :]
                wide = jnp.where((lane16 >> 5) == t, roll(row, 32 * t, 1), wide)
            turned = jnp.transpose(jnp.concatenate([wide, jnp.zeros((112, 128), F32)], axis=0))
            for t in range(4):
                al[4 * g + t] = turned[32 * t : 32 * t + 32, :]
        sub = iota((8, 128), 0)
        for q in range(4):
            low = 8 * q
            a = [al[low + t, low : low + 8, :] for t in range(8)]
            w = [(sub == t).astype(F32) for t in range(8)]
            for t in range(8):
                pivot = a[t][t : t + 1, :]
                inv = lax.rsqrt(pivot)
                inv = inv * (1.5 - 0.5 * pivot * inv * inv)
                a[t] = a[t] * inv
                w[t] = w[t] * inv
                for k in range(t + 1, 8):
                    f = a[k][t : t + 1, :] * inv
                    a[k] = a[k] - f * a[t]
                    w[k] = w[k] - f * w[t]
            lead = {}
            for r in range(q + 1, 4):
                old = [al[low + k, 8 * r : 8 * r + 8, :] for k in range(8)]
                for t in range(8):
                    total = w[t][0:1, :] * old[0]
                    for k in range(1, t + 1):
                        total = total + w[t][k : k + 1, :] * old[k]
                    lead[t, r] = total
            unit = {(t, q): w[t] for t in range(8)}
            for r in range(q):
                old = [il[low + k, 8 * r : 8 * r + 8, :] for k in range(8)]
                for t in range(8):
                    total = w[t][0:1, :] * old[0]
                    for k in range(1, t + 1):
                        total = total + w[t][k : k + 1, :] * old[k]
                    unit[t, r] = total
            for t in range(8):
                for r in range(4):
                    il[low + t, 8 * r : 8 * r + 8, :] = unit.get((t, r), jnp.zeros((8, 128), F32))
            for i in range(low + 8, 32):
                own = i // 8
                f = [lead[t, own][i % 8 : i % 8 + 1, :] for t in range(8)]
                for r in range(own, 4):
                    value = al[i, 8 * r : 8 * r + 8, :]
                    for t in range(8):
                        value = value - f[t] * lead[t, r]
                    al[i, 8 * r : 8 * r + 8, :] = value
                for r in range(q + 1):
                    value = -f[0] * unit[0, r]
                    if r < q:
                        value = value + il[i, 8 * r : 8 * r + 8, :]
                    for t in range(1, 8):
                        value = value - f[t] * unit[t, r]
                    il[i, 8 * r : 8 * r + 8, :] = value
        for g in range(8):
            stack = jnp.concatenate([il[4 * g + t] for t in range(4)], axis=0)
            turned = jnp.transpose(stack)[0:16, :]
            for t in range(4):
                tinv[pl.ds(4 * g + t, 16, stride=32), :] = jnp.where(
                    lane16 < 32, roll(turned, -32 * t, 1), 0.0
                )

    def eliminate(l):
        before, after = left[l], right[l]
        rows = block_rows(l)
        inverse = tinv[rows, 0:32]

        @pl.when(corner)
        def _():
            put(lm, l, l, nt_dot(diag[rows, 0:32], inverse))

        @pl.when(touched[l] == 0)
        def _():
            at = (rows, tile_of(lax.shift_right_logical(l, 2)))
            moved = pltpu.roll(tinv[rows, :], (32 * l) & 127, 1)
            mh[at], ml[at] = halves(moved)

            @pl.when((before >= 0) | (after >= 0))
            def _():
                mm[rows, :] = jnp.zeros((32, 512), F32)
                mm[at] = moved

        @pl.when(touched[l] > 0)
        def _():
            strip = nn(inverse, xm[rows, :])
            mm[rows, :] = strip
            mh[rows, :], ml[rows, :] = halves(strip)

        def fold(near, link):
            at = block_rows(near)
            factor = nt_dot(link[at, 0:32], inverse)
            diag[at, 0:32] = diag[at, 0:32] - nt_dot(factor, factor)
            xm[at, :] = xm[at, :] - nn(factor, mm[rows, :])
            touched[near] = jnp.int32(1)

            @pl.when(corner)
            def _():
                put(lm, near, l, factor)

        @pl.when(after >= 0)
        def _():
            fold(after, el)
            left[after] = before

        @pl.when(before >= 0)
        def _():
            fold(before, er)
            right[before] = after

        @pl.when((before >= 0) & (after >= 0))
        def _():
            one = nt_dot(er[block_rows(before), 0:32], inverse)
            two = nt_dot(el[block_rows(after), 0:32], inverse)
            er[block_rows(before), 0:32] = -nt_dot(one, two)
            el[block_rows(after), 0:32] = -nt_dot(two, one)

        ready[l] = jnp.int32(2)

    simple = jnp.logical_not(any_link | corner)

    def level(unused):
        batched_inverse()

        def mark(l):
            before, after, slot = left[l], right[l], slot0(l)
            free = (before < 0) | (slot0(jnp.maximum(before, 0)) > slot)
            free = free & ((after < 0) | (slot0(jnp.maximum(after, 0)) > slot))
            ready[l] = jnp.where(ready[l] == 2, 2, jnp.where(free, 1, 0))

        count[0] = jnp.int32(0)

        def visit(l):
            @pl.when(ready[l] == 1)
            def _():
                eliminate(l)

            @pl.when(ready[l] == 0)
            def _():
                count[0] = count[0] + 1

        @pl.when(simple)
        def _():
            for l in range(16):
                rows = slice(32 * l, 32 * l + 32)
                at = (rows, slice(128 * (l // 4), 128 * (l // 4) + 128))
                mh[at], ml[at] = halves(roll(tinv[rows, :], 32 * (l % 4), 1))

        @pl.when(jnp.logical_not(simple))
        def _():
            for_blocks(mark)
            for_blocks(visit)

        return count[0] > 0

    lax.while_loop(lambda more: more, level, jnp.bool_(True))
    out_ref[...] = jnp.zeros(out_ref.shape, F32)

    def emit(source_row, row_of, number):
        rows = pl.ds(pl.multiple_of(source_row, 128), 128)
        tall = iota((128, 128), 1)
        ua[0:128, :] = jnp.zeros((128, 512), F32)
        for l in range(16):
            slot = slot0(l)
            source = vm[rows, 128 * (l // 4) : 128 * (l // 4) + 128]
            moved = pltpu.roll(source, (32 * slot - 32 * l) & 127, 1)
            at = (slice(0, 128), tile_of(lax.shift_right_logical(slot, 2)))
            ua[at] = jnp.where((tall >> 5) == (slot & 3), moved, ua[at])
        for k in range(4):

            @pl.when(k < number)
            def _(k=k):
                out_ref[pl.ds(pl.multiple_of(row_of(k), 32), 32), 0:512] = ua[
                    32 * k : 32 * k + 32, :
                ]

    @pl.when(mine > 0)
    def _():
        @pl.when(at_z == lax.shift_right_logical(mine, 1))
        def _():
            for l in range(16):
                row = table_ref[3, l, 0]
                to = row + 16 * (mine & 1)
                moved = pltpu.roll(data_ref[64 * l : 64 * l + 32, 0:128], (32 * to) & 127, 1)
                at = (block_rows(row), tile_of(lax.shift_right_logical(to, 2)))
                out_ref[at] = jnp.where((lane >> 5) == (to & 3), moved, 0.0)

        for n in range(32):
            col_at[n] = jnp.int32(-1)
        count[0] = jnp.int32(0)
        count[1] = jnp.int32(0)

        def gather(l):
            @pl.when(table_ref[0, l, 7] > 0)
            def _():
                def one(u, at):
                    @pl.when(col_at[at] < 0)
                    def _():
                        new = count[1]
                        col_at[at] = new
                        col_list[new] = at
                        count[1] = new + 1

                        @pl.when((new & 3) == 0)
                        def _():
                            cm[:, tile_of(lax.shift_right_logical(new, 2))] = jnp.zeros(
                                (512, 128), F32
                            )

                    packed = col_at[at]
                    place(
                        cm, 32 * l, lax.shift_right_logical(packed, 2), packed & 3,
                        64 * l + 32, u,
                    )

                for_hits(0, l, one)

            @pl.when(table_ref[2, l, 7] > 0)
            def _():
                row_list[count[0]] = l
                count[0] = count[0] + 1

            @pl.when(table_ref[1, l, 7] > 0)
            def _():
                def one(u, at):
                    place(
                        out_ref, 32 * table_ref[3, l, 0], lax.shift_right_logical(at, 2),
                        at & 3, 64 * l, u,
                    )

                for_hits(1, l, one)

        for_blocks(gather)
        total = count[0]
        columns = count[1]
        tiles = lax.shift_right_logical(columns + 3, 2)

        def chunk(c, carry):
            @pl.when(total > 4 * c)
            def _():
                ua[0:128, :] = jnp.zeros((128, 512), F32)

                def fill(k, carry):
                    @pl.when(4 * c + k < total)
                    def _():
                        l = row_list[4 * c + k]
                        for_hits(
                            2,
                            l,
                            lambda u, at: place(
                                ua, 32 * k, lax.shift_right_logical(at, 2), at & 3, 64 * l, u
                            ),
                        )

                    return carry

                lax.fori_loop(0, 4, fill, 0)
                part = dot3(halves(ua[0:128, :]), (mh[...], ml[...]), NT)
                vm[0:128, :] = part
                solved = dot3(halves(part), (mh[...], ml[...]), NN)
                uh[...], ul[...] = halves(solved)

                def row_of(k):
                    return 32 * table_ref[3, row_list[jnp.minimum(4 * c + k, total - 1)], 0]

                def column(n, carry):
                    at = (slice(0, 512), tile_of(n))
                    update = dot3((uh[...], ul[...]), halves(cm[at]), NN)
                    tall = iota((128, 128), 1) >> 5
                    for q in range(4):

                        @pl.when(4 * n + q < columns)
                        def _(q=q):
                            to = col_list[4 * n + q]
                            moved = pltpu.roll(update, (32 * to - 32 * q) & 127, 1)
                            moved = jnp.where(tall == (to & 3), moved, 0.0)
                            tile = tile_of(lax.shift_right_logical(to, 2))
                            for k in range(4):

                                @pl.when(4 * c + k < total)
                                def _(k=k):
                                    rows = pl.ds(pl.multiple_of(row_of(k), 32), 32)
                                    out_ref[rows, tile] = (
                                        out_ref[rows, tile] - moved[32 * k : 32 * k + 32, :]
                                    )

                    return carry

                lax.fori_loop(0, tiles, column, 0)

                @pl.when(at_z == 0)
                def _():
                    emit(0, row_of, total - 4 * c)

            return carry

        lax.fori_loop(0, 4, chunk, 0)

    @pl.when(corner)
    def _():
        def rows(c, carry):
            vm[0:128, :] = lm[pl.ds(pl.multiple_of(128 * c, 128), 128), :]
            emit(0, lambda k: 32 * slot0(4 * c + k), 4)
            return carry

        lax.fori_loop(0, 4, rows, 0)
        lower = iota((512, 512), 0) >= iota((512, 512), 1)
        out_ref[:, 0:512] = jnp.where(lower, out_ref[:, 0:512], 0.0)


def factor(table, data):
    big = pltpu.VMEM((512, 512), F32)
    narrow = pltpu.VMEM((512, 128), F32)
    cube = pltpu.VMEM((32, 32, 128), F32)
    short = pltpu.VMEM((128, 512), F32)
    return pl.pallas_call(
        factor_kernel,
        out_shape=jax.ShapeDtypeStruct((512, 1024), F32),
        in_specs=[SM, VM],
        out_specs=VM,
        scratch_shapes=[
            narrow, cube, cube, narrow, narrow, narrow, big, big, big, short, short,
            pltpu.VMEM((512, 1024), F32),
            pltpu.VMEM((512, 512), BF16),
            pltpu.VMEM((512, 512), BF16),
            pltpu.VMEM((128, 512), BF16),
            pltpu.VMEM((128, 512), BF16),
            pltpu.SMEM((16,), jnp.int32),
            pltpu.SMEM((16,), jnp.int32),
            pltpu.SMEM((16,), jnp.int32),
            pltpu.SMEM((16,), jnp.int32),
            pltpu.SMEM((16,), jnp.int32),
            pltpu.SMEM((32,), jnp.int32),
            pltpu.SMEM((32,), jnp.int32),
            pltpu.SMEM((2,), jnp.int32),
        ],
    )(table, data)


def build_table(slot_order, mine, at_z):
    ids = jnp.arange(32, dtype=jnp.int32)[:, None]
    group = slot_order // 16
    wanted = jnp.stack([jnp.zeros((), jnp.int32), mine])
    mask = group[None] == wanted[:, None, None]
    rows = jnp.sum(jnp.where(mask, ids[None], 0), axis=1)
    slots = jnp.sum(jnp.where(mask, slot_order[None], 0), axis=1)
    steps = jnp.array([0, -4, 4, -1, 1, 0, 0], jnp.int32)
    deltas = jnp.array([0, 0, 0, 0, 0, -1, 1], jnp.int32)
    l = jnp.arange(16, dtype=jnp.int32)
    near = rows[:, :, None] + steps
    column = jnp.broadcast_to(l[:, None] + deltas, (16, 7))
    col = (rows % 4)[:, :, None]
    u = jnp.arange(7, dtype=jnp.int32)
    ok = (near >= 0) & (near < 32) & (column >= 0) & (column < 16)
    ok = ok & ~((u == 3) & (col == 0)) & ~((u == 4) & (col == 3))
    none = jnp.full((1, 32), -1, jnp.int32)
    turned = slot_order.T
    shifted = jnp.stack(
        [turned] * 5
        + [jnp.concatenate([none, turned[:-1]]), jnp.concatenate([turned[1:], none])],
        axis=1,
    )
    hit = near[..., None] == jnp.arange(32, dtype=jnp.int32)
    target = jnp.sum(jnp.where(hit, shifted[None], 0), axis=-1)
    target = jnp.where(ok, target, -1)
    at = target - 32 * at_z
    here = jnp.where((target >= 16) & (at >= 0) & (at < 32), at, -1)
    part = jnp.arange(2, dtype=jnp.int32)[:, None, None]
    here = jnp.where((part == 1) & (u == 0), -1, here)
    panel = jnp.where((target[1] >= 0) & (target[1] < 16), column, -1)
    three = jnp.concatenate([here, panel[None]], axis=0)
    flag = (jnp.max(three, axis=-1, keepdims=True) >= 0).astype(jnp.int32)
    three = jnp.concatenate([three, flag], axis=-1)
    last = jnp.stack([slots[1] - 16 * mine, rows[0], slots[0]], axis=-1)
    last = jnp.pad(last, ((0, 0), (0, 5)))
    return jnp.concatenate([three, last[None]], axis=0)


def on_device(probe_vectors, layer_ids, layer_kappa, slot_order):
    index_x = lax.axis_index("gx")
    index_y = lax.axis_index("gy")
    index_z = lax.axis_index("gz")
    grid_z = lax.axis_size("gz")
    mine = index_x * lax.axis_size("gy") + index_y
    table = build_table(slot_order, mine, index_z)

    send = pl.pallas_call(
        pack_kernel,
        out_shape=pltpu.VMEM((32, 24, 128), F32),
        in_specs=[VM, VM, SM],
        out_specs=VM,
    )(probe_vectors.reshape(32, 16, 128), layer_ids.reshape(16, 128), layer_kappa)
    pairs = [(k, k ^ 1) for k in range(lax.axis_size("gy"))]
    slab = lax.all_to_all(send, ("gx", "gy"), 0, 0, tiled=True)
    swap = near(lax.ppermute(slab[:, 16:24, :], "gy", pairs))
    slab = near(slab)
    low, high = pl.pallas_call(
        edge_kernel,
        out_shape=[pltpu.VMEM((64, 128), F32)] * 2,
        in_specs=[VM, VM],
        out_specs=[VM, VM],
    )(slab, swap)
    upward = [(i, i + 1) for i in range(grid_z - 1)]
    downward = [(b, a) for a, b in upward]
    from_left = lax.ppermute(high, "gz", upward)
    from_right = lax.ppermute(low, "gz", downward)
    planes = pltpu.VMEM((18, 32, 128), F32)
    pieces, coef = pl.pallas_call(
        filter_kernel,
        out_shape=[pltpu.VMEM((32, 56, 128), F32), pltpu.VMEM((2, 56, 128), F32)],
        in_specs=[SM, VM, VM, VM, VM],
        out_specs=[VM, VM],
        scratch_shapes=[planes] * 3
        + [pltpu.VMEM((2, 32, 128), F32)] * 2
        + [pltpu.VMEM((7, 16, 32, 128), F32), pltpu.VMEM((2, 7, 32, 128), F32)],
    )(slot_order.T, slab, swap, near(from_left), near(from_right))
    owned = lax.all_to_all(pieces, ("gx", "gy"), 0, 0, tiled=True)
    own, part = pl.pallas_call(
        galerkin_kernel,
        out_shape=[pltpu.VMEM((32, 256), F32)] * 2,
        in_specs=[VM, VM],
        out_specs=[VM, VM],
        scratch_shapes=[pltpu.VMEM((32, 2048), F32)] * 3 + [pltpu.VMEM((32, 1024), F32)],
    )(near(owned.reshape(32 * 56, 128)), near(coef))
    other = lax.ppermute(part, "gy", pairs)
    spread = pl.pallas_call(
        copies_kernel,
        out_shape=pltpu.VMEM((16, 64, 256), F32),
        in_specs=[VM, VM, VM],
        out_specs=VM,
    )(near(own), near(part), near(other))
    spread = lax.all_to_all(spread, "gz", 0, 0, tiled=True)
    return factor(table, near(spread.reshape(1024, 256)))


def solution(mesh):
    in_specs = (P(None, "gx", "gy", "gz"), P("gx", "gy", "gz"), P(), P())
    out_specs = P(("gx", "gy"), "gz")
    return jax.shard_map(
        on_device, mesh=mesh, in_specs=in_specs, out_specs=out_specs, check_vma=False
    )
```
